32 devices in a mesh: rep: 8 (over y, x, core), fsdp: 4 (over z).
Axes of the slice: x: 2, y: 2, z: 4, core: 2. Of those that a mesh axis runs over, the one named last changes fastest.
Arguments:
- tokens_in: bfloat16 [4096, 1024], P(('rep', 'fsdp')), may hold values from -20 to 20
- input_gain: float32 [1024], replicated, may hold values from 0.25 to 1.75
- q_gain: float32 [128], replicated, may hold values from 0.6 to 4.2
- k_gain: float32 [128], replicated, may hold values from 0.6 to 4.2
- w_query: bfloat16 [1024, 2048], P('fsdp'), may hold values from -0.35 to 0.35
- w_key: bfloat16 [1024, 1024], P('fsdp'), may hold values from -0.35 to 0.35
- w_value: bfloat16 [1024, 1024], P('fsdp'), may hold values from -0.1875 to 0.1875
- w_output: bfloat16 [2048, 1024], P('fsdp'), may hold values from -0.5 to 0.5
- post_gain: float32 [1024], replicated, may hold values from 0.25 to 1.75
- w_gate: bfloat16 [1024, 3072], P('fsdp'), may hold values from -0.1875 to 0.1875
- w_up: bfloat16 [1024, 3072], P('fsdp'), may hold values from -0.1875 to 0.1875
- w_down: bfloat16 [3072, 1024], P('fsdp'), may hold values from -0.109375 to 0.109375
- segment_ids: int32 [4096], P(('rep', 'fsdp')), may hold values from 0 to 95, as said below
- positions: int32 [4096], P(('rep', 'fsdp')), may hold values from 0 to 1926, as said below
- out_cotangent: bfloat16 [4096, 1024], P(('rep', 'fsdp')), may hold values from -19 to 19
Outputs:
- block_out: bfloat16 [4096, 1024], P(('rep', 'fsdp'))
- input_grad: bfloat16 [4096, 1024], P(('rep', 'fsdp'))
- grad_input_gain: float32 [1024], replicated
- grad_q_gain: float32 [128], replicated
- grad_k_gain: float32 [128], replicated
- grad_post_gain: float32 [1024], replicated
- grad_query: float32 [1024, 2048], P('fsdp')
- grad_key: float32 [1024, 1024], P('fsdp')
- grad_value: float32 [1024, 1024], P('fsdp')
- grad_output: float32 [2048, 1024], P('fsdp')
- grad_gate: float32 [1024, 3072], P('fsdp')
- grad_up: float32 [1024, 3072], P('fsdp')
- grad_down: float32 [3072, 1024], P('fsdp')
The draws below stay inside these ranges and needn't reach their ends.
Inputs may be any that keep to these rules, and one draw needn't show every extreme that they name: `segment_ids`: each sequence of 128 tokens holds pieces of one to three documents; ids never fall along a sequence, no two sequences share an id, and ids may skip values. `positions`: positions rise by one from a token to the next of the same document and are 0 at a document's first token; the first document of a sequence may have begun in an earlier sequence.
All inputs are finite; a program needn't handle non-finite values.
Results may differ from the reference program's by a relative error of at most 0.017.
Values may be sent and summed in bfloat16 or wider, within the bound.
A program may use at most 192 MiB of HBM per device.

```python
import math
from functools import partial
import jax
import jax.numpy as jnp
from jax import lax

D = 1024
FF = 3072
HQ = 16
KVH = 8
HD = 128
SEQ = 128
QW = 2048
KW = 1024
TOKENS = 4096


def draw_tokens_in(key, part):
    base_key = jax.random.fold_in(key, 101)
    first, second = jax.random.split(base_key)
    scales = jnp.exp(jax.random.uniform(second, (TOKENS, 1), jnp.float32, math.log(0.5), math.log(5.0)))
    base = jnp.clip(jax.random.normal(first, (TOKENS, D), jnp.float32), -4.0, 4.0)
    return (base * scales).astype(jnp.bfloat16)


def draw_out_cotangent(key, part):
    base_key = jax.random.fold_in(key, 111)
    ladder = jnp.arange(TOKENS, dtype=jnp.float32)[:, None] / max(TOKENS - 1, 1)
    ramp = 1.0 + 2.0 * ladder
    base = jnp.clip(jax.random.normal(base_key, (TOKENS, D), jnp.float32), -4.0, 4.0)
    return (base * ramp).astype(jnp.bfloat16)


def draw_q_gain(key, part):
    base_key = jax.random.fold_in(key, 301)
    return jax.random.uniform(base_key, (HD,), jnp.float32, 0.6, 1.6)


def draw_k_gain(key, part):
    base_key = jax.random.fold_in(key, 302)
    return jax.random.uniform(base_key, (HD,), jnp.float32, 0.6, 1.6)


def key_columns(key):
    base = jax.random.normal(jax.random.fold_in(key, 201), (D, KVH * HD), jnp.float32)
    return jnp.clip(base, -4.0, 4.0) * D ** (-0.5)


def draw_w_key(key, part):
    return key_columns(key).astype(jnp.bfloat16)


def draw_w_query(key, part):
    noise = jnp.clip(jax.random.normal(jax.random.fold_in(key, 202), (D, HQ * HD), jnp.float32), -4.0, 4.0) * D ** (-0.5)
    return noise.astype(jnp.bfloat16)


def document_layout(key):
    seq_count = TOKENS // SEQ
    base_key = jax.random.fold_in(key, 401)
    first, second, third = jax.random.split(base_key, 3)
    row_index = jnp.arange(seq_count, dtype=jnp.int32)[:, None]
    cuts = jax.random.randint(first, (seq_count, 2), 1, SEQ)
    present = jax.random.randint(second, (seq_count, 2), 0, 2)
    present = jnp.where(row_index == seq_count - 1, 1, jnp.where(row_index == 0, 0, present))
    cuts = jnp.where(present == 1, cuts, SEQ)
    lower = jnp.min(cuts, axis=1, keepdims=True)
    upper = jnp.max(cuts, axis=1, keepdims=True)
    offset = jax.random.randint(third, (seq_count, 1), 0, 1800)
    offset = jnp.where(row_index == 0, 1799, offset)
    ladder = jnp.arange(SEQ, dtype=jnp.int32)[None, :]
    passed = (ladder >= lower).astype(jnp.int32) + (ladder >= upper).astype(jnp.int32)
    start = jnp.where(ladder >= upper, upper, jnp.where(ladder >= lower, lower, -offset))
    seg_ids = row_index * 3 + passed
    places = ladder - start
    return (seg_ids.reshape(-1).astype(jnp.int32), places.reshape(-1).astype(jnp.int32))


def draw_segment_ids(key, part):
    return document_layout(key)[0]


def draw_positions(key, part):
    return document_layout(key)[1]


def steps_of(own_key, dims, cuts, least, top_value):
    factor_of, own = 1.0, jax.random.fold_in(own_key, 6)
    for position, blocks in cuts:
        draws = jnp.exp(jax.random.uniform(jax.random.fold_in(own, position), (blocks,), jnp.float32, least / len(cuts), top_value / len(cuts)))
        factor_of = factor_of * jnp.repeat(draws, dims[position] // blocks).reshape([-1 if axis == position else 1 for axis in range(len(dims))])
    return factor_of


def centred(key, shape, spread, bound, shards=(), kind=jnp.bfloat16):
    array = jax.random.normal(key, shape, jnp.float32) * spread
    if len(shards) > 0:
        array = steps_of(key, shape, shards, -0.22, 0.18) * array
    return jnp.clip(array, min=-bound, max=bound).astype(kind)


def setup_inputs(seed: int = 0) -> dict:
    seeds = jax.random.split(jax.random.key(seed), 16)
    tokens_in = draw_tokens_in(jax.random.fold_in(seeds[15], 71), 0)
    input_gain = jnp.clip(1.0 + 0.15 * jax.random.normal(seeds[1], (D,), jnp.float32), 0.25, 1.75)
    q_gain = draw_q_gain(jax.random.fold_in(seeds[15], 71), 0)
    k_gain = draw_k_gain(jax.random.fold_in(seeds[15], 71), 0)
    w_query = draw_w_query(jax.random.fold_in(seeds[15], 71), 0)
    w_key = draw_w_key(jax.random.fold_in(seeds[15], 71), 0)
    w_value = centred(seeds[6], (D, KW), D ** -0.5, 0.1875, ((0, 4),))
    w_output = centred(seeds[7], (QW, D), HD ** -0.5, 0.5, ((0, 4),))
    post_gain = jnp.clip(1.0 + 0.15 * jax.random.normal(seeds[8], (D,), jnp.float32), 0.25, 1.75)
    w_gate = centred(seeds[9], (D, FF), D ** -0.5, 0.1875, ((0, 4),))
    w_up = centred(seeds[10], (D, FF), D ** -0.5, 0.1875, ((0, 4),))
    w_down = centred(seeds[11], (FF, D), FF ** -0.5, 0.109375, ((0, 4),))
    segment_ids = draw_segment_ids(jax.random.fold_in(seeds[15], 71), 0)
    positions = draw_positions(jax.random.fold_in(seeds[15], 71), 0)
    out_cotangent = draw_out_cotangent(jax.random.fold_in(seeds[15], 71), 0)
    return dict(tokens_in=tokens_in, input_gain=input_gain, q_gain=q_gain, k_gain=k_gain, w_query=w_query, w_key=w_key, w_value=w_value, w_output=w_output, post_gain=post_gain, w_gate=w_gate, w_up=w_up, w_down=w_down, segment_ids=segment_ids, positions=positions, out_cotangent=out_cotangent)


EPS = 1e-06
ROPE_BASE = 1000000.0
NEG_FILL = -1e+30

def rms_scale(values):
    return lax.rsqrt(lax.optimization_barrier(jnp.mean(values * values, axis=-1, keepdims=True)) + EPS)

def rope_tables(places, width):
    halfway = width // 2
    ladder = jnp.arange(halfway, dtype=jnp.float32)
    inverse = jnp.exp(ladder * (-2.0 * math.log(ROPE_BASE) / width))
    angles = places.astype(jnp.float32)[:, None] * inverse[None, :]
    cosine = jnp.cos(angles)
    sine = jnp.sin(angles)
    return (jnp.concatenate([cosine, cosine], -1)[:, None, :], jnp.concatenate([sine, sine], -1)[:, None, :])

def rotate(values):
    halfway = values.shape[-1] // 2
    return jnp.concatenate([-values[..., halfway:], values[..., :halfway]], -1)

def apply_rope(values, cosine, sine):
    return values * cosine + rotate(values) * sine

def undo_rope(grads, cosine, sine):
    return grads * cosine - rotate(grads * sine)

def norm_back(grads, values, scale, gain):
    normal = values * scale
    gain_term = lax.optimization_barrier(jnp.sum(grads * normal, axis=tuple(range(grads.ndim - 1))))
    scaled = grads * gain
    back = scale * (scaled - normal * lax.optimization_barrier(jnp.mean(scaled * normal, axis=-1, keepdims=True)))
    return (back, gain_term)

def times_transposed(first, second):
    return lax.dot_general(first, second, (((1,), (1,)), ((), ())), preferred_element_type=jnp.float32)

def transposed_times(first, second):
    return lax.dot_general(first, second, (((0,), (0,)), ((), ())), preferred_element_type=jnp.float32)

def score_block(q_rot, k_rot, seg_ids, groups):
    length = q_rot.shape[0]
    heads_kv = k_rot.shape[1]
    width = k_rot.shape[2]
    grouped = q_rot.reshape(length, heads_kv, groups, width)
    scores = jnp.einsum('qkgd,tkd->kgqt', grouped.astype(jnp.float32), k_rot.astype(jnp.float32)) * width ** (-0.5)
    ladder = jnp.arange(length)
    allowed = (seg_ids[:, None] == seg_ids[None, :]) & (ladder[:, None] >= ladder[None, :])
    return (grouped, scores, allowed)

def attend_forward(q_rot, k_rot, values, seg_ids, groups):
    grouped, scores, allowed = score_block(q_rot, k_rot, seg_ids, groups)
    masked = jnp.where(allowed, scores, NEG_FILL)
    top = lax.optimization_barrier(jnp.max(masked, axis=-1, keepdims=True))
    log_total = top + jnp.log(lax.optimization_barrier(jnp.sum(jnp.exp(masked - top), axis=-1, keepdims=True)))
    probs = jnp.where(allowed, jnp.exp(masked - log_total), 0.0).astype(jnp.bfloat16)
    mixed = jnp.einsum('kgqt,tkd->qkgd', probs.astype(jnp.float32), values.astype(jnp.float32))
    return (mixed.reshape(q_rot.shape[0], -1).astype(jnp.bfloat16), log_total)

def attend_backward(q_rot, k_rot, values, seg_ids, log_total, d_mixed, groups):
    grouped, scores, allowed = score_block(q_rot, k_rot, seg_ids, groups)
    width = k_rot.shape[2]
    weights = jnp.where(allowed, jnp.exp(jnp.where(allowed, scores, NEG_FILL) - log_total), 0.0)
    d_grouped = d_mixed.reshape(grouped.shape)
    d_weights = jnp.einsum('qkgd,tkd->kgqt', d_grouped.astype(jnp.float32), values.astype(jnp.float32))
    centre = lax.optimization_barrier(jnp.sum(weights * d_weights, axis=-1, keepdims=True))
    d_scores = (weights * (d_weights - centre) * width ** (-0.5)).astype(jnp.bfloat16)
    d_query = jnp.einsum('kgqt,tkd->qkgd', d_scores.astype(jnp.float32), k_rot.astype(jnp.float32))
    d_key = jnp.einsum('kgqt,qkgd->tkd', d_scores.astype(jnp.float32), grouped.astype(jnp.float32))
    d_value = jnp.einsum('kgqt,qkgd->tkd', weights.astype(jnp.bfloat16).astype(jnp.float32), d_grouped.astype(jnp.float32))
    return (d_query.reshape(q_rot.shape), d_key, d_value)

def layer_forward(tokens, seg_ids, places, input_gain, q_gain, k_gain, w_query, w_key, w_value, w_output, post_gain, w_gate, w_up, w_down, seq_len):
    rows_total = tokens.shape[0]
    width = q_gain.shape[0]
    seqs = rows_total // seq_len
    heads_q = w_query.shape[1] // width
    heads_kv = w_key.shape[1] // width
    groups = heads_q // heads_kv
    tokens_float = tokens.astype(jnp.float32)
    in_scale = rms_scale(tokens_float)
    normed = (tokens_float * in_scale * input_gain).astype(jnp.bfloat16)
    queries = jnp.dot(normed, w_query, preferred_element_type=jnp.float32).reshape(rows_total, heads_q, width)
    keys = jnp.dot(normed, w_key, preferred_element_type=jnp.float32).reshape(rows_total, heads_kv, width)
    values = jnp.dot(normed, w_value, preferred_element_type=jnp.float32).astype(jnp.bfloat16).reshape(rows_total, heads_kv, width)
    cosine, sine = rope_tables(places, width)
    q_scale = rms_scale(queries)
    k_scale = rms_scale(keys)
    q_rot = apply_rope(queries * q_scale * q_gain, cosine, sine).astype(jnp.bfloat16)
    k_rot = apply_rope(keys * k_scale * k_gain, cosine, sine).astype(jnp.bfloat16)
    attend = jax.vmap(partial(attend_forward, groups=groups))
    mixed, log_total = attend(q_rot.reshape(seqs, seq_len, heads_q, width), k_rot.reshape(seqs, seq_len, heads_kv, width), values.reshape(seqs, seq_len, heads_kv, width), seg_ids.reshape(seqs, seq_len))
    attended = mixed.reshape(rows_total, heads_q * width)
    middle = tokens_float + jnp.dot(attended, w_output, preferred_element_type=jnp.float32)
    post_scale = rms_scale(middle)
    post_normed = (middle * post_scale * post_gain).astype(jnp.bfloat16)
    gate = jnp.dot(post_normed, w_gate, preferred_element_type=jnp.float32)
    up_proj = jnp.dot(post_normed, w_up, preferred_element_type=jnp.float32)
    hidden = (jax.nn.silu(gate) * up_proj).astype(jnp.bfloat16)
    block_out = (middle + jnp.dot(hidden, w_down, preferred_element_type=jnp.float32)).astype(jnp.bfloat16)
    saved = (tokens_float, in_scale, normed, queries, keys, q_scale, k_scale, values, q_rot, k_rot, cosine, sine, log_total, attended, middle, post_scale, post_normed, gate, up_proj, hidden)
    return (block_out, saved)

def layer_backward(saved, seg_ids, cotangent, input_gain, q_gain, k_gain, w_query, w_key, w_value, w_output, post_gain, w_gate, w_up, w_down, seq_len):
    tokens_float, in_scale, normed, queries, keys, q_scale, k_scale, values, q_rot, k_rot, cosine, sine, log_total, attended, middle, post_scale, post_normed, gate, up_proj, hidden = saved
    rows_total = tokens_float.shape[0]
    width = q_gain.shape[0]
    seqs = rows_total // seq_len
    heads_q = queries.shape[1]
    heads_kv = keys.shape[1]
    groups = heads_q // heads_kv
    d_hidden = times_transposed(cotangent, w_down)
    sigm = jax.nn.sigmoid(gate)
    d_gate = (d_hidden * up_proj * sigm * (1.0 + gate * (1.0 - sigm))).astype(jnp.bfloat16)
    d_up = (d_hidden * gate * sigm).astype(jnp.bfloat16)
    d_post = times_transposed(d_gate, w_gate) + times_transposed(d_up, w_up)
    d_norm_mid, post_term = norm_back(d_post, middle, post_scale, post_gain)
    d_middle = cotangent.astype(jnp.float32) + d_norm_mid
    d_attn_out = d_middle.astype(jnp.bfloat16)
    d_attended = times_transposed(d_attn_out, w_output).astype(jnp.bfloat16)
    attend_back = jax.vmap(partial(attend_backward, groups=groups))
    d_qrot, d_krot, d_vals = attend_back(q_rot.reshape(seqs, seq_len, heads_q, width), k_rot.reshape(seqs, seq_len, heads_kv, width), values.reshape(seqs, seq_len, heads_kv, width), seg_ids.reshape(seqs, seq_len), log_total, d_attended.reshape(seqs, seq_len, heads_q * width))
    q_back = undo_rope(d_qrot.reshape(rows_total, heads_q, width), cosine, sine)
    k_back = undo_rope(d_krot.reshape(rows_total, heads_kv, width), cosine, sine)
    d_q_float, q_term = norm_back(q_back, queries, q_scale, q_gain)
    d_k_float, k_term = norm_back(k_back, keys, k_scale, k_gain)
    d_queries = d_q_float.astype(jnp.bfloat16).reshape(rows_total, heads_q * width)
    d_keys = d_k_float.astype(jnp.bfloat16).reshape(rows_total, heads_kv * width)
    d_values = d_vals.astype(jnp.bfloat16).reshape(rows_total, heads_kv * width)
    d_normed = times_transposed(d_queries, w_query) + times_transposed(d_keys, w_key) + times_transposed(d_values, w_value)
    d_tokens, in_term = norm_back(d_normed, tokens_float, in_scale, input_gain)
    input_grad = (d_middle + d_tokens).astype(jnp.bfloat16)
    gains = (in_term, q_term, k_term, post_term)
    pairs = ((normed, d_queries), (normed, d_keys), (normed, d_values), (attended, d_attn_out), (post_normed, d_gate), (post_normed, d_up), (hidden, cotangent))
    return (input_grad, gains, pairs)

def reference(tokens_in, input_gain, q_gain, k_gain, w_query, w_key, w_value, w_output, post_gain, w_gate, w_up, w_down, segment_ids, positions, out_cotangent):
    seq_count = TOKENS // SEQ
    per_block = math.gcd(seq_count, max(1, 4096 // SEQ))
    block_rows = per_block * SEQ
    blocks_total = TOKENS // block_rows
    weights = (w_query, w_key, w_value, w_output, post_gain, w_gate, w_up, w_down)

    def step(carry, block):
        tokens, seg_ids, places, cotangent = block
        block_out, saved = layer_forward(tokens, seg_ids, places, input_gain, q_gain, k_gain, *weights, SEQ)
        input_grad, gains, pairs = layer_backward(saved, seg_ids, cotangent, input_gain, q_gain, k_gain, *weights, SEQ)
        grads = tuple((transposed_times(first, second) for first, second in pairs))
        updated = tuple((total + term for total, term in zip(carry, gains + grads)))
        return (updated, (block_out, input_grad))
    shapes = [(D,), (HD,), (HD,), (D,), (D, QW), (D, KW), (D, KW), (QW, D), (D, FF), (D, FF), (FF, D)]
    init = tuple((jnp.zeros(shape, jnp.float32) for shape in shapes))
    blocks = (tokens_in.reshape(blocks_total, block_rows, D), segment_ids.reshape(blocks_total, block_rows), positions.reshape(blocks_total, block_rows), out_cotangent.reshape(blocks_total, block_rows, D))
    carry, (outs, grads_in) = lax.scan(step, init, blocks)
    return (outs.reshape(TOKENS, D), grads_in.reshape(TOKENS, D), carry[0], carry[1], carry[2], carry[3], carry[4], carry[5], carry[6], carry[7], carry[8], carry[9], carry[10])
```

```python
from functools import partial
import math

import jax
import jax.numpy as jnp
from jax import lax
from jax.experimental import pallas as pl
from jax.experimental.pallas import tpu as pltpu
from jax.sharding import PartitionSpec as P

EPS = 1e-06
ROPE_BASE = 1000000.0
NEG_FILL = -1e30
F32 = jnp.float32
BF16 = jnp.bfloat16
VMEM_LIMIT = 60 * 1024 * 1024


def dot(first, second):
    return lax.dot_general(first, second, (((1,), (0,)), ((), ())), preferred_element_type=F32)


def dot_nt(first, second):
    return lax.dot_general(first, second, (((1,), (1,)), ((), ())), preferred_element_type=F32)


def dot_tn(first, second):
    return lax.dot_general(first, second, (((0,), (0,)), ((), ())), preferred_element_type=F32)


def rms_scale(values):
    return lax.rsqrt(jnp.mean(values * values, axis=-1, keepdims=True) + EPS)


def flip(index, bits):
    out = index
    step = 1
    while step <= bits:
        if bits & step:
            out = out + step * (1 - 2 * lax.rem(index // step, 2))
        step *= 2
    return out


def sizes_of(mesh_sizes, tokens, w_query, w_key, w_output, w_gate, w_down, q_gain):
    reps, fsdp = mesh_sizes
    width = q_gain.shape[0]
    heads_q = w_query.shape[1] // width
    heads_kv = w_key.shape[1] // width
    team = math.gcd(reps, heads_kv)
    assert team >= 2 and team & (team - 1) == 0 and team % fsdp == 0
    dims = dict(
        reps=reps,
        fsdp=fsdp,
        team=team,
        width=width,
        seq=tokens.shape[0],
        model=tokens.shape[1],
        kv=heads_kv // team,
        ratio=heads_q // heads_kv,
        qcols=w_query.shape[1] // team,
        kcols=w_key.shape[1] // team,
        ffcols=w_gate.shape[1] // team,
        band=w_query.shape[0],
        share=team // fsdp,
    )
    return dims


def layer_kernel(names, dims, *refs):
    r = dict(zip(names, refs))
    team, fsdp = dims["team"], dims["fsdp"]
    seq, model, width = dims["seq"], dims["model"], dims["width"]
    kv, ratio, band, share = dims["kv"], dims["ratio"], dims["band"], dims["share"]
    qc, kc, fc = dims["qcols"], dims["kcols"], dims["ffcols"]
    chips = team // 2
    half = width // 2

    rep = lax.axis_index("rep")
    z = lax.axis_index("fsdp")
    me = lax.rem(rep, team)
    base = rep - me
    home = me // share

    def place(member, plane):
        return {"rep": base + member, "fsdp": plane}

    def remote(src, dst, send_sem, recv_sem, member, plane):
        return pltpu.make_async_remote_copy(
            src_ref=src,
            dst_ref=dst,
            send_sem=send_sem,
            recv_sem=recv_sem,
            device_id=place(member, plane),
            device_id_type=pl.DeviceIdType.MESH,
        )

    pending = []

    def launch(copy, cond=None):
        if cond is None:
            copy.start()
        else:
            pl.when(cond)(copy.start)
        pending.append((cond, copy))

    def guarded(cond, action):
        if cond is None:
            action()
        else:
            pl.when(cond)(action)

    def rows(ref, index, count):
        return ref.at[pl.ds(pl.multiple_of(index * count, count), count)]

    def loop(count, step):
        def run(index, carry):
            step(index)
            return carry

        lax.fori_loop(0, count, run, 0)

    def gather_start(job, view, own=None, active=None):
        cond = None if active is None else active(me)
        for bits in [2 * chip for chip in range(1, chips)] + [1]:
            src = view(me) if own is None else own
            launch(
                remote(
                    src,
                    view(me),
                    r["ag_send"].at[job, bits],
                    r["ag_recv"].at[job, bits],
                    flip(me, bits),
                    z,
                ),
                cond,
            )

    def gather_wait(job, view, bits, active=None):
        block = view(flip(me, bits))
        cond = None if active is None else active(flip(me, bits))
        copy = remote(
            block, block, r["ag_send"].at[job, bits], r["ag_recv"].at[job, bits], flip(me, 1), z
        )
        guarded(cond, copy.wait_recv)

    def gather_forward(job, view, active=None):
        for chip in range(1, chips):
            bits = 2 * chip
            gather_wait(job, view, bits, active)
            block = view(flip(me, bits))
            cond = None if active is None else active(flip(me, bits))
            launch(
                remote(
                    block,
                    block,
                    r["ag_send"].at[job, bits + 1],
                    r["ag_recv"].at[job, bits + 1],
                    flip(me, 1),
                    z,
                ),
                cond,
            )

    def gather_finish(job, view, active=None):
        for chip in range(chips):
            gather_wait(job, view, 2 * chip + 1, active)

    def scatter_start(job, part):
        for chip in reversed(range(chips)):
            bits = 2 * chip + 1
            r["rs_out"][job, chip] = part(flip(me, bits)).astype(BF16)
            launch(
                remote(
                    r["rs_out"].at[job, chip],
                    r["rs_in"].at[job, chip],
                    r["rs_sem"].at[job, 0, chip],
                    r["rs_sem"].at[job, 1, chip],
                    flip(me, 1),
                    z,
                )
            )

        def arrived(chip):
            block = r["rs_in"].at[job, chip]
            remote(
                block,
                block,
                r["rs_sem"].at[job, 0, chip],
                r["rs_sem"].at[job, 1, chip],
                flip(me, 1),
                z,
            ).wait_recv()

        for chip in list(reversed(range(1, chips))):
            mine = part(flip(me, 2 * chip))
            arrived(chip)
            r["rs_in"][job, chip] = (mine + r["rs_in"][job, chip].astype(F32)).astype(BF16)
            launch(
                remote(
                    r["rs_in"].at[job, chip],
                    r["rs_last"].at[job, chip - 1],
                    r["rs_sem"].at[job, 2, chip],
                    r["rs_sem"].at[job, 3, chip],
                    flip(me, 2 * chip),
                    z,
                )
            )
        mine = part(me)
        arrived(0)
        r["rs_sum"][job] = mine + r["rs_in"][job, 0].astype(F32)

    def scatter_finish(job):
        total = r["rs_sum"][job]
        for chip in range(1, chips):
            block = r["rs_last"].at[job, chip - 1]
            remote(
                block,
                block,
                r["rs_sem"].at[job, 2, chip],
                r["rs_sem"].at[job, 3, chip],
                flip(me, 2 * chip),
                z,
            ).wait_recv()
            total = total + r["rs_last"][job, chip - 1].astype(F32)
        return total

    wide = (r["w_qkv"], r["w_gu"])
    tall = (r["w_o"], r["w_d"])
    tall_rows = (qc, fc)

    def wide_block(which, plane):
        return rows(wide[which], plane, band)

    def wide_own(which):
        block = wide_block(which, z)
        for way, cond, target in ((0, z < fsdp - 1, z + 1), (1, z > 0, z - 1)):
            launch(
                remote(
                    block,
                    block,
                    r["ww_send"].at[which, way, 0],
                    r["ww_recv"].at[which, z],
                    me,
                    target,
                ),
                cond,
            )

    def wide_pass(which, step):
        for way, exists, plane, more, target in (
            (0, z - step >= 0, z - step, z < fsdp - 1, z + 1),
            (1, z + step <= fsdp - 1, z + step, z > 0, z - 1),
        ):
            plane = jnp.clip(plane, 0, fsdp - 1)
            block = wide_block(which, plane)
            copy = remote(
                block,
                block,
                r["ww_send"].at[which, way, step],
                r["ww_recv"].at[which, plane],
                me,
                jnp.clip(target, 0, fsdp - 1),
            )
            pl.when(exists)(copy.wait_recv)
            if step < fsdp - 1:
                launch(copy, jnp.logical_and(exists, more))

    def tall_chunks(which):
        return tall_rows[which] // width

    def tall_pass(which, chunk):
        block = tall[which].at[pl.ds(chunk * width, width)]
        for way, cond, target in (
            (0, jnp.logical_and(z >= home, z < fsdp - 1), z + 1),
            (1, jnp.logical_and(z <= home, z > 0), z - 1),
        ):
            copy = remote(
                block,
                block,
                r["wt_send"].at[which, way, chunk],
                r["wt_recv"].at[which, chunk],
                me,
                jnp.clip(target, 0, fsdp - 1),
            )
            if way == 0:
                pl.when(z != home)(copy.wait_recv)
            launch(copy, cond)

    wide_sum = (r["g_qkv"], r["g_gu"])
    tall_sum = (r["g_o"], r["g_d"])
    wide_flow = (r["f_qkv"], r["f_gu"])
    tall_flow = (r["f_o"], r["f_d"])
    wide_out = (r["l_qkv"], r["l_gu"])
    tall_out = (r["l_o"], r["l_d"])

    def merge(target, own, start, count, has_incoming):
        step = 32

        def one(index):
            at = pl.ds(pl.multiple_of(start + index * step, step), step)
            value = own[at]
            if has_incoming:
                value = value + target[at].astype(F32)
            target[at] = value.astype(BF16)

        loop(count // step, one)


    def wide_level(which, level):
        for way, here in ((0, level), (1, fsdp - 1 - level)):
            flow = wide_flow[which].at[way]
            planes = range(fsdp - 1, here, -1) if way == 0 else range(here)
            target = here + 1 if way == 0 else here - 1
            copies = [
                remote(
                    flow.at[pl.ds(plane * band, band)],
                    flow.at[pl.ds(plane * band, band)],
                    r["gw_send"].at[which, way, plane],
                    r["gw_recv"].at[which, way, plane],
                    me,
                    target,
                )
                for plane in planes
            ]

            def act(flow=flow, planes=planes, copies=copies):
                for plane, copy in zip(planes, copies):
                    if level > 0:
                        copy.wait_recv()
                    merge(flow, wide_sum[which], plane * band, band, level > 0)
                    copy.start()

            cond = z == here
            pl.when(cond)(act)
            for copy in copies:
                pending.append((cond, copy))

    def wide_final(which):
        def take(way):
            flow = wide_flow[which].at[way]
            block = rows(flow, z, band)
            remote(
                block,
                block,
                r["gw_send"].at[which, way, z],
                r["gw_recv"].at[which, way, z],
                me,
                z,
            ).wait_recv()
            step = 32

            def one(index):
                at = pl.ds(pl.multiple_of(z * band + index * step, step), step)
                wide_sum[which][at] = wide_sum[which][at] + flow[at].astype(F32)

            loop(band // step, one)

        pl.when(z > 0)(lambda: take(0))
        pl.when(z < fsdp - 1)(lambda: take(1))
        wide_out[which][...] = rows(wide_sum[which], z, band)[...].astype(BF16)

    def tall_level(which, level):
        for way, here in ((0, level), (1, fsdp - 1 - level)):
            flow = tall_flow[which].at[way]
            target = here + 1 if way == 0 else here - 1
            copies = [
                remote(
                    flow.at[pl.ds(chunk * width, width)],
                    flow.at[pl.ds(chunk * width, width)],
                    r["gt_send"].at[which, way, chunk],
                    r["gt_recv"].at[which, way, chunk],
                    me,
                    target,
                )
                for chunk in range(tall_chunks(which))
            ]

            def act(flow=flow, copies=copies):
                for chunk, copy in enumerate(copies):
                    if level > 0:
                        copy.wait_recv()
                    merge(flow, tall_sum[which], chunk * width, width, level > 0)
                    copy.start()

            toward = home > here if way == 0 else home < here
            cond = jnp.logical_and(z == here, toward)
            pl.when(cond)(act)
            for copy in copies:
                pending.append((cond, copy))

    def tall_final(which):
        count = tall_rows[which]

        def take(way):
            flow = tall_flow[which].at[way]
            for chunk in range(tall_chunks(which)):
                block = flow.at[pl.ds(chunk * width, width)]
                remote(
                    block,
                    block,
                    r["gt_send"].at[which, way, chunk],
                    r["gt_recv"].at[which, way, chunk],
                    me,
                    z,
                ).wait_recv()
            step = 32

            def one(index):
                at = pl.ds(pl.multiple_of(index * step, step), step)
                tall_sum[which][at] = tall_sum[which][at] + flow[at].astype(F32)

            loop(count // step, one)

        pl.when(jnp.logical_and(z == home, z > 0))(lambda: take(0))
        pl.when(jnp.logical_and(z == home, z < fsdp - 1))(lambda: take(1))

        def close():
            tall_out[which][...] = tall_sum[which][...].astype(BF16)

        pl.when(z == home)(close)

    loads = []
    wide_at = lambda which, start, size: wide_block(which, z).at[:, pl.ds(start, size)]

    def column(ref, member, size):
        return ref.at[:, pl.ds(pl.multiple_of(member * size, size), size)]

    for src, dst in (
        (column(r["wq"], me, qc), wide_at(0, 0, qc)),
        (column(r["wk"], me, kc), wide_at(0, qc, kc)),
        (column(r["wv"], me, kc), wide_at(0, qc + kc, kc)),
        (column(r["wg"], me, fc), wide_at(1, 0, fc)),
        (column(r["wu"], me, fc), wide_at(1, fc, fc)),
    ):
        load = pltpu.make_async_copy(src, dst, r["load_sem"].at[len(loads)])
        load.start()
        loads.append(load)
    slot = lax.rem(me, share)
    tall_loads = []
    for which, src in ((0, r["wo"]), (1, r["wd"])):
        load = pltpu.make_async_copy(
            rows(src, slot, tall_rows[which]), tall[which], r["load_sem"].at[5 + which]
        )
        pl.when(z == home)(load.start)
        tall_loads.append(load)

    barrier = pltpu.get_barrier_semaphore()
    partners = [2 * chip for chip in range(1, chips)] + [1]
    for bits in partners:
        pl.semaphore_signal(
            barrier,
            inc=1,
            device_id=place(flip(me, bits), z),
            device_id_type=pl.DeviceIdType.MESH,
        )
    for away in range(1, fsdp):
        pl.semaphore_signal(
            barrier,
            inc=1,
            device_id=place(me, lax.rem(z + away, fsdp)),
            device_id_type=pl.DeviceIdType.MESH,
        )

    tokens = r["tokens"][...].astype(F32)
    in_scale = rms_scale(tokens)
    rows(r["xn"], me, seq)[...] = (tokens * in_scale * r["in_gain"][...]).astype(BF16)
    rows(r["tab"], me, seq)[...] = r["table"][...]
    rows(r["msk"], me, seq)[...] = r["mask"][...]
    rows(r["cot"], me, seq)[...] = r["cotangent"][...]
    r["gain_own"][...] = jnp.zeros_like(r["gain_own"])

    pl.semaphore_wait(barrier, len(partners) + fsdp - 1)

    view_xn = lambda member: rows(r["xn"], member, seq)
    view_tab = lambda member: rows(r["tab"], member, seq)
    view_msk = lambda member: rows(r["msk"], member, seq)
    view_cot = lambda member: rows(r["cot"], member, seq)
    view_pn = lambda member: rows(r["pn"], member, seq)
    view_da = lambda member: rows(r["da"], member, seq)

    for load in loads[:3]:
        load.wait()
    wide_own(0)
    gather_start(0, view_xn)
    gather_start(1, view_tab)
    gather_start(2, view_msk)
    gather_start(3, view_cot)
    for load in tall_loads:
        pl.when(z == home)(load.wait)
    for load in loads[3:]:
        load.wait()

    def pass_tall_source(which):
        for chunk in range(tall_chunks(which)):
            tall_pass(which, chunk)

    for step in range(1, fsdp):
        wide_pass(0, step)
        if step == 1:
            wide_own(1)
        if step == 1:
            for job, view in ((0, view_xn), (1, view_tab), (2, view_msk)):
                gather_forward(job, view)
    for job, view in ((0, view_xn), (1, view_tab), (2, view_msk)):
        gather_finish(job, view)

    lane = lax.broadcasted_iota(jnp.int32, (seq, width), 1)
    front = lane < half
    sign = jnp.where(front, -1.0, 1.0).astype(F32)
    root = width ** (-0.5)

    def turn(values):
        return pltpu.roll(values, half, 1)

    def tables(at):
        table = r["tab"][at]
        swapped = turn(table)
        return jnp.where(front, table, swapped), jnp.where(front, swapped, table)

    def at_seq(index):
        return pl.ds(pl.multiple_of(index * seq, seq), seq)

    def attend(index):
        at = at_seq(index)
        cosine, sine = tables(at)
        signed = sine * sign
        qkv = dot(r["xn"][at], r["w_qkv"][...])
        r["qk"][at] = qkv[:, : qc + kc]
        allowed = r["msk"][at].astype(F32) > 0.5
        allowed = jnp.concatenate([allowed] * ratio, 0) if ratio > 1 else allowed

        def spun(values, gain):
            values = values * rms_scale(values) * gain
            return (values * cosine + turn(values) * signed).astype(BF16)

        for group in range(kv):
            k_rot = spun(qkv[:, qc + group * width : qc + (group + 1) * width], r["kg"][...])
            start = qc + kc + group * width
            values = qkv[:, start : start + width].astype(BF16)
            spins = []
            for head in range(ratio):
                place_at = (group * ratio + head) * width
                spin = spun(qkv[:, place_at : place_at + width], r["qg"][...])
                r["rot"][at, place_at : place_at + width] = spin
                spins.append(spin)
            r["rot"][at, qc + group * width : qc + (group + 1) * width] = k_rot
            r["rot"][at, start : start + width] = values
            q_rot = jnp.concatenate(spins, 0)
            scores = dot_nt(q_rot, k_rot) * root
            masked = jnp.where(allowed, scores, NEG_FILL)
            top = jnp.max(masked, axis=-1, keepdims=True)
            total = top + jnp.log(jnp.sum(jnp.exp(masked - top), axis=-1, keepdims=True))
            probs = jnp.where(allowed, jnp.exp(masked - total), 0.0)
            r["probs"][index, group] = probs
            mixed = dot(probs.astype(BF16), values).astype(BF16)
            for head in range(ratio):
                place_at = (group * ratio + head) * width
                r["att"][at, place_at : place_at + width] = mixed[head * seq : (head + 1) * seq]

    loop(team, attend)

    pass_tall_source(0)
    for step in range(1, fsdp - 1):
        wide_pass(1, step)
    scatter_start(0, lambda member: dot(rows(r["att"], member, seq)[...], r["w_o"][...]))
    middle = tokens + scatter_finish(0)
    r["middle"][...] = middle
    post_scale = rms_scale(middle)
    view_pn(me)[...] = (middle * post_scale * r["post_gain"][...]).astype(BF16)
    gather_start(4, view_pn)
    gather_forward(3, view_cot)
    wide_pass(1, fsdp - 1)
    pass_tall_source(1)
    gather_forward(4, view_pn)
    gather_finish(3, view_cot)
    gather_finish(4, view_pn)

    def feed(index):
        at = at_seq(index)
        both = dot(r["pn"][at], r["w_gu"][...])
        gate, up = both[:, :fc], both[:, fc:]
        sigm = jax.nn.sigmoid(gate)
        soft = gate * sigm
        r["hid"][at] = (soft * up).astype(BF16)
        d_hidden = dot_nt(r["cot"][at], r["w_d"][...])
        r["dgu"][at, :fc] = (d_hidden * up * sigm * (1.0 + gate * (1.0 - sigm))).astype(BF16)
        r["dgu"][at, fc:] = (d_hidden * soft).astype(BF16)

    loop(team, feed)

    scatter_start(1, lambda member: dot_nt(rows(r["dgu"], member, seq)[...], r["w_gu"][...]))
    r["g_d"][...] = dot_tn(r["hid"][...], r["cot"][...])
    tall_level(1, 0)

    def grad_gu(index):
        at = pl.ds(pl.multiple_of(index * band, band), band)
        r["g_gu"][at] = dot_tn(r["pn"][:, at], r["dgu"][...])

    def grad_qkv(index):
        at = pl.ds(pl.multiple_of(index * band, band), band)
        r["g_qkv"][at] = dot_tn(r["xn"][:, at], r["dqkv"][...])

    loop(fsdp, grad_gu)
    wide_level(1, 0)

    def norm_back(grads, values, scale, gain):
        normal = values * scale
        gain_term = jnp.sum(grads * normal, axis=0, keepdims=True)
        scaled = grads * gain
        back = scale * (scaled - normal * jnp.mean(scaled * normal, axis=-1, keepdims=True))
        return back, gain_term

    d_post = scatter_finish(1)
    middle = r["middle"][...]
    back, term = norm_back(d_post, middle, rms_scale(middle), r["post_gain"][...])
    r["gain_own"][1:2] = term
    d_middle = r["cotangent"][...].astype(F32) + back
    r["d_middle"][...] = d_middle
    view_da(me)[...] = d_middle.astype(BF16)
    gather_start(5, view_da)
    for level in range(1, fsdp - 1):
        tall_level(1, level)
    gather_forward(5, view_da)
    wide_level(1, 1) if fsdp > 2 else None
    gather_finish(5, view_da)
    scatter_start(2, lambda member: dot(rows(r["hid"], member, seq)[...], r["w_d"][...]))

    def attend_back(index):
        at = at_seq(index)
        cosine, sine = tables(at)
        d_att = dot_nt(r["da"][at], r["w_o"][...]).astype(BF16)

        def unspun(grads):
            return grads * cosine - turn(grads * sine) * sign

        for group in range(kv):
            k_at = slice(qc + group * width, qc + (group + 1) * width)
            v_at = slice(qc + kc + group * width, qc + kc + (group + 1) * width)
            heads = [
                slice((group * ratio + head) * width, (group * ratio + head + 1) * width)
                for head in range(ratio)
            ]
            d_mixed = jnp.concatenate([d_att[:, head] for head in heads], 0)
            q_rot = jnp.concatenate([r["rot"][at, head] for head in heads], 0)
            k_rot = r["rot"][at, k_at]
            values = r["rot"][at, v_at]
            probs = r["probs"][index, group]
            d_probs = dot_nt(d_mixed, values)
            centre = jnp.sum(probs * d_probs, axis=-1, keepdims=True)
            d_scores = (probs * (d_probs - centre) * root).astype(BF16)
            d_query = dot(d_scores, k_rot)
            d_key = dot_tn(d_scores, q_rot)
            d_value = dot_tn(probs.astype(BF16), d_mixed)
            for number, head in enumerate(heads):
                queries = r["qk"][at, head]
                back, term = norm_back(
                    unspun(d_query[number * seq : (number + 1) * seq]),
                    queries,
                    rms_scale(queries),
                    r["qg"][...],
                )
                r["dqkv"][at, head] = back.astype(BF16)
                r["gain_own"][2:3, :width] += term
            keys = r["qk"][at, k_at]
            back, term = norm_back(unspun(d_key), keys, rms_scale(keys), r["kg"][...])
            r["dqkv"][at, k_at] = back.astype(BF16)
            r["gain_own"][3:4, :width] += term
            r["dqkv"][at, v_at] = d_value.astype(BF16)

    loop(team, attend_back)
    scatter_start(3, lambda member: dot_nt(rows(r["dqkv"], member, seq)[...], r["w_qkv"][...]))
    loop(fsdp, grad_qkv)
    wide_level(0, 0)
    r["g_o"][...] = dot_tn(r["att"][...], r["da"][...])
    tall_level(0, 0)
    for level in range(2, fsdp - 1):
        wide_level(1, level)
    tall_final(1)

    def home_of(member):
        return member // share == z

    def tall_view(out, which):
        return lambda member: rows(out, lax.rem(member, share), tall_rows[which])

    stores = []

    def keep(src, dst, cond=None):
        copy = pltpu.make_async_copy(src, dst, r["store_sem"].at[len(stores)])
        guarded(cond, copy.start)
        stores.append((cond, copy))

    def send_tall(which, out, job):
        view = tall_view(out, which)
        keep(tall_out[which], view(me), home_of(me))
        gather_start(job, view, tall_out[which], home_of)

    def send_wide(which, parts):
        for job, out, start, size in parts:
            view = partial(column, out, size=size)
            own = wide_out[which].at[:, pl.ds(start, size)]
            keep(own, view(me))
            gather_start(job, view, own)

    gu_parts = ((8, r["gg"], 0, fc), (9, r["gu"], fc, fc))
    qkv_parts = ((10, r["gq"], 0, qc), (11, r["gk"], qc, kc), (12, r["gv"], qc + kc, kc))

    send_tall(1, r["gd"], 6)
    wide_final(1)
    send_wide(1, gu_parts)

    d_normed = scatter_finish(3)
    tokens = r["tokens"][...].astype(F32)
    back, term = norm_back(d_normed, tokens, rms_scale(tokens), r["in_gain"][...])
    r["gain_own"][0:1] = term
    r["out_grad"][...] = (r["d_middle"][...] + back).astype(BF16)

    for level in range(1, fsdp - 1):
        tall_level(0, level)
        wide_level(0, level)
    view_gain = lambda member: r["gain_all"].at[member]
    view_gain(me)[...] = r["gain_own"][...]
    gather_start(13, view_gain)
    r["out_block"][...] = (r["middle"][...] + scatter_finish(2)).astype(BF16)
    gather_forward(6, tall_view(r["gd"], 1), home_of)
    gather_forward(13, view_gain)
    tall_final(0)
    send_tall(0, r["go"], 7)
    wide_final(0)
    send_wide(0, qkv_parts)
    gather_finish(13, view_gain)
    total = r["gain_all"][0]
    for member in range(1, team):
        total = total + r["gain_all"][member]
    r["gain_line"][z] = total
    for away in range(1, fsdp):
        launch(
            remote(
                r["gain_line"].at[z],
                r["gain_line"].at[z],
                r["gl_sem"].at[0, away],
                r["gl_sem"].at[1, away],
                me,
                lax.rem(z + away, fsdp),
            )
        )
    for job, out, start, size in gu_parts:
        gather_forward(job, partial(column, out, size=size))
    for away in range(1, fsdp):
        block = r["gain_line"].at[lax.rem(z + fsdp - away, fsdp)]
        remote(
            block, block, r["gl_sem"].at[0, away], r["gl_sem"].at[1, away], me, z
        ).wait_recv()
    total = r["gain_line"][0]
    for plane in range(1, fsdp):
        total = total + r["gain_line"][plane]
    r["out_gain"][...] = total
    gather_forward(7, tall_view(r["go"], 0), home_of)
    for job, out, start, size in qkv_parts:
        gather_forward(job, partial(column, out, size=size))
    for job, out, start, size in gu_parts + qkv_parts:
        gather_finish(job, partial(column, out, size=size))
    gather_finish(6, tall_view(r["gd"], 1), home_of)
    gather_finish(7, tall_view(r["go"], 0), home_of)
    for cond, copy in stores:
        guarded(cond, copy.wait)
    for cond, copy in pending:
        guarded(cond, copy.wait_send)


def run_layer(dims, operands, weight_shapes):
    team, fsdp, seq, model = dims["team"], dims["fsdp"], dims["seq"], dims["model"]
    width, kv, ratio, band = dims["width"], dims["kv"], dims["ratio"], dims["band"]
    qc, kc, fc = dims["qcols"], dims["kcols"], dims["ffcols"]
    chips = team // 2
    qkv, gu, many = qc + 2 * kc, 2 * fc, team * seq
    jobs = 14
    chunks = max(qc, fc) // width
    inputs = [
        "tokens",
        "table",
        "mask",
        "cotangent",
        "in_gain",
        "post_gain",
        "qg",
        "kg",
        "wq",
        "wk",
        "wv",
        "wo",
        "wg",
        "wu",
        "wd",
    ]
    outputs = [
        "out_block",
        "out_grad",
        "out_gain",
        "gq",
        "gk",
        "gv",
        "go",
        "gg",
        "gu",
        "gd",
    ]
    dma = pltpu.SemaphoreType.DMA
    scratch = dict(
        xn=pltpu.VMEM((many, model), BF16),
        tab=pltpu.VMEM((many, width), F32),
        msk=pltpu.VMEM((many, seq), BF16),
        cot=pltpu.VMEM((many, model), BF16),
        pn=pltpu.VMEM((many, model), BF16),
        da=pltpu.VMEM((many, model), BF16),
        w_qkv=pltpu.VMEM((model, qkv), BF16),
        w_gu=pltpu.VMEM((model, gu), BF16),
        w_o=pltpu.VMEM((qc, model), BF16),
        w_d=pltpu.VMEM((fc, model), BF16),
        qk=pltpu.VMEM((many, qc + kc), F32),
        rot=pltpu.VMEM((many, qkv), BF16),
        probs=pltpu.VMEM((team, kv, ratio * seq, seq), F32),
        att=pltpu.VMEM((many, qc), BF16),
        hid=pltpu.VMEM((many, fc), BF16),
        dgu=pltpu.VMEM((many, gu), BF16),
        dqkv=pltpu.VMEM((many, qkv), BF16),
        middle=pltpu.VMEM((seq, model), F32),
        d_middle=pltpu.VMEM((seq, model), F32),
        rs_out=pltpu.VMEM((4, chips, seq, model), BF16),
        rs_in=pltpu.VMEM((4, chips, seq, model), BF16),
        rs_last=pltpu.VMEM((4, max(chips - 1, 1), seq, model), BF16),
        rs_sum=pltpu.VMEM((4, seq, model), F32),
        g_qkv=pltpu.VMEM((model, qkv), F32),
        g_gu=pltpu.VMEM((model, gu), F32),
        g_o=pltpu.VMEM((qc, model), F32),
        g_d=pltpu.VMEM((fc, model), F32),
        f_qkv=pltpu.VMEM((2, model, qkv), BF16),
        f_gu=pltpu.VMEM((2, model, gu), BF16),
        f_o=pltpu.VMEM((2, qc, model), BF16),
        f_d=pltpu.VMEM((2, fc, model), BF16),
        l_qkv=pltpu.VMEM((band, qkv), BF16),
        l_gu=pltpu.VMEM((band, gu), BF16),
        l_o=pltpu.VMEM((qc, model), BF16),
        l_d=pltpu.VMEM((fc, model), BF16),
        gain_own=pltpu.VMEM((8, model), F32),
        gain_all=pltpu.VMEM((team, 8, model), F32),
        gain_line=pltpu.VMEM((fsdp, 8, model), F32),
        ag_send=dma((jobs, team)),
        ag_recv=dma((jobs, team)),
        rs_sem=dma((4, 4, chips)),
        ww_send=dma((2, 2, fsdp)),
        ww_recv=dma((2, fsdp)),
        wt_send=dma((2, 2, chunks)),
        wt_recv=dma((2, chunks)),
        gw_send=dma((2, 2, fsdp)),
        gw_recv=dma((2, 2, fsdp)),
        gt_send=dma((2, 2, chunks)),
        gt_recv=dma((2, 2, chunks)),
        gl_sem=dma((2, fsdp)),
        load_sem=dma((7,)),
        store_sem=dma((7,)),
    )
    vmem = pl.BlockSpec(memory_space=pltpu.VMEM)
    anywhere = pl.BlockSpec(memory_space=pl.ANY)
    shapes = [
        jax.ShapeDtypeStruct((seq, model), BF16),
        jax.ShapeDtypeStruct((seq, model), BF16),
        jax.ShapeDtypeStruct((8, model), F32),
    ] + [jax.ShapeDtypeStruct(shape, BF16) for shape in weight_shapes]
    return pl.pallas_call(
        partial(layer_kernel, inputs + outputs + list(scratch), dims),
        out_shape=shapes,
        in_specs=[vmem] * 8 + [anywhere] * 7,
        out_specs=[vmem] * 3 + [anywhere] * 7,
        scratch_shapes=list(scratch.values()),
        compiler_params=pltpu.CompilerParams(
            collective_id=0, has_side_effects=True, vmem_limit_bytes=VMEM_LIMIT
        ),
        name="layer",
    )(*operands)


def body(
    mesh_sizes,
    tokens_in,
    input_gain,
    q_gain,
    k_gain,
    w_query,
    w_key,
    w_value,
    w_output,
    post_gain,
    w_gate,
    w_up,
    w_down,
    segment_ids,
    positions,
    out_cotangent,
):
    dims = sizes_of(mesh_sizes, tokens_in, w_query, w_key, w_output, w_gate, w_down, q_gain)
    seq, width = dims["seq"], dims["width"]
    ladder = jnp.arange(width // 2, dtype=F32)
    inverse = jnp.exp(ladder * (-2.0 * math.log(ROPE_BASE) / width))
    angles = positions.astype(F32)[:, None] * inverse[None, :]
    table = jnp.concatenate([jnp.cos(angles), jnp.sin(angles)], -1)
    steps = jnp.arange(seq)
    mask = (
        (segment_ids[:, None] == segment_ids[None, :]) & (steps[:, None] >= steps[None, :])
    ).astype(BF16)
    weights = (w_query, w_key, w_value, w_output, w_gate, w_up, w_down)
    done = run_layer(
        dims,
        (
            tokens_in,
            table,
            mask,
            out_cotangent,
            input_gain[None],
            post_gain[None],
            q_gain[None],
            k_gain[None],
            *weights,
        ),
        [weight.shape for weight in weights],
    )
    gains, grads = done[2], tuple(done[3:])
    reps, team = dims["reps"], dims["team"]
    if reps > team:
        rings = [list(range(first, reps, team)) for first in range(team)]
        gains = lax.psum(gains, "rep", axis_index_groups=rings)
        grads = lax.psum(grads, "rep", axis_index_groups=rings)
    return (
        done[0],
        done[1],
        gains[0],
        gains[2, :width],
        gains[3, :width],
        gains[1],
        *(grad.astype(F32) for grad in grads),
    )


def solution(mesh):
    tokens = P(("rep", "fsdp"), None)
    ids = P(("rep", "fsdp"))
    weight = P("fsdp", None)
    in_specs = (
        (tokens,)
        + (P(),) * 3
        + (weight,) * 4
        + (P(),)
        + (weight,) * 3
        + (ids, ids, tokens)
    )
    out_specs = (tokens, tokens) + (P(),) * 4 + (weight,) * 7
    return jax.shard_map(
        partial(body, (mesh.shape["rep"], mesh.shape["fsdp"])),
        mesh=mesh,
        in_specs=in_specs,
        out_specs=out_specs,
        check_vma=False,
    )
```

```python
from functools import partial
import math
from types import SimpleNamespace

import jax
import jax.numpy as jnp
from jax import lax
from jax.experimental import pallas as pl
from jax.experimental.pallas import tpu as pltpu
from jax.sharding import PartitionSpec as P

EPS = 1e-06
ROPE_BASE = 1000000.0
NEG_FILL = -1e30
F32 = jnp.float32
BF16 = jnp.bfloat16
VMEM_LIMIT = 60 * 1024 * 1024


def dot(first, second):
    return lax.dot_general(first, second, (((1,), (0,)), ((), ())), preferred_element_type=F32)


def dot_nt(first, second):
    return lax.dot_general(first, second, (((1,), (1,)), ((), ())), preferred_element_type=F32)


def dot_tn(first, second):
    return lax.dot_general(first, second, (((0,), (0,)), ((), ())), preferred_element_type=F32)


def rms_scale(values):
    return lax.rsqrt(jnp.mean(values * values, axis=-1, keepdims=True) + EPS)


def flip(index, bits):
    out = index
    step = 1
    while step <= bits:
        if bits & step:
            out = out + step * (1 - 2 * lax.rem(index // step, 2))
        step *= 2
    return out


def sizes_of(mesh_sizes, tokens, w_query, w_key, w_output, w_gate, w_down, q_gain):
    reps, fsdp = mesh_sizes
    width = q_gain.shape[0]
    heads_q = w_query.shape[1] // width
    heads_kv = w_key.shape[1] // width
    team = math.gcd(reps, heads_kv)
    assert team >= 2 and team & (team - 1) == 0 and team % fsdp == 0
    dims = SimpleNamespace(
        reps=reps,
        fsdp=fsdp,
        team=team,
        width=width,
        seq=tokens.shape[0],
        model=tokens.shape[1],
        kv=heads_kv // team,
        ratio=heads_q // heads_kv,
        qcols=w_query.shape[1] // team,
        kcols=w_key.shape[1] // team,
        ffcols=w_gate.shape[1] // team,
        band=w_query.shape[0],
        share=team // fsdp,
    )
    return dims


def layer_kernel(names, dims, *refs):
    r = SimpleNamespace(**dict(zip(names, refs)))
    team, fsdp = dims.team, dims.fsdp
    seq, model, width = dims.seq, dims.model, dims.width
    kv, ratio, band, share = dims.kv, dims.ratio, dims.band, dims.share
    qc, kc, fc = dims.qcols, dims.kcols, dims.ffcols
    chips = team // 2
    half = width // 2

    rep = lax.axis_index("rep")
    z = lax.axis_index("fsdp")
    me = lax.rem(rep, team)
    base = rep - me
    home = me // share

    def place(member, plane):
        return {"rep": base + member, "fsdp": plane}

    def remote(src, dst, send_sem, recv_sem, member, plane):
        return pltpu.make_async_remote_copy(
            src_ref=src,
            dst_ref=dst,
            send_sem=send_sem,
            recv_sem=recv_sem,
            device_id=place(member, plane),
            device_id_type=pl.DeviceIdType.MESH,
        )

    pending = []

    def launch(copy, cond=None):
        if cond is None:
            copy.start()
        else:
            pl.when(cond)(copy.start)
        pending.append((cond, copy))

    def guarded(cond, action):
        if cond is None:
            action()
        else:
            pl.when(cond)(action)

    queues = {}

    def paced(queue, limit, cond, copy, before=None):
        items = queues.setdefault(queue, [])
        if len(items) >= limit:
            earlier, first = items.pop(0)
            pl.when(earlier)(first.wait_send)

        def start():
            if before is not None:
                before()
            copy.start()

        pl.when(cond)(start)
        items.append((cond, copy))

    def rows(ref, index, count):
        return ref.at[pl.ds(pl.multiple_of(index * count, count), count)]

    def loop(count, step, first=0):
        def run(index, carry):
            step(index)
            return carry

        lax.fori_loop(first, count, run, 0)

    near = [2] if chips == 2 else [2, 4]
    far = [2 * chip for chip in range(1, chips) if 2 * chip not in near]
    core = lax.rem(me, 2)
    passes = chips == 4
    along = flip(me, 2) * (1 - core) + flip(me, 4) * core
    across = flip(me, 4) * (1 - core) + flip(me, 2) * core

    def gather_send(job, block, bits, member, cond):
        send_sem, recv_sem = r.ag_send.at[job, bits], r.ag_recv.at[job, bits]
        launch(remote(block, block, send_sem, recv_sem, member, z), cond)

    def gather_start(job, view, active=None):
        cond = None if active is None else active(me)
        for bits in near + [1] + ([] if passes else far):
            gather_send(job, view(me), bits, flip(me, bits), cond)

    def gather_wait(job, view, bits, active=None):
        block = view(flip(me, bits))
        cond = None if active is None else active(flip(me, bits))
        copy = remote(
            block, block, r.ag_send.at[job, bits], r.ag_recv.at[job, bits], flip(me, 1), z
        )
        guarded(cond, copy.wait_recv)

    def gather_beside(job, view, bits, active):
        block = view(flip(me, bits))
        cond = None if active is None else active(flip(me, bits))
        gather_send(job, block, bits + 1, flip(me, 1), cond)

    def gather_forward(job, view, active=None):
        for bits in near:
            gather_wait(job, view, bits, active)
        if passes:
            block = view(along)
            cond = None if active is None else active(along)
            gather_send(job, block, far[0], across, cond)
        for bits in near:
            gather_beside(job, view, bits, active)

    def gather_last(job, view, active=None):
        for bits in far:
            gather_wait(job, view, bits, active)
            gather_beside(job, view, bits, active)

    def gather_finish(job, view, active=None):
        for chip in range(chips):
            gather_wait(job, view, 2 * chip + 1, active)

    def ring_jobs(which):
        first = 0 if which == 0 else tall_chunks(0)
        for chunk in range(tall_chunks(which)):

            def view(member, chunk=chunk):
                return tall_view[which](member).at[pl.ds(chunk * width, width)]

            yield 10 + first + chunk, view

    def ring_start(which):
        for job, view in ring_jobs(which):
            if not passes:
                gather_start(job, view, home_of)
                continue
            bits = 2 + 2 * core
            block, cond = view(me), home_of(me)
            send, recv = r.ag_send.at[job, 0], r.ag_recv.at[job, bits]
            launch(remote(block, block, send, recv, along, z), cond)
            gather_send(job, block, 1, flip(me, 1), cond)

    def ring_pass(which, stage):
        for job, view in ring_jobs(which):
            if not passes:
                if stage == 1:
                    gather_forward(job, view, home_of)
                    gather_last(job, view, home_of)
                continue
            bits = (2 + 2 * core, 6, 4 - 2 * core)[stage - 1]
            owner = (along, flip(me, 6), across)[stage - 1]
            block, cond = view(owner), home_of(owner)
            recv = r.ag_recv.at[job, bits]
            copy = remote(block, block, r.ag_send.at[job, 0], recv, along, z)
            guarded(cond, copy.wait_recv)
            if stage < 3:
                target = across if stage == 1 else along
                after = r.ag_recv.at[job, 6 if stage == 1 else 4 - 2 * core]
                send = r.ag_send.at[job, 2 * stage]
                launch(remote(block, block, send, after, target, z), cond)
            send, after = r.ag_send.at[job, 1 + 2 * stage], r.ag_recv.at[job, bits + 1]
            launch(remote(block, block, send, after, flip(me, 1), z), cond)

    def ring_finish(which):
        for job, view in ring_jobs(which):
            gather_finish(job, view, home_of)

    def home_of(member):
        return member // share == z

    def scatter_start(job, part):
        for chip in reversed(range(chips)):
            bits = 2 * chip + 1
            r.rs_out[job, chip] = part(flip(me, bits)).astype(BF16)
            launch(
                remote(
                    r.rs_out.at[job, chip],
                    r.rs_in.at[job, chip],
                    r.rs_sem.at[job, 0, chip],
                    r.rs_sem.at[job, 1, chip],
                    flip(me, 1),
                    z,
                )
            )

        def arrived(chip):
            block = r.rs_in.at[job, chip]
            remote(
                block,
                block,
                r.rs_sem.at[job, 0, chip],
                r.rs_sem.at[job, 1, chip],
                flip(me, 1),
                z,
            ).wait_recv()

        for chip in list(reversed(range(1, chips))):
            mine = part(flip(me, 2 * chip))
            arrived(chip)
            r.rs_in[job, chip] = (mine + r.rs_in[job, chip].astype(F32)).astype(BF16)
            launch(
                remote(
                    r.rs_in.at[job, chip],
                    r.rs_last.at[job, chip - 1],
                    r.rs_sem.at[job, 2, chip],
                    r.rs_sem.at[job, 3, chip],
                    flip(me, 2 * chip),
                    z,
                )
            )
        mine = part(me)
        arrived(0)
        r.rs_sum[job] = mine + r.rs_in[job, 0].astype(F32)

    def scatter_finish(job):
        total = r.rs_sum[job]
        for chip in range(1, chips):
            block = r.rs_last.at[job, chip - 1]
            remote(
                block,
                block,
                r.rs_sem.at[job, 2, chip],
                r.rs_sem.at[job, 3, chip],
                flip(me, 2 * chip),
                z,
            ).wait_recv()
            total = total + r.rs_last[job, chip - 1].astype(F32)
        return total

    wide = (r.w_qkv, r.w_gu)
    tall = (r.w_o, r.w_d)
    tall_rows = (qc, fc)

    def wide_block(which, plane):
        return rows(wide[which], plane, band)

    def wide_pass(which, step):
        for way, exists, plane, more, target in (
            (0, z - step >= 0, z - step, z < fsdp - 1, z + 1),
            (1, z + step <= fsdp - 1, z + step, z > 0, z - 1),
        ):
            plane = jnp.clip(plane, 0, fsdp - 1)
            block = wide_block(which, plane)
            copy = remote(
                block,
                block,
                r.ww_send.at[which, way, step],
                r.ww_recv.at[which, plane],
                me,
                jnp.clip(target, 0, fsdp - 1),
            )
            if step > 0:
                pl.when(exists)(copy.wait_recv)
            if step < fsdp - 1:
                paced(("wide", way), 2, jnp.logical_and(exists, more), copy)

    def tall_chunks(which):
        return tall_rows[which] // width

    def tall_pass(which, chunk, stage):
        block = tall[which].at[pl.ds(chunk * width, width)]
        up = jnp.logical_and(z >= home, z < fsdp - 1)
        down = jnp.logical_and(z <= home, z > 0)
        begins = z == home
        ends = jnp.logical_and(z != home, jnp.logical_or(z == 0, z == fsdp - 1))
        between = jnp.logical_and(z != home, jnp.logical_and(z > 0, z < fsdp - 1))
        for way, cond, target in ((0, up, z + 1), (1, down, z - 1)):
            copy = remote(
                block,
                block,
                r.wt_send.at[which, way, chunk],
                r.wt_recv.at[which, chunk],
                me,
                jnp.clip(target, 0, fsdp - 1),
            )
            if stage == 2:
                if way == 0:
                    pl.when(ends)(copy.wait_recv)
                continue
            if stage == 1 and way == 0:
                pl.when(between)(copy.wait_recv)
            own = begins if stage == 0 else between
            paced(("tall", way, stage), 1, jnp.logical_and(cond, own), copy)

    wide_sum = (r.g_qkv, r.g_gu)
    tall_sum = (r.g_o, r.g_d)
    wide_flow = (r.f_qkv, r.f_gu)
    tall_flow = (r.f_o, r.f_d)
    wide_view = (lambda member: rows(r.oqkv, member, band), lambda member: rows(r.ogu, member, band))
    tall_view = (
        lambda member: rows(r.oo, lax.rem(member, share), qc),
        lambda member: rows(r.od, lax.rem(member, share), fc),
    )

    def merge(target, own, start, count, has_incoming):
        step = 32

        def one(index):
            at = pl.ds(pl.multiple_of(start + index * step, step), step)
            value = own[at]
            if has_incoming:
                value = value + target[at].astype(F32)
            target[at] = value.astype(BF16)

        loop(count // step, one)


    def wide_level(which, level, turn):
        for way, here in ((0, level), (1, fsdp - 1 - level)):
            flow = wide_flow[which].at[way]
            plane = fsdp - 1 - turn if way == 0 else turn
            block = flow.at[pl.ds(plane * band, band)]
            copy = remote(
                block,
                block,
                r.gw_send.at[which, way, plane],
                r.gw_recv.at[which, way, plane],
                me,
                here + 1 if way == 0 else here - 1,
            )

            def before(flow=flow, plane=plane, copy=copy):
                if level > 0:
                    copy.wait_recv()
                merge(flow, wide_sum[which], plane * band, band, level > 0)

            paced(("level", way, level), 4, z == here, copy, before)

    def wide_final(which):
        def take(way):
            flow = wide_flow[which].at[way]
            block = rows(flow, z, band)
            remote(
                block,
                block,
                r.gw_send.at[which, way, z],
                r.gw_recv.at[which, way, z],
                me,
                z,
            ).wait_recv()
            step = 32

            def one(index):
                at = pl.ds(pl.multiple_of(z * band + index * step, step), step)
                wide_sum[which][at] = wide_sum[which][at] + flow[at].astype(F32)

            loop(band // step, one)

        pl.when(z > 0)(lambda: take(0))
        pl.when(z < fsdp - 1)(lambda: take(1))
        wide_view[which](me)[...] = rows(wide_sum[which], z, band)[...].astype(BF16)

    def tall_level(which, level, chunk):
        for way, here in ((0, level), (1, fsdp - 1 - level)):
            flow = tall_flow[which].at[way]
            block = flow.at[pl.ds(chunk * width, width)]
            copy = remote(
                block,
                block,
                r.gt_send.at[which, way, chunk],
                r.gt_recv.at[which, way, chunk],
                me,
                here + 1 if way == 0 else here - 1,
            )

            def before(flow=flow, chunk=chunk, copy=copy):
                if level > 0:
                    copy.wait_recv()
                merge(flow, tall_sum[which], chunk * width, width, level > 0)

            toward = home > here if way == 0 else home < here
            paced(("level", way, level), 4, jnp.logical_and(z == here, toward), copy, before)

    flow_order = [("tall", 1, chunk) for chunk in range(tall_chunks(1))]
    flow_order += [("wide", 1, turn) for turn in range(fsdp - 1)]
    flow_order += [("tall", 0, chunk) for chunk in range(tall_chunks(0))]
    flow_order += [("wide", 0, turn) for turn in range(fsdp - 1)]
    reached = [0] * max(fsdp - 1, 1)

    def advance(level, count):
        for kind, which, piece in flow_order[reached[level] : reached[level] + count]:
            if kind == "tall":
                tall_level(which, level, piece)
            elif piece < fsdp - 1 - level:
                wide_level(which, level, piece)
        reached[level] += count

    def advance_to(level, kind, which):
        last = max(at for at, item in enumerate(flow_order) if item[:2] == (kind, which))
        if level < fsdp - 1 and last >= reached[level]:
            advance(level, last + 1 - reached[level])

    def tall_final(which):
        count = tall_rows[which]

        def take(way):
            flow = tall_flow[which].at[way]
            for chunk in range(tall_chunks(which)):
                block = flow.at[pl.ds(chunk * width, width)]
                remote(
                    block,
                    block,
                    r.gt_send.at[which, way, chunk],
                    r.gt_recv.at[which, way, chunk],
                    me,
                    z,
                ).wait_recv()
            step = 32

            def one(index):
                at = pl.ds(pl.multiple_of(index * step, step), step)
                tall_sum[which][at] = tall_sum[which][at] + flow[at].astype(F32)

            loop(count // step, one)

        pl.when(jnp.logical_and(z == home, z > 0))(lambda: take(0))
        pl.when(jnp.logical_and(z == home, z < fsdp - 1))(lambda: take(1))

        def close():
            tall_view[which](me)[...] = tall_sum[which][...].astype(BF16)

        pl.when(z == home)(close)

    loads = []
    wide_at = lambda which, start, size: wide_block(which, z).at[:, pl.ds(start, size)]

    def column(ref, member, size):
        return ref.at[:, pl.ds(pl.multiple_of(member * size, size), size)]

    for src, dst in (
        (column(r.wq, me, qc), wide_at(0, 0, qc)),
        (column(r.wk, me, kc), wide_at(0, qc, kc)),
        (column(r.wv, me, kc), wide_at(0, qc + kc, kc)),
        (column(r.wg, me, fc), wide_at(1, 0, fc)),
        (column(r.wu, me, fc), wide_at(1, fc, fc)),
    ):
        load = pltpu.make_async_copy(src, dst, r.load_sem.at[len(loads)])
        load.start()
        loads.append(load)
    slot = lax.rem(me, share)
    tall_loads = []
    for which, src in ((0, r.wo), (1, r.wd)):
        load = pltpu.make_async_copy(
            rows(src, slot, tall_rows[which]), tall[which], r.load_sem.at[5 + which]
        )
        pl.when(z == home)(load.start)
        tall_loads.append(load)

    barrier = pltpu.get_barrier_semaphore()
    partners = [2 * chip for chip in range(1, chips)] + [1]
    for bits in partners:
        pl.semaphore_signal(
            barrier,
            inc=1,
            device_id=place(flip(me, bits), z),
            device_id_type=pl.DeviceIdType.MESH,
        )
    for away in range(1, fsdp):
        pl.semaphore_signal(
            barrier,
            inc=1,
            device_id=place(me, lax.rem(z + away, fsdp)),
            device_id_type=pl.DeviceIdType.MESH,
        )

    tokens = r.tokens[...].astype(F32)
    in_scale = rms_scale(tokens)
    rows(r.xn, me, seq)[...] = (tokens * in_scale * r.in_gain[...]).astype(BF16)
    rows(r.tab, me, seq)[...] = r.table[...]
    rows(r.msk, me, seq)[...] = r.mask[...]
    rows(r.cot, me, seq)[...] = r.cotangent[...]
    r.gain_own[...] = jnp.zeros_like(r.gain_own)

    pl.semaphore_wait(barrier, len(partners) + fsdp - 1)

    view_xn = lambda member: rows(r.xn, member, seq)
    view_tab = lambda member: rows(r.tab, member, seq)
    view_msk = lambda member: rows(r.msk, member, seq)
    view_cot = lambda member: rows(r.cot, member, seq)
    view_pn = lambda member: rows(r.pn, member, seq)
    view_da = lambda member: rows(r.da, member, seq)

    def home_sends(which, chunk):
        if chunk < tall_chunks(which):
            tall_pass(which, chunk, 0)

    def tall_passes(which, chunk):
        if chunk < tall_chunks(which):
            tall_pass(which, chunk, 1)

    for load in loads[:3]:
        load.wait()
    wide_pass(0, 0)
    for job, view in ((0, view_xn), (1, view_tab), (2, view_msk)):
        gather_start(job, view)
    for load in loads[3:]:
        load.wait()
    for load in tall_loads:
        pl.when(z == home)(load.wait)
    gather_forward(0, view_xn)
    if fsdp > 2:
        wide_pass(0, 1)
    home_sends(0, 0)
    for job, view in ((1, view_tab), (2, view_msk)):
        gather_forward(job, view)
    gather_last(0, view_xn)
    for step in range(2, fsdp - 1):
        wide_pass(0, step)
    wide_pass(1, 0)
    for job, view in ((1, view_tab), (2, view_msk)):
        gather_last(job, view)
    for job, view in ((0, view_xn), (1, view_tab), (2, view_msk)):
        gather_finish(job, view)
    home_sends(0, 1)
    wide_pass(0, fsdp - 1)

    lane = lax.broadcasted_iota(jnp.int32, (seq, width), 1)
    front = lane < half
    sign = jnp.where(front, -1.0, 1.0).astype(F32)
    root = width ** (-0.5)

    def turn(values):
        return pltpu.roll(values, half, 1)

    def tables(at):
        table = r.tab[at]
        swapped = turn(table)
        return jnp.where(front, table, swapped), jnp.where(front, swapped, table)

    def at_seq(index):
        return pl.ds(pl.multiple_of(index * seq, seq), seq)

    def attend(index):
        at = at_seq(index)
        cosine, sine = tables(at)
        signed = sine * sign
        qkv = dot(r.xn[at], r.w_qkv[...])
        r.qk[at] = qkv[:, : qc + kc]
        allowed = r.msk[at].astype(F32) > 0.5
        allowed = jnp.concatenate([allowed] * ratio, 0) if ratio > 1 else allowed

        def spun(values, gain):
            values = values * rms_scale(values) * gain
            return (values * cosine + turn(values) * signed).astype(BF16)

        for group in range(kv):
            k_rot = spun(qkv[:, qc + group * width : qc + (group + 1) * width], r.kg[...])
            start = qc + kc + group * width
            values = qkv[:, start : start + width].astype(BF16)
            spins = []
            for head in range(ratio):
                place_at = (group * ratio + head) * width
                spin = spun(qkv[:, place_at : place_at + width], r.qg[...])
                r.rot[at, place_at : place_at + width] = spin
                spins.append(spin)
            r.rot[at, qc + group * width : qc + (group + 1) * width] = k_rot
            r.rot[at, start : start + width] = values
            q_rot = jnp.concatenate(spins, 0)
            scores = dot_nt(q_rot, k_rot) * root
            masked = jnp.where(allowed, scores, NEG_FILL)
            top = jnp.max(masked, axis=-1, keepdims=True)
            total = top + jnp.log(jnp.sum(jnp.exp(masked - top), axis=-1, keepdims=True))
            probs = jnp.where(allowed, jnp.exp(masked - total), 0.0)
            r.probs[index, group] = probs
            mixed = dot(probs.astype(BF16), values).astype(BF16)
            for head in range(ratio):
                place_at = (group * ratio + head) * width
                r.att[at, place_at : place_at + width] = mixed[head * seq : (head + 1) * seq]

    gather_start(3, view_cot)
    loop(team // 2, attend)
    tall_passes(0, 0)
    if fsdp > 2:
        wide_pass(1, 1)
    loop(team, attend, team // 2)
    for chunk in range(1, tall_chunks(0)):
        tall_passes(0, chunk)
    for chunk in range(2, tall_chunks(0)):
        home_sends(0, chunk)
    home_sends(1, 0)

    for chunk in range(tall_chunks(0)):
        tall_pass(0, chunk, 2)
    scatter_start(0, lambda member: dot(rows(r.att, member, seq)[...], r.w_o[...]))
    for step in range(2, fsdp - 1):
        wide_pass(1, step)
    home_sends(1, 1)
    gather_forward(3, view_cot)
    tall_passes(1, 0)
    middle = tokens + scatter_finish(0)
    r.middle[...] = middle
    post_scale = rms_scale(middle)
    view_pn(me)[...] = (middle * post_scale * r.post_gain[...]).astype(BF16)
    gather_start(4, view_pn)
    for chunk in range(2, tall_chunks(1)):
        home_sends(1, chunk)
    gather_last(3, view_cot)
    tall_passes(1, 1)
    gather_forward(4, view_pn)
    for chunk in range(2, tall_chunks(1)):
        tall_passes(1, chunk)
    gather_last(4, view_pn)
    wide_pass(1, fsdp - 1)
    gather_finish(3, view_cot)
    gather_finish(4, view_pn)
    for chunk in range(tall_chunks(1)):
        tall_pass(1, chunk, 2)

    def feed(index):
        at = at_seq(index)
        both = dot(r.pn[at], r.w_gu[...])
        gate, up = both[:, :fc], both[:, fc:]
        sigm = jax.nn.sigmoid(gate)
        soft = gate * sigm
        r.hid[at] = (soft * up).astype(BF16)
        d_hidden = dot_nt(r.cot[at], r.w_d[...])
        r.dgu[at, :fc] = (d_hidden * up * sigm * (1.0 + gate * (1.0 - sigm))).astype(BF16)
        r.dgu[at, fc:] = (d_hidden * soft).astype(BF16)

    loop(team, feed)

    r.g_d[...] = dot_tn(r.hid[...], r.cot[...])
    advance(0, tall_chunks(1))
    scatter_start(1, lambda member: dot_nt(rows(r.dgu, member, seq)[...], r.w_gu[...]))

    def grad_gu(index):
        at = pl.ds(pl.multiple_of(index * band, band), band)
        r.g_gu[at] = dot_tn(r.pn[:, at], r.dgu[...])

    def grad_qkv(index):
        at = pl.ds(pl.multiple_of(index * band, band), band)
        r.g_qkv[at] = dot_tn(r.xn[:, at], r.dqkv[...])

    loop(fsdp, grad_gu)
    advance(0, 1)
    middle_levels = range(1, fsdp - 1)

    def norm_back(grads, values, scale, gain):
        normal = values * scale
        gain_term = jnp.sum(grads * normal, axis=0, keepdims=True)
        scaled = grads * gain
        back = scale * (scaled - normal * jnp.mean(scaled * normal, axis=-1, keepdims=True))
        return back, gain_term

    d_post = scatter_finish(1)
    middle = r.middle[...]
    back, term = norm_back(d_post, middle, rms_scale(middle), r.post_gain[...])
    r.gain_own[1:2] = term
    d_middle = r.cotangent[...].astype(F32) + back
    r.d_middle[...] = d_middle
    view_da(me)[...] = d_middle.astype(BF16)
    gather_start(5, view_da)
    for level in middle_levels[:1]:
        advance_to(level, "tall", 1)
    advance(0, 1)
    gather_forward(5, view_da)
    for level in middle_levels[1:]:
        advance_to(level, "tall", 1)
    advance_to(0, "wide", 1)
    gather_last(5, view_da)
    gather_finish(5, view_da)
    r.g_o[...] = dot_tn(r.att[...], r.da[...])
    advance_to(0, "tall", 0)
    for level in middle_levels[:1]:
        advance_to(level, "wide", 1)

    def attend_back(index):
        at = at_seq(index)
        cosine, sine = tables(at)
        d_att = dot_nt(r.da[at], r.w_o[...]).astype(BF16)

        def unspun(grads):
            return grads * cosine - turn(grads * sine) * sign

        for group in range(kv):
            k_at = slice(qc + group * width, qc + (group + 1) * width)
            v_at = slice(qc + kc + group * width, qc + kc + (group + 1) * width)
            heads = [
                slice((group * ratio + head) * width, (group * ratio + head + 1) * width)
                for head in range(ratio)
            ]
            d_mixed = jnp.concatenate([d_att[:, head] for head in heads], 0)
            q_rot = jnp.concatenate([r.rot[at, head] for head in heads], 0)
            k_rot = r.rot[at, k_at]
            values = r.rot[at, v_at]
            probs = r.probs[index, group]
            d_probs = dot_nt(d_mixed, values)
            centre = jnp.sum(probs * d_probs, axis=-1, keepdims=True)
            d_scores = (probs * (d_probs - centre) * root).astype(BF16)
            d_query = dot(d_scores, k_rot)
            d_key = dot_tn(d_scores, q_rot)
            d_value = dot_tn(probs.astype(BF16), d_mixed)
            for number, head in enumerate(heads):
                queries = r.qk[at, head]
                back, term = norm_back(
                    unspun(d_query[number * seq : (number + 1) * seq]),
                    queries,
                    rms_scale(queries),
                    r.qg[...],
                )
                r.dqkv[at, head] = back.astype(BF16)
                r.gain_own[2:3, :width] += term
            keys = r.qk[at, k_at]
            back, term = norm_back(unspun(d_key), keys, rms_scale(keys), r.kg[...])
            r.dqkv[at, k_at] = back.astype(BF16)
            r.gain_own[3:4, :width] += term
            r.dqkv[at, v_at] = d_value.astype(BF16)

    view_gain = lambda member: r.gain_all.at[member]
    view_qkv, view_gu = wide_view
    loop(team // 2, attend_back)
    tall_final(1)
    ring_start(1)
    loop(team, attend_back, team // 2)
    scatter_start(3, lambda member: dot_nt(rows(r.dqkv, member, seq)[...], r.w_qkv[...]))
    loop(fsdp, grad_qkv)
    advance_to(0, "wide", 0)
    ring_pass(1, 1)
    for level in middle_levels[1:]:
        advance_to(level, "wide", 1)
    d_normed = scatter_finish(3)
    tokens = r.tokens[...].astype(F32)
    back, term = norm_back(d_normed, tokens, rms_scale(tokens), r.in_gain[...])
    r.gain_own[0:1] = term
    r.out_grad[...] = (r.d_middle[...] + back).astype(BF16)
    view_gain(me)[...] = r.gain_own[...]
    gather_start(6, view_gain)
    ring_pass(1, 2)
    wide_final(1)
    gather_start(8, view_gu)
    for level in middle_levels[:1]:
        advance_to(level, "tall", 0)
    scatter_start(2, lambda member: dot(rows(r.hid, member, seq)[...], r.w_d[...]))
    ring_pass(1, 3)
    gather_forward(6, view_gain)
    gather_last(6, view_gain)
    for level in middle_levels[1:]:
        advance_to(level, "tall", 0)
    gather_forward(8, view_gu)
    tall_final(0)
    ring_start(0)
    for level in middle_levels[:1]:
        advance_to(level, "wide", 0)
    gather_last(8, view_gu)
    for level in middle_levels[1:]:
        advance_to(level, "wide", 0)
    ring_pass(0, 1)
    r.out_block[...] = (r.middle[...] + scatter_finish(2)).astype(BF16)
    gather_finish(6, view_gain)
    total = r.gain_all[0]
    for member in range(1, team):
        total = total + r.gain_all[member]
    r.gain_line[z] = total
    for away in range(1, fsdp):
        launch(
            remote(
                r.gain_line.at[z],
                r.gain_line.at[z],
                r.gl_sem.at[0, away],
                r.gl_sem.at[1, away],
                me,
                lax.rem(z + away, fsdp),
            )
        )
    ring_pass(0, 2)
    wide_final(0)
    gather_start(9, view_qkv)
    for away in range(1, fsdp):
        block = r.gain_line.at[lax.rem(z + fsdp - away, fsdp)]
        remote(block, block, r.gl_sem.at[0, away], r.gl_sem.at[1, away], me, z).wait_recv()
    total = r.gain_line[0]
    for plane in range(1, fsdp):
        total = total + r.gain_line[plane]
    r.out_gain[...] = total
    ring_pass(0, 3)
    gather_forward(9, view_qkv)
    gather_last(9, view_qkv)
    gather_finish(8, view_gu)
    gather_finish(9, view_qkv)
    ring_finish(1)
    ring_finish(0)
    for items in queues.values():
        pending.extend(items)
    for cond, copy in pending:
        guarded(cond, copy.wait_send)


def run_layer(dims, operands):
    team, fsdp, seq, model = dims.team, dims.fsdp, dims.seq, dims.model
    width, kv, ratio, band = dims.width, dims.kv, dims.ratio, dims.band
    qc, kc, fc = dims.qcols, dims.kcols, dims.ffcols
    chips = team // 2
    qkv, gu, many = qc + 2 * kc, 2 * fc, team * seq
    chunks = max(qc, fc) // width
    jobs = 10 + (qc + fc) // width
    inputs = [
        "tokens",
        "table",
        "mask",
        "cotangent",
        "in_gain",
        "post_gain",
        "qg",
        "kg",
        "wq",
        "wk",
        "wv",
        "wo",
        "wg",
        "wu",
        "wd",
    ]
    outputs = [
        "out_block",
        "out_grad",
        "out_gain",
        "oqkv",
        "ogu",
        "oo",
        "od",
    ]
    dma = pltpu.SemaphoreType.DMA
    scratch = dict(
        xn=pltpu.VMEM((many, model), BF16),
        tab=pltpu.VMEM((many, width), F32),
        msk=pltpu.VMEM((many, seq), BF16),
        cot=pltpu.VMEM((many, model), BF16),
        pn=pltpu.VMEM((many, model), BF16),
        da=pltpu.VMEM((many, model), BF16),
        w_qkv=pltpu.VMEM((model, qkv), BF16),
        w_gu=pltpu.VMEM((model, gu), BF16),
        w_o=pltpu.VMEM((qc, model), BF16),
        w_d=pltpu.VMEM((fc, model), BF16),
        qk=pltpu.VMEM((many, qc + kc), F32),
        rot=pltpu.VMEM((many, qkv), BF16),
        probs=pltpu.VMEM((team, kv, ratio * seq, seq), F32),
        att=pltpu.VMEM((many, qc), BF16),
        hid=pltpu.VMEM((many, fc), BF16),
        dgu=pltpu.VMEM((many, gu), BF16),
        dqkv=pltpu.VMEM((many, qkv), BF16),
        middle=pltpu.VMEM((seq, model), F32),
        d_middle=pltpu.VMEM((seq, model), F32),
        rs_out=pltpu.VMEM((4, chips, seq, model), BF16),
        rs_in=pltpu.VMEM((4, chips, seq, model), BF16),
        rs_last=pltpu.VMEM((4, max(chips - 1, 1), seq, model), BF16),
        rs_sum=pltpu.VMEM((4, seq, model), F32),
        g_qkv=pltpu.VMEM((model, qkv), F32),
        g_gu=pltpu.VMEM((model, gu), F32),
        g_o=pltpu.VMEM((qc, model), F32),
        g_d=pltpu.VMEM((fc, model), F32),
        f_qkv=pltpu.VMEM((2, model, qkv), BF16),
        f_gu=pltpu.VMEM((2, model, gu), BF16),
        f_o=pltpu.VMEM((2, qc, model), BF16),
        f_d=pltpu.VMEM((2, fc, model), BF16),

        gain_own=pltpu.VMEM((8, model), F32),
        gain_all=pltpu.VMEM((team, 8, model), F32),
        gain_line=pltpu.VMEM((fsdp, 8, model), F32),
        ag_send=dma((jobs, team)),
        ag_recv=dma((jobs, team)),
        rs_sem=dma((4, 4, chips)),
        ww_send=dma((2, 2, fsdp)),
        ww_recv=dma((2, fsdp)),
        wt_send=dma((2, 2, chunks)),
        wt_recv=dma((2, chunks)),
        gw_send=dma((2, 2, fsdp)),
        gw_recv=dma((2, 2, fsdp)),
        gt_send=dma((2, 2, chunks)),
        gt_recv=dma((2, 2, chunks)),
        gl_sem=dma((2, fsdp)),
        load_sem=dma((7,)),
    )
    vmem = pl.BlockSpec(memory_space=pltpu.VMEM)
    anywhere = pl.BlockSpec(memory_space=pl.ANY)
    shapes = [
        jax.ShapeDtypeStruct((seq, model), BF16),
        jax.ShapeDtypeStruct((seq, model), BF16),
        jax.ShapeDtypeStruct((8, model), F32),
    ] + [
        jax.ShapeDtypeStruct(shape, BF16)
        for shape in (
            (team * band, qkv),
            (team * band, gu),
            (dims.share * qc, model),
            (dims.share * fc, model),
        )
    ]
    return pl.pallas_call(
        partial(layer_kernel, inputs + outputs + list(scratch), dims),
        out_shape=shapes,
        in_specs=[vmem] * 8 + [anywhere] * 7,
        out_specs=[vmem] * 7,
        scratch_shapes=list(scratch.values()),
        compiler_params=pltpu.CompilerParams(
            collective_id=0, has_side_effects=True, vmem_limit_bytes=VMEM_LIMIT
        ),
        name="layer",
    )(*operands)


def body(
    mesh_sizes,
    tokens_in,
    input_gain,
    q_gain,
    k_gain,
    w_query,
    w_key,
    w_value,
    w_output,
    post_gain,
    w_gate,
    w_up,
    w_down,
    segment_ids,
    positions,
    out_cotangent,
):
    dims = sizes_of(mesh_sizes, tokens_in, w_query, w_key, w_output, w_gate, w_down, q_gain)
    seq, width = dims.seq, dims.width
    ladder = jnp.arange(width // 2, dtype=F32)
    inverse = jnp.exp(ladder * (-2.0 * math.log(ROPE_BASE) / width))
    angles = positions.astype(F32)[:, None] * inverse[None, :]
    table = jnp.concatenate([jnp.cos(angles), jnp.sin(angles)], -1)
    steps = jnp.arange(seq)
    mask = (
        (segment_ids[:, None] == segment_ids[None, :]) & (steps[:, None] >= steps[None, :])
    ).astype(BF16)
    weights = (w_query, w_key, w_value, w_output, w_gate, w_up, w_down)
    done = run_layer(
        dims,
        (
            tokens_in,
            table,
            mask,
            out_cotangent,
            input_gain[None],
            post_gain[None],
            q_gain[None],
            k_gain[None],
            *weights,
        ),
    )
    gains, grads = done[2], tuple(done[3:])
    reps, team = dims.reps, dims.team
    if reps > team:
        rings = [list(range(first, reps, team)) for first in range(team)]
        gains = lax.psum(gains, "rep", axis_index_groups=rings)
        grads = lax.psum(grads, "rep", axis_index_groups=rings)
    return widen(dims, done[0], done[1], gains, grads)


def widen_kernel(dims, *refs):
    width, qc, kc, fc = dims.width, dims.qcols, dims.kcols, dims.ffcols
    block, grad, gains, qkv, gu, tall_o, tall_d = refs[:7]
    outs = refs[7:]
    outs[0][...] = block[...]
    outs[1][...] = grad[...]
    outs[2][...] = gains[0]
    outs[3][...] = gains[2, :width]
    outs[4][...] = gains[3, :width]
    outs[5][...] = gains[1]
    outs[6][...] = qkv[:, :qc].astype(F32)
    outs[7][...] = qkv[:, qc : qc + kc].astype(F32)
    outs[8][...] = qkv[:, qc + kc :].astype(F32)
    outs[9][...] = tall_o[...].astype(F32)
    outs[10][...] = gu[:, :fc].astype(F32)
    outs[11][...] = gu[:, fc:].astype(F32)
    outs[12][...] = tall_d[...].astype(F32)


def widen(dims, block_out, input_grad, gains, grads):
    steps, model, width, band = dims.team, dims.model, dims.width, dims.band
    qc, kc, fc = dims.qcols, dims.kcols, dims.ffcols

    def by_rows(count):
        return pl.BlockSpec((count // steps, model), lambda step: (step, 0))

    def stacked(size):
        return pl.BlockSpec((band, size), lambda step: (step, 0))

    def by_columns(size):
        return pl.BlockSpec((band, size), lambda step: (0, step))

    def flat(size):
        return pl.BlockSpec((size,), lambda step: (0,))

    count_o, count_d = grads[2].shape[0], grads[3].shape[0]
    return pl.pallas_call(
        partial(widen_kernel, dims),
        grid=(steps,),
        in_specs=[
            by_rows(dims.seq),
            by_rows(dims.seq),
            pl.BlockSpec(gains.shape, lambda step: (0, 0)),
            stacked(qc + 2 * kc),
            stacked(2 * fc),
            by_rows(count_o),
            by_rows(count_d),
        ],
        out_specs=[
            by_rows(dims.seq),
            by_rows(dims.seq),
            flat(model),
            flat(width),
            flat(width),
            flat(model),
            by_columns(qc),
            by_columns(kc),
            by_columns(kc),
            by_rows(count_o),
            by_columns(fc),
            by_columns(fc),
            by_rows(count_d),
        ],
        out_shape=[
            jax.ShapeDtypeStruct((dims.seq, model), BF16),
            jax.ShapeDtypeStruct((dims.seq, model), BF16),
            jax.ShapeDtypeStruct((model,), F32),
            jax.ShapeDtypeStruct((width,), F32),
            jax.ShapeDtypeStruct((width,), F32),
            jax.ShapeDtypeStruct((model,), F32),
            jax.ShapeDtypeStruct((band, steps * qc), F32),
            jax.ShapeDtypeStruct((band, steps * kc), F32),
            jax.ShapeDtypeStruct((band, steps * kc), F32),
            jax.ShapeDtypeStruct((count_o, model), F32),
            jax.ShapeDtypeStruct((band, steps * fc), F32),
            jax.ShapeDtypeStruct((band, steps * fc), F32),
            jax.ShapeDtypeStruct((count_d, model), F32),
        ],
        compiler_params=pltpu.CompilerParams(vmem_limit_bytes=VMEM_LIMIT),
        name="widen",
    )(block_out, input_grad, gains, *grads)


def solution(mesh):
    tokens = P(("rep", "fsdp"), None)
    ids = P(("rep", "fsdp"))
    weight = P("fsdp", None)
    in_specs = (
        (tokens,)
        + (P(),) * 3
        + (weight,) * 4
        + (P(),)
        + (weight,) * 3
        + (ids, ids, tokens)
    )
    out_specs = (tokens, tokens) + (P(),) * 4 + (weight,) * 7
    return jax.shard_map(
        partial(body, (mesh.shape["rep"], mesh.shape["fsdp"])),
        mesh=mesh,
        in_specs=in_specs,
        out_specs=out_specs,
        check_vma=False,
    )
```

```python
from functools import partial
import math
from types import SimpleNamespace

import jax
import jax.numpy as jnp
from jax import lax
from jax.experimental import pallas as pl
from jax.experimental.pallas import tpu as pltpu
from jax.sharding import PartitionSpec as P

EPS = 1e-06
ROPE_BASE = 1000000.0
NEG_FILL = -1e30
F32 = jnp.float32
BF16 = jnp.bfloat16
VMEM_LIMIT = 63 * 1024 * 1024


def dot(first, second):
    return lax.dot_general(first, second, (((1,), (0,)), ((), ())), preferred_element_type=F32)


def dot_nt(first, second):
    return lax.dot_general(first, second, (((1,), (1,)), ((), ())), preferred_element_type=F32)


def dot_tn(first, second):
    return lax.dot_general(first, second, (((0,), (0,)), ((), ())), preferred_element_type=F32)


def rms_scale(values):
    return lax.rsqrt(jnp.mean(values * values, axis=-1, keepdims=True) + EPS)


def flip(index, bits):
    out = index
    step = 1
    while step <= bits:
        if bits & step:
            out = out + step * (1 - 2 * lax.rem(index // step, 2))
        step *= 2
    return out


def sizes_of(mesh_sizes, tokens, w_query, w_key, w_output, w_gate, w_down, q_gain):
    reps, fsdp = mesh_sizes
    width = q_gain.shape[0]
    heads_q = w_query.shape[1] // width
    heads_kv = w_key.shape[1] // width
    team = math.gcd(reps, heads_kv)
    assert team >= 2 and team & (team - 1) == 0 and team % fsdp == 0
    dims = SimpleNamespace(
        reps=reps,
        fsdp=fsdp,
        team=team,
        width=width,
        seq=tokens.shape[0],
        model=tokens.shape[1],
        kv=heads_kv // team,
        ratio=heads_q // heads_kv,
        qcols=w_query.shape[1] // team,
        kcols=w_key.shape[1] // team,
        ffcols=w_gate.shape[1] // team,
        band=w_query.shape[0],
        share=team // fsdp,
    )
    return dims


def layer_kernel(names, dims, *refs):
    r = SimpleNamespace(**dict(zip(names, refs)))
    team, fsdp = dims.team, dims.fsdp
    seq, model, width = dims.seq, dims.model, dims.width
    kv, ratio, band, share = dims.kv, dims.ratio, dims.band, dims.share
    qc, kc, fc = dims.qcols, dims.kcols, dims.ffcols
    chips = team // 2
    half = width // 2

    rep = lax.axis_index("rep")
    z = lax.axis_index("fsdp")
    me = lax.rem(rep, team)
    base = rep - me
    home = me // share

    def place(member, plane):
        return {"rep": base + member, "fsdp": plane}

    def remote(src, dst, send_sem, recv_sem, member, plane):
        return pltpu.make_async_remote_copy(
            src_ref=src,
            dst_ref=dst,
            send_sem=send_sem,
            recv_sem=recv_sem,
            device_id=place(member, plane),
            device_id_type=pl.DeviceIdType.MESH,
        )

    pending = []

    def launch(copy, cond=None):
        if cond is None:
            copy.start()
        else:
            pl.when(cond)(copy.start)
        pending.append((cond, copy))

    def guarded(cond, action):
        if cond is None:
            action()
        else:
            pl.when(cond)(action)

    queues = {}

    def paced(queue, limit, cond, copy, before=None):
        items = queues.setdefault(queue, [])
        if len(items) >= limit:
            earlier, first = items.pop(0)
            pl.when(earlier)(first.wait_send)

        def start():
            if before is not None:
                before()
            copy.start()

        pl.when(cond)(start)
        items.append((cond, copy))

    def rows(ref, index, count):
        return ref.at[pl.ds(pl.multiple_of(index * count, count), count)]

    def loop(count, step, first=0):
        def run(index, carry):
            step(index)
            return carry

        lax.fori_loop(first, count, run, 0, unroll=2)

    near = [2] if chips == 2 else [2, 4]
    far = [2 * chip for chip in range(1, chips) if 2 * chip not in near]
    core = lax.rem(me, 2)
    passes = chips == 4
    along = flip(me, 2) * (1 - core) + flip(me, 4) * core
    across = flip(me, 4) * (1 - core) + flip(me, 2) * core

    def gather_send(job, block, bits, member, cond):
        send_sem, recv_sem = r.ag_send.at[job, bits], r.ag_recv.at[job, bits]
        launch(remote(block, block, send_sem, recv_sem, member, z), cond)

    def gather_start(job, view, active=None):
        cond = None if active is None else active(me)
        for bits in near + [1] + ([] if passes else far):
            gather_send(job, view(me), bits, flip(me, bits), cond)

    def gather_wait(job, view, bits, active=None):
        block = view(flip(me, bits))
        cond = None if active is None else active(flip(me, bits))
        copy = remote(
            block, block, r.ag_send.at[job, bits], r.ag_recv.at[job, bits], flip(me, 1), z
        )
        guarded(cond, copy.wait_recv)

    def gather_beside(job, view, bits, active):
        block = view(flip(me, bits))
        cond = None if active is None else active(flip(me, bits))
        gather_send(job, block, bits + 1, flip(me, 1), cond)

    def gather_forward(job, view, active=None):
        for bits in near:
            gather_wait(job, view, bits, active)
        if passes:
            block = view(along)
            cond = None if active is None else active(along)
            gather_send(job, block, far[0], across, cond)
        for bits in near:
            gather_beside(job, view, bits, active)

    def gather_last(job, view, active=None):
        for bits in far:
            gather_wait(job, view, bits, active)
            gather_beside(job, view, bits, active)

    def gather_finish(job, view, active=None):
        for chip in range(chips):
            gather_wait(job, view, 2 * chip + 1, active)

    def ring_jobs(which):
        first = 0 if which == 0 else tall_chunks(0)
        for chunk in range(tall_chunks(which)):

            def view(member, chunk=chunk):
                return tall_view[which](member).at[pl.ds(chunk * width, width)]

            yield 10 + first + chunk, view

    def ring_start(which):
        for job, view in ring_jobs(which):
            if not passes:
                gather_start(job, view, home_of)
                continue
            bits = 2 + 2 * core
            block, cond = view(me), home_of(me)
            send, recv = r.ag_send.at[job, 0], r.ag_recv.at[job, bits]
            launch(remote(block, block, send, recv, along, z), cond)
            gather_send(job, block, 1, flip(me, 1), cond)

    def ring_pass(which, stage):
        for job, view in ring_jobs(which):
            if not passes:
                if stage == 1:
                    gather_forward(job, view, home_of)
                    gather_last(job, view, home_of)
                continue
            bits = (2 + 2 * core, 6, 4 - 2 * core)[stage - 1]
            owner = (along, flip(me, 6), across)[stage - 1]
            block, cond = view(owner), home_of(owner)
            recv = r.ag_recv.at[job, bits]
            copy = remote(block, block, r.ag_send.at[job, 0], recv, along, z)
            guarded(cond, copy.wait_recv)
            if stage < 3:
                target = across if stage == 1 else along
                after = r.ag_recv.at[job, 6 if stage == 1 else 4 - 2 * core]
                send = r.ag_send.at[job, 2 * stage]
                launch(remote(block, block, send, after, target, z), cond)
            send, after = r.ag_send.at[job, 1 + 2 * stage], r.ag_recv.at[job, bits + 1]
            launch(remote(block, block, send, after, flip(me, 1), z), cond)

    def ring_finish(which):
        for job, view in ring_jobs(which):
            gather_finish(job, view, home_of)

    def home_of(member):
        return member // share == z

    def scatter_start(job, part):
        for chip in reversed(range(chips)):
            bits = 2 * chip + 1
            r.rs_out[job, chip] = part(flip(me, bits)).astype(BF16)
            launch(
                remote(
                    r.rs_out.at[job, chip],
                    r.rs_in.at[job, chip],
                    r.rs_sem.at[job, 0, chip],
                    r.rs_sem.at[job, 1, chip],
                    flip(me, 1),
                    z,
                )
            )

        def arrived(chip):
            block = r.rs_in.at[job, chip]
            remote(
                block,
                block,
                r.rs_sem.at[job, 0, chip],
                r.rs_sem.at[job, 1, chip],
                flip(me, 1),
                z,
            ).wait_recv()

        for chip in list(reversed(range(1, chips))):
            mine = part(flip(me, 2 * chip))
            arrived(chip)
            r.rs_in[job, chip] = (mine + r.rs_in[job, chip].astype(F32)).astype(BF16)
            launch(
                remote(
                    r.rs_in.at[job, chip],
                    r.rs_last.at[job, chip - 1],
                    r.rs_sem.at[job, 2, chip],
                    r.rs_sem.at[job, 3, chip],
                    flip(me, 2 * chip),
                    z,
                )
            )
        mine = part(me)
        arrived(0)
        r.rs_sum[job] = mine + r.rs_in[job, 0].astype(F32)

    def scatter_finish(job):
        total = r.rs_sum[job]
        for chip in range(1, chips):
            block = r.rs_last.at[job, chip - 1]
            remote(
                block,
                block,
                r.rs_sem.at[job, 2, chip],
                r.rs_sem.at[job, 3, chip],
                flip(me, 2 * chip),
                z,
            ).wait_recv()
            total = total + r.rs_last[job, chip - 1].astype(F32)
        return total

    wide = (r.w_qkv, r.w_gu)
    tall = (r.w_o, r.w_d)
    tall_rows = (qc, fc)

    def wide_block(which, plane):
        return rows(wide[which], plane, band)

    def wide_pass(which, step):
        for way, exists, plane, more, target in (
            (0, z - step >= 0, z - step, z < fsdp - 1, z + 1),
            (1, z + step <= fsdp - 1, z + step, z > 0, z - 1),
        ):
            plane = jnp.clip(plane, 0, fsdp - 1)
            block = wide_block(which, plane)
            copy = remote(
                block,
                block,
                r.ww_send.at[which, way, step],
                r.ww_recv.at[which, plane],
                me,
                jnp.clip(target, 0, fsdp - 1),
            )
            if step > 0:
                pl.when(exists)(copy.wait_recv)
            if step < fsdp - 1:
                paced(("wide", way), 2, jnp.logical_and(exists, more), copy)

    def tall_chunks(which):
        return tall_rows[which] // width

    def tall_pass(which, chunk, stage):
        block = tall[which].at[pl.ds(chunk * width, width)]
        up = jnp.logical_and(z >= home, z < fsdp - 1)
        down = jnp.logical_and(z <= home, z > 0)
        begins = z == home
        ends = jnp.logical_and(z != home, jnp.logical_or(z == 0, z == fsdp - 1))
        between = jnp.logical_and(z != home, jnp.logical_and(z > 0, z < fsdp - 1))
        for way, cond, target in ((0, up, z + 1), (1, down, z - 1)):
            copy = remote(
                block,
                block,
                r.wt_send.at[which, way, chunk],
                r.wt_recv.at[which, chunk],
                me,
                jnp.clip(target, 0, fsdp - 1),
            )
            if stage == 2:
                if way == 0:
                    pl.when(ends)(copy.wait_recv)
                continue
            if stage == 1 and way == 0:
                pl.when(between)(copy.wait_recv)
            own = begins if stage == 0 else between
            paced(("tall", way, stage), 1, jnp.logical_and(cond, own), copy)

    wide_sum = (r.g_qkv, r.g_gu)
    tall_sum = (r.g_o, r.g_d)
    wide_flow = (r.f_qkv, r.f_gu)
    tall_flow = (r.f_o, r.f_d)
    wide_view = (lambda member: rows(r.oqkv, member, band), lambda member: rows(r.ogu, member, band))
    tall_view = (
        lambda member: rows(r.oo, lax.rem(member, share), qc),
        lambda member: rows(r.od, lax.rem(member, share), fc),
    )

    def merge(target, own, start, count, has_incoming):
        step = 32

        def one(index):
            at = pl.ds(pl.multiple_of(start + index * step, step), step)
            value = own[at]
            if has_incoming:
                value = value + target[at].astype(F32)
            target[at] = value.astype(BF16)

        loop(count // step, one)


    def wide_level(which, level, turn):
        for way, here in ((0, level), (1, fsdp - 1 - level)):
            flow = wide_flow[which].at[way]
            plane = fsdp - 1 - turn if way == 0 else turn
            block = flow.at[pl.ds(plane * band, band)]
            copy = remote(
                block,
                block,
                r.gw_send.at[which, way, plane],
                r.gw_recv.at[which, way, plane],
                me,
                here + 1 if way == 0 else here - 1,
            )

            def before(flow=flow, plane=plane, copy=copy):
                if level > 0:
                    copy.wait_recv()
                merge(flow, wide_sum[which], plane * band, band, level > 0)

            paced(("level", way, level), 4, z == here, copy, before)

    def wide_final(which):
        def take(way):
            flow = wide_flow[which].at[way]
            block = rows(flow, z, band)
            remote(
                block,
                block,
                r.gw_send.at[which, way, z],
                r.gw_recv.at[which, way, z],
                me,
                z,
            ).wait_recv()
            step = 32

            def one(index):
                at = pl.ds(pl.multiple_of(z * band + index * step, step), step)
                wide_sum[which][at] = wide_sum[which][at] + flow[at].astype(F32)

            loop(band // step, one)

        pl.when(z > 0)(lambda: take(0))
        pl.when(z < fsdp - 1)(lambda: take(1))
        wide_view[which](me)[...] = rows(wide_sum[which], z, band)[...].astype(BF16)

    def tall_level(which, level, chunk):
        for way, here in ((0, level), (1, fsdp - 1 - level)):
            flow = tall_flow[which].at[way]
            block = flow.at[pl.ds(chunk * width, width)]
            copy = remote(
                block,
                block,
                r.gt_send.at[which, way, chunk],
                r.gt_recv.at[which, way, chunk],
                me,
                here + 1 if way == 0 else here - 1,
            )

            def before(flow=flow, chunk=chunk, copy=copy):
                if level > 0:
                    copy.wait_recv()
                merge(flow, tall_sum[which], chunk * width, width, level > 0)

            toward = home > here if way == 0 else home < here
            paced(("level", way, level), 4, jnp.logical_and(z == here, toward), copy, before)

    flow_order = [("tall", 1, chunk) for chunk in range(tall_chunks(1))]
    flow_order += [("wide", 1, turn) for turn in range(fsdp - 1)]
    flow_order += [("tall", 0, chunk) for chunk in range(tall_chunks(0))]
    flow_order += [("wide", 0, turn) for turn in range(fsdp - 1)]
    reached = [0] * max(fsdp - 1, 1)

    def advance(level, count):
        for kind, which, piece in flow_order[reached[level] : reached[level] + count]:
            if kind == "tall":
                tall_level(which, level, piece)
            elif piece < fsdp - 1 - level:
                wide_level(which, level, piece)
        reached[level] += count

    def advance_to(level, kind, which):
        last = max(at for at, item in enumerate(flow_order) if item[:2] == (kind, which))
        if level < fsdp - 1 and last >= reached[level]:
            advance(level, last + 1 - reached[level])

    def tall_final(which):
        count = tall_rows[which]

        def take(way):
            flow = tall_flow[which].at[way]
            for chunk in range(tall_chunks(which)):
                block = flow.at[pl.ds(chunk * width, width)]
                remote(
                    block,
                    block,
                    r.gt_send.at[which, way, chunk],
                    r.gt_recv.at[which, way, chunk],
                    me,
                    z,
                ).wait_recv()
            step = 32

            def one(index):
                at = pl.ds(pl.multiple_of(index * step, step), step)
                tall_sum[which][at] = tall_sum[which][at] + flow[at].astype(F32)

            loop(count // step, one)

        pl.when(jnp.logical_and(z == home, z > 0))(lambda: take(0))
        pl.when(jnp.logical_and(z == home, z < fsdp - 1))(lambda: take(1))

        def close():
            tall_view[which](me)[...] = tall_sum[which][...].astype(BF16)

        pl.when(z == home)(close)

    loads = []
    wide_at = lambda which, start, size: wide_block(which, z).at[:, pl.ds(start, size)]

    def column(ref, member, size):
        return ref.at[:, pl.ds(pl.multiple_of(member * size, size), size)]

    for src, dst in (
        (column(r.wq, me, qc), wide_at(0, 0, qc)),
        (column(r.wk, me, kc), wide_at(0, qc, kc)),
        (column(r.wv, me, kc), wide_at(0, qc + kc, kc)),
        (column(r.wg, me, fc), wide_at(1, 0, fc)),
        (column(r.wu, me, fc), wide_at(1, fc, fc)),
    ):
        load = pltpu.make_async_copy(src, dst, r.load_sem.at[len(loads)])
        load.start()
        loads.append(load)
    slot = lax.rem(me, share)
    tall_loads = []
    for which, src in ((0, r.wo), (1, r.wd)):
        load = pltpu.make_async_copy(
            rows(src, slot, tall_rows[which]), tall[which], r.load_sem.at[5 + which]
        )
        pl.when(z == home)(load.start)
        tall_loads.append(load)

    barrier = pltpu.get_barrier_semaphore()
    partners = [2 * chip for chip in range(1, chips)] + [1]
    for bits in partners:
        pl.semaphore_signal(
            barrier,
            inc=1,
            device_id=place(flip(me, bits), z),
            device_id_type=pl.DeviceIdType.MESH,
        )
    for away in range(1, fsdp):
        pl.semaphore_signal(
            barrier,
            inc=1,
            device_id=place(me, lax.rem(z + away, fsdp)),
            device_id_type=pl.DeviceIdType.MESH,
        )

    tokens = r.tokens[...].astype(F32)
    in_scale = rms_scale(tokens)
    rows(r.xn, me, seq)[...] = (tokens * in_scale * r.in_gain[...]).astype(BF16)
    rows(r.tab, me, seq)[...] = r.table[...]
    rows(r.msk, me, seq)[...] = r.mask[...]
    rows(r.cot, me, seq)[...] = r.cotangent[...]
    r.gain_own[...] = jnp.zeros_like(r.gain_own)

    pl.semaphore_wait(barrier, len(partners) + fsdp - 1)

    view_xn = lambda member: rows(r.xn, member, seq)
    view_tab = lambda member: rows(r.tab, member, seq)
    view_msk = lambda member: rows(r.msk, member, seq)
    view_cot = lambda member: rows(r.cot, member, seq)
    view_pn = lambda member: rows(r.pn, member, seq)
    view_da = lambda member: rows(r.da, member, seq)

    def home_sends(which, chunk):
        if chunk < tall_chunks(which):
            tall_pass(which, chunk, 0)

    def tall_passes(which, chunk):
        if chunk < tall_chunks(which):
            tall_pass(which, chunk, 1)

    for load in loads[:3]:
        load.wait()
    wide_pass(0, 0)
    for job, view in ((0, view_xn), (1, view_tab), (2, view_msk)):
        gather_start(job, view)
    for load in loads[3:]:
        load.wait()
    for load in tall_loads:
        pl.when(z == home)(load.wait)
    gather_forward(0, view_xn)
    if fsdp > 2:
        wide_pass(0, 1)
    home_sends(0, 0)
    for job, view in ((1, view_tab), (2, view_msk)):
        gather_forward(job, view)
    gather_last(0, view_xn)
    for step in range(2, fsdp - 1):
        wide_pass(0, step)
    wide_pass(1, 0)
    for job, view in ((1, view_tab), (2, view_msk)):
        gather_last(job, view)
    for job, view in ((0, view_xn), (1, view_tab), (2, view_msk)):
        gather_finish(job, view)
    home_sends(0, 1)
    wide_pass(0, fsdp - 1)

    lane = lax.broadcasted_iota(jnp.int32, (seq, width), 1)
    front = lane < half
    sign = jnp.where(front, -1.0, 1.0).astype(F32)
    root = width ** (-0.5)

    def turn(values):
        return pltpu.roll(values, half, 1)

    def tables(at):
        table = r.tab[at]
        swapped = turn(table)
        return jnp.where(front, table, swapped), jnp.where(front, swapped, table)

    def at_seq(index):
        return pl.ds(pl.multiple_of(index * seq, seq), seq)

    def attend(index):
        at = at_seq(index)
        cosine, sine = tables(at)
        signed = sine * sign
        qkv = dot(r.xn[at], r.w_qkv[...])
        r.qk[at] = qkv[:, : qc + kc]
        allowed = r.msk[at].astype(F32) > 0.5
        allowed = jnp.concatenate([allowed] * ratio, 0) if ratio > 1 else allowed

        def spun(values, gain):
            values = values * rms_scale(values) * gain
            return (values * cosine + turn(values) * signed).astype(BF16)

        for group in range(kv):
            k_rot = spun(qkv[:, qc + group * width : qc + (group + 1) * width], r.kg[...])
            start = qc + kc + group * width
            values = qkv[:, start : start + width].astype(BF16)
            spins = []
            for head in range(ratio):
                place_at = (group * ratio + head) * width
                spin = spun(qkv[:, place_at : place_at + width], r.qg[...])
                r.rot[at, place_at : place_at + width] = spin
                spins.append(spin)
            r.rot[at, qc + group * width : qc + (group + 1) * width] = k_rot
            r.rot[at, start : start + width] = values
            q_rot = jnp.concatenate(spins, 0)
            scores = dot_nt(q_rot, k_rot) * root
            masked = jnp.where(allowed, scores, NEG_FILL)
            top = jnp.max(masked, axis=-1, keepdims=True)
            total = top + jnp.log(jnp.sum(jnp.exp(masked - top), axis=-1, keepdims=True))
            probs = jnp.where(allowed, jnp.exp(masked - total), 0.0)
            r.probs[index, group] = probs
            mixed = dot(probs.astype(BF16), values).astype(BF16)
            for head in range(ratio):
                place_at = (group * ratio + head) * width
                r.att[at, place_at : place_at + width] = mixed[head * seq : (head + 1) * seq]

    gather_start(3, view_cot)
    loop(team // 2, attend)
    tall_passes(0, 0)
    if fsdp > 2:
        wide_pass(1, 1)
    loop(team, attend, team // 2)
    for chunk in range(1, tall_chunks(0)):
        tall_passes(0, chunk)
    for chunk in range(2, tall_chunks(0)):
        home_sends(0, chunk)
    home_sends(1, 0)

    for chunk in range(tall_chunks(0)):
        tall_pass(0, chunk, 2)
    scatter_start(0, lambda member: dot(rows(r.att, member, seq)[...], r.w_o[...]))
    for step in range(2, fsdp - 1):
        wide_pass(1, step)
    home_sends(1, 1)
    gather_forward(3, view_cot)
    tall_passes(1, 0)
    middle = tokens + scatter_finish(0)
    r.middle[...] = middle
    post_scale = rms_scale(middle)
    view_pn(me)[...] = (middle * post_scale * r.post_gain[...]).astype(BF16)
    gather_start(4, view_pn)
    for chunk in range(2, tall_chunks(1)):
        home_sends(1, chunk)
    gather_last(3, view_cot)
    tall_passes(1, 1)
    gather_forward(4, view_pn)
    for chunk in range(2, tall_chunks(1)):
        tall_passes(1, chunk)
    gather_last(4, view_pn)
    wide_pass(1, fsdp - 1)
    gather_finish(3, view_cot)
    gather_finish(4, view_pn)
    for chunk in range(tall_chunks(1)):
        tall_pass(1, chunk, 2)

    def feed(index):
        at = at_seq(index)
        both = dot(r.pn[at], r.w_gu[...])
        gate, up = both[:, :fc], both[:, fc:]
        sigm = jax.nn.sigmoid(gate)
        soft = gate * sigm
        r.hid[at] = (soft * up).astype(BF16)
        d_hidden = dot_nt(r.cot[at], r.w_d[...])
        r.dgu[at, :fc] = (d_hidden * up * sigm * (1.0 + gate * (1.0 - sigm))).astype(BF16)
        r.dgu[at, fc:] = (d_hidden * soft).astype(BF16)

    loop(team, feed)

    r.g_d[...] = dot_tn(r.hid[...], r.cot[...])
    advance(0, tall_chunks(1))
    scatter_start(1, lambda member: dot_nt(rows(r.dgu, member, seq)[...], r.w_gu[...]))

    def grad_gu(index):
        at = pl.ds(pl.multiple_of(index * band, band), band)
        r.g_gu[at] = dot_tn(r.pn[:, at], r.dgu[...])

    def grad_qkv(index):
        at = pl.ds(pl.multiple_of(index * band, band), band)
        r.g_qkv[at] = dot_tn(r.xn[:, at], r.dqkv[...])

    loop(fsdp, grad_gu)
    advance(0, 1)
    middle_levels = range(1, fsdp - 1)

    def norm_back(grads, values, scale, gain):
        normal = values * scale
        gain_term = jnp.sum(grads * normal, axis=0, keepdims=True)
        scaled = grads * gain
        back = scale * (scaled - normal * jnp.mean(scaled * normal, axis=-1, keepdims=True))
        return back, gain_term

    d_post = scatter_finish(1)
    middle = r.middle[...]
    back, term = norm_back(d_post, middle, rms_scale(middle), r.post_gain[...])
    r.gain_own[1:2] = term
    d_middle = r.cotangent[...].astype(F32) + back
    r.d_middle[...] = d_middle
    view_da(me)[...] = d_middle.astype(BF16)
    gather_start(5, view_da)
    for level in middle_levels[:1]:
        advance_to(level, "tall", 1)
    advance(0, 1)
    gather_forward(5, view_da)
    advance_to(0, "wide", 1)
    gather_last(5, view_da)
    gather_finish(5, view_da)
    r.g_o[...] = dot_tn(r.att[...], r.da[...])
    advance_to(0, "tall", 0)

    def attend_back(index):
        at = at_seq(index)
        cosine, sine = tables(at)
        d_att = dot_nt(r.da[at], r.w_o[...]).astype(BF16)

        def unspun(grads):
            return grads * cosine - turn(grads * sine) * sign

        for group in range(kv):
            k_at = slice(qc + group * width, qc + (group + 1) * width)
            v_at = slice(qc + kc + group * width, qc + kc + (group + 1) * width)
            heads = [
                slice((group * ratio + head) * width, (group * ratio + head + 1) * width)
                for head in range(ratio)
            ]
            d_mixed = jnp.concatenate([d_att[:, head] for head in heads], 0)
            q_rot = jnp.concatenate([r.rot[at, head] for head in heads], 0)
            k_rot = r.rot[at, k_at]
            values = r.rot[at, v_at]
            probs = r.probs[index, group]
            d_probs = dot_nt(d_mixed, values)
            centre = jnp.sum(probs * d_probs, axis=-1, keepdims=True)
            d_scores = (probs * (d_probs - centre) * root).astype(BF16)
            d_query = dot(d_scores, k_rot)
            d_key = dot_tn(d_scores, q_rot)
            d_value = dot_tn(probs.astype(BF16), d_mixed)
            for number, head in enumerate(heads):
                queries = r.qk[at, head]
                back, term = norm_back(
                    unspun(d_query[number * seq : (number + 1) * seq]),
                    queries,
                    rms_scale(queries),
                    r.qg[...],
                )
                r.dqkv[at, head] = back.astype(BF16)
                r.gain_own[2:3, :width] += term
            keys = r.qk[at, k_at]
            back, term = norm_back(unspun(d_key), keys, rms_scale(keys), r.kg[...])
            r.dqkv[at, k_at] = back.astype(BF16)
            r.gain_own[3:4, :width] += term
            r.dqkv[at, v_at] = d_value.astype(BF16)

    view_gain = lambda member: r.gain_all.at[member]
    view_qkv, view_gu = wide_view
    loop(team // 2, attend_back)
    for level in middle_levels[1:]:
        advance_to(level, "tall", 1)
    for level in middle_levels[:1]:
        advance(level, 1)
    loop(team, attend_back, team // 2)
    scatter_start(3, lambda member: dot_nt(rows(r.dqkv, member, seq)[...], r.w_qkv[...]))
    loop(fsdp, grad_qkv)
    advance(0, 1)
    for level in middle_levels[:1]:
        advance_to(level, "wide", 1)
    tall_final(1)
    ring_start(1)
    advance(0, 1)
    for level in middle_levels[1:]:
        advance_to(level, "wide", 1)
    d_normed = scatter_finish(3)
    advance_to(0, "wide", 0)
    for level in middle_levels[:1]:
        advance_to(level, "tall", 0)
    tokens = r.tokens[...].astype(F32)
    back, term = norm_back(d_normed, tokens, rms_scale(tokens), r.in_gain[...])
    r.gain_own[0:1] = term
    r.out_grad[...] = (r.d_middle[...] + back).astype(BF16)
    view_gain(me)[...] = r.gain_own[...]
    gather_start(6, view_gain)
    ring_pass(1, 1)
    wide_final(1)
    gather_start(8, view_gu)
    for level in middle_levels[:1]:
        advance(level, 1)
    scatter_start(2, lambda member: dot(rows(r.hid, member, seq)[...], r.w_d[...]))
    for level in middle_levels[:1]:
        advance_to(level, "wide", 0)
    ring_pass(1, 2)
    for level in middle_levels[1:]:
        advance_to(level, "tall", 0)
    gather_forward(6, view_gain)
    gather_forward(8, view_gu)
    for level in middle_levels[1:]:
        advance_to(level, "wide", 0)
    gather_last(6, view_gain)
    tall_final(0)
    ring_start(0)
    wide_final(0)
    gather_start(9, view_qkv)
    gather_last(8, view_gu)
    ring_pass(1, 3)
    gather_finish(6, view_gain)
    total = r.gain_all[0]
    for member in range(1, team):
        total = total + r.gain_all[member]
    r.gain_line[z] = total
    for away in range(1, fsdp):
        launch(
            remote(
                r.gain_line.at[z],
                r.gain_line.at[z],
                r.gl_sem.at[0, away],
                r.gl_sem.at[1, away],
                me,
                lax.rem(z + away, fsdp),
            )
        )
    r.out_block[...] = (r.middle[...] + scatter_finish(2)).astype(BF16)
    ring_pass(0, 1)
    for away in range(1, fsdp):
        block = r.gain_line.at[lax.rem(z + fsdp - away, fsdp)]
        remote(block, block, r.gl_sem.at[0, away], r.gl_sem.at[1, away], me, z).wait_recv()
    total = r.gain_line[0]
    for plane in range(1, fsdp):
        total = total + r.gain_line[plane]
    r.out_gain[...] = total
    gather_forward(9, view_qkv)
    ring_pass(0, 2)
    gather_last(9, view_qkv)
    ring_pass(0, 3)
    gather_finish(8, view_gu)
    gather_finish(9, view_qkv)
    ring_finish(1)
    ring_finish(0)
    for items in queues.values():
        pending.extend(items)
    for cond, copy in pending:
        guarded(cond, copy.wait_send)


def run_layer(dims, operands):
    team, fsdp, seq, model = dims.team, dims.fsdp, dims.seq, dims.model
    width, kv, ratio, band = dims.width, dims.kv, dims.ratio, dims.band
    qc, kc, fc = dims.qcols, dims.kcols, dims.ffcols
    chips = team // 2
    qkv, gu, many = qc + 2 * kc, 2 * fc, team * seq
    chunks = max(qc, fc) // width
    jobs = 10 + (qc + fc) // width
    inputs = [
        "tokens",
        "table",
        "mask",
        "cotangent",
        "in_gain",
        "post_gain",
        "qg",
        "kg",
        "wq",
        "wk",
        "wv",
        "wo",
        "wg",
        "wu",
        "wd",
    ]
    outputs = [
        "out_block",
        "out_grad",
        "out_gain",
        "oqkv",
        "ogu",
        "oo",
        "od",
    ]
    dma = pltpu.SemaphoreType.DMA
    scratch = dict(
        xn=pltpu.VMEM((many, model), BF16),
        tab=pltpu.VMEM((many, width), F32),
        msk=pltpu.VMEM((many, seq), BF16),
        cot=pltpu.VMEM((many, model), BF16),
        pn=pltpu.VMEM((many, model), BF16),
        da=pltpu.VMEM((many, model), BF16),
        w_qkv=pltpu.VMEM((model, qkv), BF16),
        w_gu=pltpu.VMEM((model, gu), BF16),
        w_o=pltpu.VMEM((qc, model), BF16),
        w_d=pltpu.VMEM((fc, model), BF16),
        qk=pltpu.VMEM((many, qc + kc), F32),
        rot=pltpu.VMEM((many, qkv), BF16),
        probs=pltpu.VMEM((team, kv, ratio * seq, seq), F32),
        att=pltpu.VMEM((many, qc), BF16),
        hid=pltpu.VMEM((many, fc), BF16),
        dgu=pltpu.VMEM((many, gu), BF16),
        dqkv=pltpu.VMEM((many, qkv), BF16),
        middle=pltpu.VMEM((seq, model), F32),
        d_middle=pltpu.VMEM((seq, model), F32),
        rs_out=pltpu.VMEM((4, chips, seq, model), BF16),
        rs_in=pltpu.VMEM((4, chips, seq, model), BF16),
        rs_last=pltpu.VMEM((4, max(chips - 1, 1), seq, model), BF16),
        rs_sum=pltpu.VMEM((4, seq, model), F32),
        g_qkv=pltpu.VMEM((model, qkv), F32),
        g_gu=pltpu.VMEM((model, gu), F32),
        g_o=pltpu.VMEM((qc, model), F32),
        g_d=pltpu.VMEM((fc, model), F32),
        f_qkv=pltpu.VMEM((2, model, qkv), BF16),
        f_gu=pltpu.VMEM((2, model, gu), BF16),
        f_o=pltpu.VMEM((2, qc, model), BF16),
        f_d=pltpu.VMEM((2, fc, model), BF16),

        gain_own=pltpu.VMEM((8, model), F32),
        gain_all=pltpu.VMEM((team, 8, model), F32),
        gain_line=pltpu.VMEM((fsdp, 8, model), F32),
        ag_send=dma((jobs, team)),
        ag_recv=dma((jobs, team)),
        rs_sem=dma((4, 4, chips)),
        ww_send=dma((2, 2, fsdp)),
        ww_recv=dma((2, fsdp)),
        wt_send=dma((2, 2, chunks)),
        wt_recv=dma((2, chunks)),
        gw_send=dma((2, 2, fsdp)),
        gw_recv=dma((2, 2, fsdp)),
        gt_send=dma((2, 2, chunks)),
        gt_recv=dma((2, 2, chunks)),
        gl_sem=dma((2, fsdp)),
        load_sem=dma((7,)),
    )
    vmem = pl.BlockSpec(memory_space=pltpu.VMEM)
    anywhere = pl.BlockSpec(memory_space=pl.ANY)
    shapes = [
        jax.ShapeDtypeStruct((seq, model), BF16),
        jax.ShapeDtypeStruct((seq, model), BF16),
        jax.ShapeDtypeStruct((8, model), F32),
    ] + [
        jax.ShapeDtypeStruct(shape, BF16)
        for shape in (
            (team * band, qkv),
            (team * band, gu),
            (dims.share * qc, model),
            (dims.share * fc, model),
        )
    ]
    return pl.pallas_call(
        partial(layer_kernel, inputs + outputs + list(scratch), dims),
        out_shape=shapes,
        in_specs=[vmem] * 8 + [anywhere] * 7,
        out_specs=[vmem] * 7,
        scratch_shapes=list(scratch.values()),
        compiler_params=pltpu.CompilerParams(
            collective_id=0, has_side_effects=True, vmem_limit_bytes=VMEM_LIMIT
        ),
        name="layer",
    )(*operands)


def body(
    mesh_sizes,
    tokens_in,
    input_gain,
    q_gain,
    k_gain,
    w_query,
    w_key,
    w_value,
    w_output,
    post_gain,
    w_gate,
    w_up,
    w_down,
    segment_ids,
    positions,
    out_cotangent,
):
    dims = sizes_of(mesh_sizes, tokens_in, w_query, w_key, w_output, w_gate, w_down, q_gain)
    seq, width = dims.seq, dims.width
    ladder = jnp.arange(width // 2, dtype=F32)
    inverse = jnp.exp(ladder * (-2.0 * math.log(ROPE_BASE) / width))
    angles = positions.astype(F32)[:, None] * inverse[None, :]
    table = jnp.concatenate([jnp.cos(angles), jnp.sin(angles)], -1)
    steps = jnp.arange(seq)
    mask = (
        (segment_ids[:, None] == segment_ids[None, :]) & (steps[:, None] >= steps[None, :])
    ).astype(BF16)
    weights = (w_query, w_key, w_value, w_output, w_gate, w_up, w_down)
    done = run_layer(
        dims,
        (
            tokens_in,
            table,
            mask,
            out_cotangent,
            input_gain[None],
            post_gain[None],
            q_gain[None],
            k_gain[None],
            *weights,
        ),
    )
    gains, grads = done[2], tuple(done[3:])
    reps, team = dims.reps, dims.team
    if reps > team:
        rings = [list(range(first, reps, team)) for first in range(team)]
        gains = lax.psum(gains, "rep", axis_index_groups=rings)
        grads = lax.psum(grads, "rep", axis_index_groups=rings)
    return widen(dims, done[0], done[1], gains, grads)


def widen_kernel(dims, *refs):
    width, qc, kc, fc = dims.width, dims.qcols, dims.kcols, dims.ffcols
    block, grad, gains, qkv, gu, tall_o, tall_d = refs[:7]
    outs = refs[7:]
    outs[0][...] = block[...]
    outs[1][...] = grad[...]
    outs[2][...] = gains[0]
    outs[3][...] = gains[2, :width]
    outs[4][...] = gains[3, :width]
    outs[5][...] = gains[1]
    outs[6][...] = qkv[:, :qc].astype(F32)
    outs[7][...] = qkv[:, qc : qc + kc].astype(F32)
    outs[8][...] = qkv[:, qc + kc :].astype(F32)
    outs[9][...] = tall_o[...].astype(F32)
    outs[10][...] = gu[:, :fc].astype(F32)
    outs[11][...] = gu[:, fc:].astype(F32)
    outs[12][...] = tall_d[...].astype(F32)


def widen(dims, block_out, input_grad, gains, grads):
    steps, model, width, band = dims.team, dims.model, dims.width, dims.band
    qc, kc, fc = dims.qcols, dims.kcols, dims.ffcols

    def by_rows(count):
        return pl.BlockSpec((count // steps, model), lambda step: (step, 0))

    def stacked(size):
        return pl.BlockSpec((band, size), lambda step: (step, 0))

    def by_columns(size):
        return pl.BlockSpec((band, size), lambda step: (0, step))

    def flat(size):
        return pl.BlockSpec((size,), lambda step: (0,))

    count_o, count_d = grads[2].shape[0], grads[3].shape[0]
    return pl.pallas_call(
        partial(widen_kernel, dims),
        grid=(steps,),
        in_specs=[
            by_rows(dims.seq),
            by_rows(dims.seq),
            pl.BlockSpec(gains.shape, lambda step: (0, 0)),
            stacked(qc + 2 * kc),
            stacked(2 * fc),
            by_rows(count_o),
            by_rows(count_d),
        ],
        out_specs=[
            by_rows(dims.seq),
            by_rows(dims.seq),
            flat(model),
            flat(width),
            flat(width),
            flat(model),
            by_columns(qc),
            by_columns(kc),
            by_columns(kc),
            by_rows(count_o),
            by_columns(fc),
            by_columns(fc),
            by_rows(count_d),
        ],
        out_shape=[
            jax.ShapeDtypeStruct((dims.seq, model), BF16),
            jax.ShapeDtypeStruct((dims.seq, model), BF16),
            jax.ShapeDtypeStruct((model,), F32),
            jax.ShapeDtypeStruct((width,), F32),
            jax.ShapeDtypeStruct((width,), F32),
            jax.ShapeDtypeStruct((model,), F32),
            jax.ShapeDtypeStruct((band, steps * qc), F32),
            jax.ShapeDtypeStruct((band, steps * kc), F32),
            jax.ShapeDtypeStruct((band, steps * kc), F32),
            jax.ShapeDtypeStruct((count_o, model), F32),
            jax.ShapeDtypeStruct((band, steps * fc), F32),
            jax.ShapeDtypeStruct((band, steps * fc), F32),
            jax.ShapeDtypeStruct((count_d, model), F32),
        ],
        compiler_params=pltpu.CompilerParams(vmem_limit_bytes=VMEM_LIMIT),
        name="widen",
    )(block_out, input_grad, gains, *grads)


def solution(mesh):
    tokens = P(("rep", "fsdp"), None)
    ids = P(("rep", "fsdp"))
    weight = P("fsdp", None)
    in_specs = (
        (tokens,)
        + (P(),) * 3
        + (weight,) * 4
        + (P(),)
        + (weight,) * 3
        + (ids, ids, tokens)
    )
    out_specs = (tokens, tokens) + (P(),) * 4 + (weight,) * 7
    return jax.shard_map(
        partial(body, (mesh.shape["rep"], mesh.shape["fsdp"])),
        mesh=mesh,
        in_specs=in_specs,
        out_specs=out_specs,
        check_vma=False,
    )
```

```python
from functools import partial
import math
from types import SimpleNamespace

import jax
import jax.numpy as jnp
from jax import lax
from jax.experimental import pallas as pl
from jax.experimental.pallas import tpu as pltpu
from jax.sharding import PartitionSpec as P

EPS = 1e-06
ROPE_BASE = 1000000.0
NEG_FILL = -1e30
F32 = jnp.float32
BF16 = jnp.bfloat16
VMEM_LIMIT = 63 * 1024 * 1024


def dot(first, second):
    return lax.dot_general(first, second, (((1,), (0,)), ((), ())), preferred_element_type=F32)


def dot_nt(first, second):
    return lax.dot_general(first, second, (((1,), (1,)), ((), ())), preferred_element_type=F32)


def dot_tn(first, second):
    return lax.dot_general(first, second, (((0,), (0,)), ((), ())), preferred_element_type=F32)


def rms_scale(values):
    return lax.rsqrt(jnp.mean(values * values, axis=-1, keepdims=True) + EPS)


def flip(index, bits):
    out = index
    step = 1
    while step <= bits:
        if bits & step:
            out = out + step * (1 - 2 * lax.rem(index // step, 2))
        step *= 2
    return out


def sizes_of(mesh_sizes, tokens, w_query, w_key, w_output, w_gate, w_down, q_gain):
    reps, fsdp = mesh_sizes
    width = q_gain.shape[0]
    heads_q = w_query.shape[1] // width
    heads_kv = w_key.shape[1] // width
    team = math.gcd(reps, heads_kv)
    assert team >= 2 and team & (team - 1) == 0 and team % fsdp == 0
    dims = SimpleNamespace(
        reps=reps,
        fsdp=fsdp,
        team=team,
        width=width,
        seq=tokens.shape[0],
        model=tokens.shape[1],
        kv=heads_kv // team,
        ratio=heads_q // heads_kv,
        qcols=w_query.shape[1] // team,
        kcols=w_key.shape[1] // team,
        ffcols=w_gate.shape[1] // team,
        band=w_query.shape[0],
        share=team // fsdp,
    )
    return dims


def layer_kernel(names, dims, *refs):
    r = SimpleNamespace(**dict(zip(names, refs)))
    team, fsdp = dims.team, dims.fsdp
    seq, model, width = dims.seq, dims.model, dims.width
    kv, ratio, band, share = dims.kv, dims.ratio, dims.band, dims.share
    qc, kc, fc = dims.qcols, dims.kcols, dims.ffcols
    chips = team // 2
    half = width // 2

    rep = lax.axis_index("rep")
    z = lax.axis_index("fsdp")
    me = lax.rem(rep, team)
    base = rep - me
    home = me // share

    def place(member, plane):
        return {"rep": base + member, "fsdp": plane}

    def remote(src, dst, send_sem, recv_sem, member, plane):
        return pltpu.make_async_remote_copy(
            src_ref=src,
            dst_ref=dst,
            send_sem=send_sem,
            recv_sem=recv_sem,
            device_id=place(member, plane),
            device_id_type=pl.DeviceIdType.MESH,
        )

    pending = []

    def launch(copy, cond=None):
        if cond is None:
            copy.start()
        else:
            pl.when(cond)(copy.start)
        pending.append((cond, copy))

    def guarded(cond, action):
        if cond is None:
            action()
        else:
            pl.when(cond)(action)

    queues = {}

    def paced(queue, limit, cond, copy, before=None):
        items = queues.setdefault(queue, [])
        if len(items) >= limit:
            earlier, first = items.pop(0)
            pl.when(earlier)(first.wait_send)

        def start():
            if before is not None:
                before()
            copy.start()

        pl.when(cond)(start)
        items.append((cond, copy))

    def rows(ref, index, count):
        return ref.at[pl.ds(pl.multiple_of(index * count, count), count)]

    def loop(count, step, first=0):
        def run(index, carry):
            step(index)
            return carry

        lax.fori_loop(first, count, run, 0, unroll=2)

    near = [2] if chips == 2 else [2, 4]
    far = [2 * chip for chip in range(1, chips) if 2 * chip not in near]
    core = lax.rem(me, 2)
    passes = chips == 4
    along = flip(me, 2) * (1 - core) + flip(me, 4) * core
    across = flip(me, 4) * (1 - core) + flip(me, 2) * core

    def gather_send(job, block, bits, member, cond):
        send_sem, recv_sem = r.ag_send.at[job, bits], r.ag_recv.at[job, bits]
        launch(remote(block, block, send_sem, recv_sem, member, z), cond)

    def gather_start(job, view, active=None):
        cond = None if active is None else active(me)
        for bits in near + [1] + ([] if passes else far):
            gather_send(job, view(me), bits, flip(me, bits), cond)

    def gather_wait(job, view, bits, active=None):
        block = view(flip(me, bits))
        cond = None if active is None else active(flip(me, bits))
        copy = remote(
            block, block, r.ag_send.at[job, bits], r.ag_recv.at[job, bits], flip(me, 1), z
        )
        guarded(cond, copy.wait_recv)

    def gather_beside(job, view, bits, active):
        block = view(flip(me, bits))
        cond = None if active is None else active(flip(me, bits))
        gather_send(job, block, bits + 1, flip(me, 1), cond)

    def gather_forward(job, view, active=None):
        for bits in near:
            gather_wait(job, view, bits, active)
        if passes:
            block = view(along)
            cond = None if active is None else active(along)
            gather_send(job, block, far[0], across, cond)
        for bits in near:
            gather_beside(job, view, bits, active)

    def gather_last(job, view, active=None):
        for bits in far:
            gather_wait(job, view, bits, active)
            gather_beside(job, view, bits, active)

    def gather_finish(job, view, active=None):
        for chip in range(chips):
            gather_wait(job, view, 2 * chip + 1, active)

    def ring_jobs(which):
        first = 0 if which == 0 else tall_chunks(0)
        for chunk in range(tall_chunks(which)):

            def view(member, chunk=chunk):
                return tall_view[which](member).at[pl.ds(chunk * width, width)]

            yield 10 + first + chunk, view

    def ring_start(which):
        for job, view in ring_jobs(which):
            if not passes:
                gather_start(job, view, home_of)
                continue
            bits = 2 + 2 * core
            block, cond = view(me), home_of(me)
            send, recv = r.ag_send.at[job, 0], r.ag_recv.at[job, bits]
            launch(remote(block, block, send, recv, along, z), cond)
            gather_send(job, block, 1, flip(me, 1), cond)

    def ring_pass(which, stage):
        for job, view in ring_jobs(which):
            if not passes:
                if stage == 1:
                    gather_forward(job, view, home_of)
                    gather_last(job, view, home_of)
                continue
            bits = (2 + 2 * core, 6, 4 - 2 * core)[stage - 1]
            owner = (along, flip(me, 6), across)[stage - 1]
            block, cond = view(owner), home_of(owner)
            recv = r.ag_recv.at[job, bits]
            copy = remote(block, block, r.ag_send.at[job, 0], recv, along, z)
            guarded(cond, copy.wait_recv)
            if stage < 3:
                target = across if stage == 1 else along
                after = r.ag_recv.at[job, 6 if stage == 1 else 4 - 2 * core]
                send = r.ag_send.at[job, 2 * stage]
                launch(remote(block, block, send, after, target, z), cond)
            send, after = r.ag_send.at[job, 1 + 2 * stage], r.ag_recv.at[job, bits + 1]
            launch(remote(block, block, send, after, flip(me, 1), z), cond)

    def ring_finish(which):
        for job, view in ring_jobs(which):
            gather_finish(job, view, home_of)

    def home_of(member):
        return member // share == z

    def scatter_start(job, part):
        for chip in reversed(range(chips)):
            bits = 2 * chip + 1
            r.rs_out[job, chip] = part(flip(me, bits)).astype(BF16)
            launch(
                remote(
                    r.rs_out.at[job, chip],
                    r.rs_in.at[job, chip],
                    r.rs_sem.at[job, 0, chip],
                    r.rs_sem.at[job, 1, chip],
                    flip(me, 1),
                    z,
                )
            )

        def arrived(chip):
            block = r.rs_in.at[job, chip]
            remote(
                block,
                block,
                r.rs_sem.at[job, 0, chip],
                r.rs_sem.at[job, 1, chip],
                flip(me, 1),
                z,
            ).wait_recv()

        for chip in list(reversed(range(1, chips))):
            mine = part(flip(me, 2 * chip))
            arrived(chip)
            r.rs_in[job, chip] = (mine + r.rs_in[job, chip].astype(F32)).astype(BF16)
            launch(
                remote(
                    r.rs_in.at[job, chip],
                    r.rs_last.at[job, chip - 1],
                    r.rs_sem.at[job, 2, chip],
                    r.rs_sem.at[job, 3, chip],
                    flip(me, 2 * chip),
                    z,
                )
            )
        mine = part(me)
        arrived(0)
        r.rs_sum[job] = mine + r.rs_in[job, 0].astype(F32)

    def scatter_finish(job):
        total = r.rs_sum[job]
        for chip in range(1, chips):
            block = r.rs_last.at[job, chip - 1]
            remote(
                block,
                block,
                r.rs_sem.at[job, 2, chip],
                r.rs_sem.at[job, 3, chip],
                flip(me, 2 * chip),
                z,
            ).wait_recv()
            total = total + r.rs_last[job, chip - 1].astype(F32)
        return total

    wide = (r.w_qkv, r.w_gu)
    tall = (r.w_o, r.w_d)
    tall_rows = (qc, fc)

    def wide_block(which, plane):
        return rows(wide[which], plane, band)

    def wide_pass(which, step):
        for way, exists, plane, more, target in (
            (0, z - step >= 0, z - step, z < fsdp - 1, z + 1),
            (1, z + step <= fsdp - 1, z + step, z > 0, z - 1),
        ):
            plane = jnp.clip(plane, 0, fsdp - 1)
            block = wide_block(which, plane)
            copy = remote(
                block,
                block,
                r.ww_send.at[which, way, step],
                r.ww_recv.at[which, plane],
                me,
                jnp.clip(target, 0, fsdp - 1),
            )
            if step > 0:
                pl.when(exists)(copy.wait_recv)
            if step < fsdp - 1:
                paced(("wide", way), 2, jnp.logical_and(exists, more), copy)

    def tall_chunks(which):
        return tall_rows[which] // width

    def tall_pass(which, chunk, stage):
        block = tall[which].at[pl.ds(chunk * width, width)]
        up = jnp.logical_and(z >= home, z < fsdp - 1)
        down = jnp.logical_and(z <= home, z > 0)
        begins = z == home
        ends = jnp.logical_and(z != home, jnp.logical_or(z == 0, z == fsdp - 1))
        between = jnp.logical_and(z != home, jnp.logical_and(z > 0, z < fsdp - 1))
        for way, cond, target in ((0, up, z + 1), (1, down, z - 1)):
            copy = remote(
                block,
                block,
                r.wt_send.at[which, way, chunk],
                r.wt_recv.at[which, chunk],
                me,
                jnp.clip(target, 0, fsdp - 1),
            )
            if stage == 2:
                if way == 0:
                    pl.when(ends)(copy.wait_recv)
                continue
            if stage == 1 and way == 0:
                pl.when(between)(copy.wait_recv)
            own = begins if stage == 0 else between
            paced(("tall", way, stage), 1, jnp.logical_and(cond, own), copy)

    wide_sum = (r.g_qkv, r.g_gu)
    tall_sum = (r.g_o, r.g_d)
    wide_flow = (r.f_qkv, r.f_gu)
    tall_flow = (r.f_o, r.f_d)
    wide_view = (lambda member: rows(r.oqkv, member, band), lambda member: rows(r.ogu, member, band))
    tall_view = (
        lambda member: rows(r.oo, lax.rem(member, share), qc),
        lambda member: rows(r.od, lax.rem(member, share), fc),
    )

    def merge(target, own, start, count, has_incoming):
        step = 32

        def one(index):
            at = pl.ds(pl.multiple_of(start + index * step, step), step)
            value = own[at]
            if has_incoming:
                value = value + target[at].astype(F32)
            target[at] = value.astype(BF16)

        loop(count // step, one)


    def wide_level(which, level, turn):
        for way, here in ((0, level), (1, fsdp - 1 - level)):
            flow = wide_flow[which].at[way]
            plane = fsdp - 1 - turn if way == 0 else turn
            block = flow.at[pl.ds(plane * band, band)]
            copy = remote(
                block,
                block,
                r.gw_send.at[which, way, plane],
                r.gw_recv.at[which, way, plane],
                me,
                here + 1 if way == 0 else here - 1,
            )

            def before(flow=flow, plane=plane, copy=copy):
                if level > 0:
                    copy.wait_recv()
                merge(flow, wide_sum[which], plane * band, band, level > 0)

            paced(("level", way, level), 4, z == here, copy, before)

    def wide_final(which):
        def take(way):
            flow = wide_flow[which].at[way]
            block = rows(flow, z, band)
            remote(
                block,
                block,
                r.gw_send.at[which, way, z],
                r.gw_recv.at[which, way, z],
                me,
                z,
            ).wait_recv()
            step = 32

            def one(index):
                at = pl.ds(pl.multiple_of(z * band + index * step, step), step)
                wide_sum[which][at] = wide_sum[which][at] + flow[at].astype(F32)

            loop(band // step, one)

        pl.when(z > 0)(lambda: take(0))
        pl.when(z < fsdp - 1)(lambda: take(1))
        wide_view[which](me)[...] = rows(wide_sum[which], z, band)[...].astype(BF16)

    def tall_level(which, level, chunk):
        for way, here in ((0, level), (1, fsdp - 1 - level)):
            flow = tall_flow[which].at[way]
            block = flow.at[pl.ds(chunk * width, width)]
            copy = remote(
                block,
                block,
                r.gt_send.at[which, way, chunk],
                r.gt_recv.at[which, way, chunk],
                me,
                here + 1 if way == 0 else here - 1,
            )

            def before(flow=flow, chunk=chunk, copy=copy):
                if level > 0:
                    copy.wait_recv()
                merge(flow, tall_sum[which], chunk * width, width, level > 0)

            toward = home > here if way == 0 else home < here
            paced(("level", way, level), 4, jnp.logical_and(z == here, toward), copy, before)

    flow_order = [("tall", 1, chunk) for chunk in range(tall_chunks(1))]
    flow_order += [("wide", 1, turn) for turn in range(fsdp - 1)]
    flow_order += [("tall", 0, chunk) for chunk in range(tall_chunks(0))]
    flow_order += [("wide", 0, turn) for turn in range(fsdp - 1)]
    reached = [0] * max(fsdp - 1, 1)

    def advance(level, count):
        for kind, which, piece in flow_order[reached[level] : reached[level] + count]:
            if kind == "tall":
                tall_level(which, level, piece)
            elif piece < fsdp - 1 - level:
                wide_level(which, level, piece)
        reached[level] += count

    def advance_to(level, kind, which):
        last = max(at for at, item in enumerate(flow_order) if item[:2] == (kind, which))
        if level < fsdp - 1 and last >= reached[level]:
            advance(level, last + 1 - reached[level])

    def tall_final(which):
        count = tall_rows[which]

        def take(way):
            flow = tall_flow[which].at[way]
            for chunk in range(tall_chunks(which)):
                block = flow.at[pl.ds(chunk * width, width)]
                remote(
                    block,
                    block,
                    r.gt_send.at[which, way, chunk],
                    r.gt_recv.at[which, way, chunk],
                    me,
                    z,
                ).wait_recv()
            step = 32

            def one(index):
                at = pl.ds(pl.multiple_of(index * step, step), step)
                tall_sum[which][at] = tall_sum[which][at] + flow[at].astype(F32)

            loop(count // step, one)

        pl.when(jnp.logical_and(z == home, z > 0))(lambda: take(0))
        pl.when(jnp.logical_and(z == home, z < fsdp - 1))(lambda: take(1))

        def close():
            tall_view[which](me)[...] = tall_sum[which][...].astype(BF16)

        pl.when(z == home)(close)

    loads = []
    wide_at = lambda which, start, size: wide_block(which, z).at[:, pl.ds(start, size)]

    def column(ref, member, size):
        return ref.at[:, pl.ds(pl.multiple_of(member * size, size), size)]

    for src, dst in (
        (column(r.wq, me, qc), wide_at(0, 0, qc)),
        (column(r.wk, me, kc), wide_at(0, qc, kc)),
        (column(r.wv, me, kc), wide_at(0, qc + kc, kc)),
        (column(r.wg, me, fc), wide_at(1, 0, fc)),
        (column(r.wu, me, fc), wide_at(1, fc, fc)),
    ):
        load = pltpu.make_async_copy(src, dst, r.load_sem.at[len(loads)])
        load.start()
        loads.append(load)
    slot = lax.rem(me, share)
    tall_loads = []
    for which, src in ((0, r.wo), (1, r.wd)):
        load = pltpu.make_async_copy(
            rows(src, slot, tall_rows[which]), tall[which], r.load_sem.at[5 + which]
        )
        pl.when(z == home)(load.start)
        tall_loads.append(load)

    barrier = pltpu.get_barrier_semaphore()
    partners = [2 * chip for chip in range(1, chips)] + [1]
    for bits in partners:
        pl.semaphore_signal(
            barrier,
            inc=1,
            device_id=place(flip(me, bits), z),
            device_id_type=pl.DeviceIdType.MESH,
        )
    for away in range(1, fsdp):
        pl.semaphore_signal(
            barrier,
            inc=1,
            device_id=place(me, lax.rem(z + away, fsdp)),
            device_id_type=pl.DeviceIdType.MESH,
        )

    tokens = r.tokens[...].astype(F32)
    in_scale = rms_scale(tokens)
    rows(r.xn, me, seq)[...] = (tokens * in_scale * r.in_gain[...]).astype(BF16)
    rows(r.tab, me, seq)[...] = r.table[...]
    rows(r.msk, me, seq)[...] = r.mask[...]
    rows(r.cot, me, seq)[...] = r.cotangent[...]
    r.gain_own[...] = jnp.zeros_like(r.gain_own)

    pl.semaphore_wait(barrier, len(partners) + fsdp - 1)

    view_xn = lambda member: rows(r.xn, member, seq)
    view_tab = lambda member: rows(r.tab, member, seq)
    view_msk = lambda member: rows(r.msk, member, seq)
    view_cot = lambda member: rows(r.cot, member, seq)
    view_pn = lambda member: rows(r.pn, member, seq)
    view_da = lambda member: rows(r.da, member, seq)

    def home_sends(which, chunk):
        if chunk < tall_chunks(which):
            tall_pass(which, chunk, 0)

    def tall_passes(which, chunk):
        if chunk < tall_chunks(which):
            tall_pass(which, chunk, 1)

    for load in loads[:3]:
        load.wait()
    wide_pass(0, 0)
    for job, view in ((0, view_xn), (1, view_tab), (2, view_msk)):
        gather_start(job, view)
    for load in loads[3:]:
        load.wait()
    for load in tall_loads:
        pl.when(z == home)(load.wait)
    gather_forward(0, view_xn)
    if fsdp > 2:
        wide_pass(0, 1)
    home_sends(0, 0)
    for job, view in ((1, view_tab), (2, view_msk)):
        gather_forward(job, view)
    gather_last(0, view_xn)
    for step in range(2, fsdp - 1):
        wide_pass(0, step)
    wide_pass(1, 0)
    for job, view in ((1, view_tab), (2, view_msk)):
        gather_last(job, view)
    for job, view in ((0, view_xn), (1, view_tab), (2, view_msk)):
        gather_finish(job, view)
    home_sends(0, 1)
    wide_pass(0, fsdp - 1)

    lane = lax.broadcasted_iota(jnp.int32, (seq, width), 1)
    front = lane < half
    sign = jnp.where(front, -1.0, 1.0).astype(F32)
    root = width ** (-0.5)

    def turn(values):
        return pltpu.roll(values, half, 1)

    def tables(at):
        table = r.tab[at]
        swapped = turn(table)
        return jnp.where(front, table, swapped), jnp.where(front, swapped, table)

    def at_seq(index):
        return pl.ds(pl.multiple_of(index * seq, seq), seq)

    def attend(index):
        at = at_seq(index)
        cosine, sine = tables(at)
        signed = sine * sign
        qkv = dot(r.xn[at], r.w_qkv[...])
        r.qk[at] = qkv[:, : qc + kc]
        allowed = r.msk[at].astype(F32) > 0.5
        allowed = jnp.concatenate([allowed] * ratio, 0) if ratio > 1 else allowed

        def spun(values, gain):
            values = values * rms_scale(values) * gain
            return (values * cosine + turn(values) * signed).astype(BF16)

        for group in range(kv):
            k_rot = spun(qkv[:, qc + group * width : qc + (group + 1) * width], r.kg[...])
            start = qc + kc + group * width
            values = qkv[:, start : start + width].astype(BF16)
            spins = []
            for head in range(ratio):
                place_at = (group * ratio + head) * width
                spin = spun(qkv[:, place_at : place_at + width], r.qg[...])
                r.rot[at, place_at : place_at + width] = spin
                spins.append(spin)
            r.rot[at, qc + group * width : qc + (group + 1) * width] = k_rot
            r.rot[at, start : start + width] = values
            q_rot = jnp.concatenate(spins, 0)
            scores = dot_nt(q_rot, k_rot) * root
            masked = jnp.where(allowed, scores, NEG_FILL)
            top = jnp.max(masked, axis=-1, keepdims=True)
            total = top + jnp.log(jnp.sum(jnp.exp(masked - top), axis=-1, keepdims=True))
            probs = jnp.where(allowed, jnp.exp(masked - total), 0.0)
            r.probs[index, group] = probs
            mixed = dot(probs.astype(BF16), values).astype(BF16)
            for head in range(ratio):
                place_at = (group * ratio + head) * width
                r.att[at, place_at : place_at + width] = mixed[head * seq : (head + 1) * seq]

    gather_start(3, view_cot)
    loop(team // 2, attend)
    tall_passes(0, 0)
    if fsdp > 2:
        wide_pass(1, 1)
    loop(team, attend, team // 2)
    for chunk in range(1, tall_chunks(0)):
        tall_passes(0, chunk)
    for chunk in range(2, tall_chunks(0)):
        home_sends(0, chunk)
    home_sends(1, 0)

    for chunk in range(tall_chunks(0)):
        tall_pass(0, chunk, 2)
    scatter_start(0, lambda member: dot(rows(r.att, member, seq)[...], r.w_o[...]))
    for step in range(2, fsdp - 1):
        wide_pass(1, step)
    home_sends(1, 1)
    gather_forward(3, view_cot)
    tall_passes(1, 0)
    middle = tokens + scatter_finish(0)
    r.middle[...] = middle
    post_scale = rms_scale(middle)
    view_pn(me)[...] = (middle * post_scale * r.post_gain[...]).astype(BF16)
    gather_start(4, view_pn)
    for chunk in range(2, tall_chunks(1)):
        home_sends(1, chunk)
    gather_last(3, view_cot)
    tall_passes(1, 1)
    gather_forward(4, view_pn)
    for chunk in range(2, tall_chunks(1)):
        tall_passes(1, chunk)
    gather_last(4, view_pn)
    wide_pass(1, fsdp - 1)
    gather_finish(3, view_cot)
    gather_finish(4, view_pn)
    for chunk in range(tall_chunks(1)):
        tall_pass(1, chunk, 2)

    def feed(index):
        at = at_seq(index)
        both = dot(r.pn[at], r.w_gu[...])
        gate, up = both[:, :fc], both[:, fc:]
        sigm = jax.nn.sigmoid(gate)
        soft = gate * sigm
        r.hid[at] = (soft * up).astype(BF16)
        d_hidden = dot_nt(r.cot[at], r.w_d[...])
        r.dgu[at, :fc] = (d_hidden * up * sigm * (1.0 + gate * (1.0 - sigm))).astype(BF16)
        r.dgu[at, fc:] = (d_hidden * soft).astype(BF16)

    loop(team, feed)

    r.g_d[...] = dot_tn(r.hid[...], r.cot[...])
    advance(0, tall_chunks(1))
    scatter_start(1, lambda member: dot_nt(rows(r.dgu, member, seq)[...], r.w_gu[...]))

    def grad_gu(index):
        at = pl.ds(pl.multiple_of(index * band, band), band)
        r.g_gu[at] = dot_tn(r.pn[:, at], r.dgu[...])

    def grad_qkv(index):
        at = pl.ds(pl.multiple_of(index * band, band), band)
        r.g_qkv[at] = dot_tn(r.xn[:, at], r.dqkv[...])

    loop(fsdp, grad_gu)
    advance(0, 1)
    middle_levels = range(1, fsdp - 1)

    def norm_back(grads, values, scale, gain):
        normal = values * scale
        gain_term = jnp.sum(grads * normal, axis=0, keepdims=True)
        scaled = grads * gain
        back = scale * (scaled - normal * jnp.mean(scaled * normal, axis=-1, keepdims=True))
        return back, gain_term

    d_post = scatter_finish(1)
    middle = r.middle[...]
    back, term = norm_back(d_post, middle, rms_scale(middle), r.post_gain[...])
    r.gain_own[1:2] = term
    d_middle = r.cotangent[...].astype(F32) + back
    r.d_middle[...] = d_middle
    view_da(me)[...] = d_middle.astype(BF16)
    gather_start(5, view_da)
    for level in middle_levels[:1]:
        advance_to(level, "tall", 1)
    advance(0, 1)
    gather_forward(5, view_da)
    advance_to(0, "wide", 1)
    gather_last(5, view_da)
    gather_finish(5, view_da)
    r.g_o[...] = dot_tn(r.att[...], r.da[...])
    advance_to(0, "tall", 0)

    def attend_back(index):
        at = at_seq(index)
        cosine, sine = tables(at)
        d_att = dot_nt(r.da[at], r.w_o[...]).astype(BF16)

        def unspun(grads):
            return grads * cosine - turn(grads * sine) * sign

        for group in range(kv):
            k_at = slice(qc + group * width, qc + (group + 1) * width)
            v_at = slice(qc + kc + group * width, qc + kc + (group + 1) * width)
            heads = [
                slice((group * ratio + head) * width, (group * ratio + head + 1) * width)
                for head in range(ratio)
            ]
            d_mixed = jnp.concatenate([d_att[:, head] for head in heads], 0)
            q_rot = jnp.concatenate([r.rot[at, head] for head in heads], 0)
            k_rot = r.rot[at, k_at]
            values = r.rot[at, v_at]
            probs = r.probs[index, group]
            d_probs = dot_nt(d_mixed, values)
            centre = jnp.sum(probs * d_probs, axis=-1, keepdims=True)
            d_scores = (probs * (d_probs - centre) * root).astype(BF16)
            d_query = dot(d_scores, k_rot)
            d_key = dot_tn(d_scores, q_rot)
            d_value = dot_tn(probs.astype(BF16), d_mixed)
            for number, head in enumerate(heads):
                queries = r.qk[at, head]
                back, term = norm_back(
                    unspun(d_query[number * seq : (number + 1) * seq]),
                    queries,
                    rms_scale(queries),
                    r.qg[...],
                )
                r.dqkv[at, head] = back.astype(BF16)
                r.gain_own[2:3, :width] += term
            keys = r.qk[at, k_at]
            back, term = norm_back(unspun(d_key), keys, rms_scale(keys), r.kg[...])
            r.dqkv[at, k_at] = back.astype(BF16)
            r.gain_own[3:4, :width] += term
            r.dqkv[at, v_at] = d_value.astype(BF16)

    view_gain = lambda member: r.gain_all.at[member]
    view_qkv, view_gu = wide_view
    loop(team // 2, attend_back)
    for level in middle_levels[1:]:
        advance_to(level, "tall", 1)
    for level in middle_levels[:1]:
        advance(level, 1)
    loop(team, attend_back, team // 2)
    scatter_start(3, lambda member: dot_nt(rows(r.dqkv, member, seq)[...], r.w_qkv[...]))
    loop(fsdp, grad_qkv)
    advance(0, 1)
    for level in middle_levels[:1]:
        advance_to(level, "wide", 1)
    tall_final(1)
    ring_start(1)
    scatter_start(2, lambda member: dot(rows(r.hid, member, seq)[...], r.w_d[...]))
    advance(0, 1)
    for level in middle_levels[1:]:
        advance_to(level, "wide", 1)
    d_normed = scatter_finish(3)
    advance_to(0, "wide", 0)
    for level in middle_levels[:1]:
        advance_to(level, "tall", 0)
    tokens = r.tokens[...].astype(F32)
    back, term = norm_back(d_normed, tokens, rms_scale(tokens), r.in_gain[...])
    r.gain_own[0:1] = term
    r.out_grad[...] = (r.d_middle[...] + back).astype(BF16)
    view_gain(me)[...] = r.gain_own[...]
    gather_start(6, view_gain)
    ring_pass(1, 1)
    wide_final(1)
    gather_start(8, view_gu)
    for level in middle_levels[:1]:
        advance(level, 1)
    for level in middle_levels[:1]:
        advance_to(level, "wide", 0)
    ring_pass(1, 2)
    for level in middle_levels[1:]:
        advance_to(level, "tall", 0)
    gather_forward(6, view_gain)
    gather_forward(8, view_gu)
    for level in middle_levels[1:]:
        advance_to(level, "wide", 0)
    gather_last(6, view_gain)
    tall_final(0)
    ring_start(0)
    wide_final(0)
    gather_start(9, view_qkv)
    gather_last(8, view_gu)
    ring_pass(1, 3)
    gather_finish(6, view_gain)
    total = r.gain_all[0]
    for member in range(1, team):
        total = total + r.gain_all[member]
    r.gain_line[z] = total
    for away in range(1, fsdp):
        launch(
            remote(
                r.gain_line.at[z],
                r.gain_line.at[z],
                r.gl_sem.at[0, away],
                r.gl_sem.at[1, away],
                me,
                lax.rem(z + away, fsdp),
            )
        )
    r.out_block[...] = (r.middle[...] + scatter_finish(2)).astype(BF16)
    ring_pass(0, 1)
    for away in range(1, fsdp):
        block = r.gain_line.at[lax.rem(z + fsdp - away, fsdp)]
        remote(block, block, r.gl_sem.at[0, away], r.gl_sem.at[1, away], me, z).wait_recv()
    total = r.gain_line[0]
    for plane in range(1, fsdp):
        total = total + r.gain_line[plane]
    r.out_gain[...] = total
    gather_forward(9, view_qkv)
    ring_pass(0, 2)
    gather_last(9, view_qkv)
    ring_pass(0, 3)
    gather_finish(8, view_gu)
    gather_finish(9, view_qkv)
    ring_finish(1)
    ring_finish(0)
    for items in queues.values():
        pending.extend(items)
    for cond, copy in pending:
        guarded(cond, copy.wait_send)


def run_layer(dims, operands):
    team, fsdp, seq, model = dims.team, dims.fsdp, dims.seq, dims.model
    width, kv, ratio, band = dims.width, dims.kv, dims.ratio, dims.band
    qc, kc, fc = dims.qcols, dims.kcols, dims.ffcols
    chips = team // 2
    qkv, gu, many = qc + 2 * kc, 2 * fc, team * seq
    chunks = max(qc, fc) // width
    jobs = 10 + (qc + fc) // width
    inputs = [
        "tokens",
        "table",
        "mask",
        "cotangent",
        "in_gain",
        "post_gain",
        "qg",
        "kg",
        "wq",
        "wk",
        "wv",
        "wo",
        "wg",
        "wu",
        "wd",
    ]
    outputs = [
        "out_block",
        "out_grad",
        "out_gain",
        "oqkv",
        "ogu",
        "oo",
        "od",
    ]
    dma = pltpu.SemaphoreType.DMA
    scratch = dict(
        xn=pltpu.VMEM((many, model), BF16),
        tab=pltpu.VMEM((many, width), F32),
        msk=pltpu.VMEM((many, seq), BF16),
        cot=pltpu.VMEM((many, model), BF16),
        pn=pltpu.VMEM((many, model), BF16),
        da=pltpu.VMEM((many, model), BF16),
        w_qkv=pltpu.VMEM((model, qkv), BF16),
        w_gu=pltpu.VMEM((model, gu), BF16),
        w_o=pltpu.VMEM((qc, model), BF16),
        w_d=pltpu.VMEM((fc, model), BF16),
        qk=pltpu.VMEM((many, qc + kc), F32),
        rot=pltpu.VMEM((many, qkv), BF16),
        probs=pltpu.VMEM((team, kv, ratio * seq, seq), F32),
        att=pltpu.VMEM((many, qc), BF16),
        hid=pltpu.VMEM((many, fc), BF16),
        dgu=pltpu.VMEM((many, gu), BF16),
        dqkv=pltpu.VMEM((many, qkv), BF16),
        middle=pltpu.VMEM((seq, model), F32),
        d_middle=pltpu.VMEM((seq, model), F32),
        rs_out=pltpu.VMEM((4, chips, seq, model), BF16),
        rs_in=pltpu.VMEM((4, chips, seq, model), BF16),
        rs_last=pltpu.VMEM((4, max(chips - 1, 1), seq, model), BF16),
        rs_sum=pltpu.VMEM((4, seq, model), F32),
        g_qkv=pltpu.VMEM((model, qkv), F32),
        g_gu=pltpu.VMEM((model, gu), F32),
        g_o=pltpu.VMEM((qc, model), F32),
        g_d=pltpu.VMEM((fc, model), F32),
        f_qkv=pltpu.VMEM((2, model, qkv), BF16),
        f_gu=pltpu.VMEM((2, model, gu), BF16),
        f_o=pltpu.VMEM((2, qc, model), BF16),
        f_d=pltpu.VMEM((2, fc, model), BF16),

        gain_own=pltpu.VMEM((8, model), F32),
        gain_all=pltpu.VMEM((team, 8, model), F32),
        gain_line=pltpu.VMEM((fsdp, 8, model), F32),
        ag_send=dma((jobs, team)),
        ag_recv=dma((jobs, team)),
        rs_sem=dma((4, 4, chips)),
        ww_send=dma((2, 2, fsdp)),
        ww_recv=dma((2, fsdp)),
        wt_send=dma((2, 2, chunks)),
        wt_recv=dma((2, chunks)),
        gw_send=dma((2, 2, fsdp)),
        gw_recv=dma((2, 2, fsdp)),
        gt_send=dma((2, 2, chunks)),
        gt_recv=dma((2, 2, chunks)),
        gl_sem=dma((2, fsdp)),
        load_sem=dma((7,)),
    )
    vmem = pl.BlockSpec(memory_space=pltpu.VMEM)
    anywhere = pl.BlockSpec(memory_space=pl.ANY)
    shapes = [
        jax.ShapeDtypeStruct((seq, model), BF16),
        jax.ShapeDtypeStruct((seq, model), BF16),
        jax.ShapeDtypeStruct((8, model), F32),
    ] + [
        jax.ShapeDtypeStruct(shape, BF16)
        for shape in (
            (team * band, qkv),
            (team * band, gu),
            (dims.share * qc, model),
            (dims.share * fc, model),
        )
    ]
    return pl.pallas_call(
        partial(layer_kernel, inputs + outputs + list(scratch), dims),
        out_shape=shapes,
        in_specs=[vmem] * 8 + [anywhere] * 7,
        out_specs=[vmem] * 7,
        scratch_shapes=list(scratch.values()),
        compiler_params=pltpu.CompilerParams(
            collective_id=0, has_side_effects=True, vmem_limit_bytes=VMEM_LIMIT
        ),
        name="layer",
    )(*operands)


def body(
    mesh_sizes,
    tokens_in,
    input_gain,
    q_gain,
    k_gain,
    w_query,
    w_key,
    w_value,
    w_output,
    post_gain,
    w_gate,
    w_up,
    w_down,
    segment_ids,
    positions,
    out_cotangent,
):
    dims = sizes_of(mesh_sizes, tokens_in, w_query, w_key, w_output, w_gate, w_down, q_gain)
    seq, width = dims.seq, dims.width
    ladder = jnp.arange(width // 2, dtype=F32)
    inverse = jnp.exp(ladder * (-2.0 * math.log(ROPE_BASE) / width))
    angles = positions.astype(F32)[:, None] * inverse[None, :]
    table = jnp.concatenate([jnp.cos(angles), jnp.sin(angles)], -1)
    steps = jnp.arange(seq)
    mask = (
        (segment_ids[:, None] == segment_ids[None, :]) & (steps[:, None] >= steps[None, :])
    ).astype(BF16)
    weights = (w_query, w_key, w_value, w_output, w_gate, w_up, w_down)
    done = run_layer(
        dims,
        (
            tokens_in,
            table,
            mask,
            out_cotangent,
            input_gain[None],
            post_gain[None],
            q_gain[None],
            k_gain[None],
            *weights,
        ),
    )
    gains, grads = done[2], tuple(done[3:])
    reps, team = dims.reps, dims.team
    if reps > team:
        rings = [list(range(first, reps, team)) for first in range(team)]
        gains = lax.psum(gains, "rep", axis_index_groups=rings)
        grads = lax.psum(grads, "rep", axis_index_groups=rings)
    return widen(dims, done[0], done[1], gains, grads)


def widen_kernel(dims, *refs):
    width, qc, kc, fc = dims.width, dims.qcols, dims.kcols, dims.ffcols
    block, grad, gains, qkv, gu, tall_o, tall_d = refs[:7]
    outs = refs[7:]
    outs[0][...] = block[...]
    outs[1][...] = grad[...]
    outs[2][...] = gains[0]
    outs[3][...] = gains[2, :width]
    outs[4][...] = gains[3, :width]
    outs[5][...] = gains[1]
    outs[6][...] = qkv[:, :qc].astype(F32)
    outs[7][...] = qkv[:, qc : qc + kc].astype(F32)
    outs[8][...] = qkv[:, qc + kc :].astype(F32)
    outs[9][...] = tall_o[...].astype(F32)
    outs[10][...] = gu[:, :fc].astype(F32)
    outs[11][...] = gu[:, fc:].astype(F32)
    outs[12][...] = tall_d[...].astype(F32)


def widen(dims, block_out, input_grad, gains, grads):
    steps, model, width, band = dims.team, dims.model, dims.width, dims.band
    qc, kc, fc = dims.qcols, dims.kcols, dims.ffcols

    def by_rows(count):
        return pl.BlockSpec((count // steps, model), lambda step: (step, 0))

    def stacked(size):
        return pl.BlockSpec((band, size), lambda step: (step, 0))

    def by_columns(size):
        return pl.BlockSpec((band, size), lambda step: (0, step))

    def flat(size):
        return pl.BlockSpec((size,), lambda step: (0,))

    count_o, count_d = grads[2].shape[0], grads[3].shape[0]
    return pl.pallas_call(
        partial(widen_kernel, dims),
        grid=(steps,),
        in_specs=[
            by_rows(dims.seq),
            by_rows(dims.seq),
            pl.BlockSpec(gains.shape, lambda step: (0, 0)),
            stacked(qc + 2 * kc),
            stacked(2 * fc),
            by_rows(count_o),
            by_rows(count_d),
        ],
        out_specs=[
            by_rows(dims.seq),
            by_rows(dims.seq),
            flat(model),
            flat(width),
            flat(width),
            flat(model),
            by_columns(qc),
            by_columns(kc),
            by_columns(kc),
            by_rows(count_o),
            by_columns(fc),
            by_columns(fc),
            by_rows(count_d),
        ],
        out_shape=[
            jax.ShapeDtypeStruct((dims.seq, model), BF16),
            jax.ShapeDtypeStruct((dims.seq, model), BF16),
            jax.ShapeDtypeStruct((model,), F32),
            jax.ShapeDtypeStruct((width,), F32),
            jax.ShapeDtypeStruct((width,), F32),
            jax.ShapeDtypeStruct((model,), F32),
            jax.ShapeDtypeStruct((band, steps * qc), F32),
            jax.ShapeDtypeStruct((band, steps * kc), F32),
            jax.ShapeDtypeStruct((band, steps * kc), F32),
            jax.ShapeDtypeStruct((count_o, model), F32),
            jax.ShapeDtypeStruct((band, steps * fc), F32),
            jax.ShapeDtypeStruct((band, steps * fc), F32),
            jax.ShapeDtypeStruct((count_d, model), F32),
        ],
        compiler_params=pltpu.CompilerParams(vmem_limit_bytes=VMEM_LIMIT),
        name="widen",
    )(block_out, input_grad, gains, *grads)


def solution(mesh):
    tokens = P(("rep", "fsdp"), None)
    ids = P(("rep", "fsdp"))
    weight = P("fsdp", None)
    in_specs = (
        (tokens,)
        + (P(),) * 3
        + (weight,) * 4
        + (P(),)
        + (weight,) * 3
        + (ids, ids, tokens)
    )
    out_specs = (tokens, tokens) + (P(),) * 4 + (weight,) * 7
    return jax.shard_map(
        partial(body, (mesh.shape["rep"], mesh.shape["fsdp"])),
        mesh=mesh,
        in_specs=in_specs,
        out_specs=out_specs,
        check_vma=False,
    )
```

```python
from functools import partial
import math
from types import SimpleNamespace

import jax
import jax.numpy as jnp
from jax import lax
from jax.experimental import pallas as pl
from jax.experimental.pallas import tpu as pltpu
from jax.sharding import PartitionSpec as P

EPS = 1e-06
ROPE_BASE = 1000000.0
NEG_FILL = -1e30
F32 = jnp.float32
BF16 = jnp.bfloat16
VMEM_LIMIT = 63 * 1024 * 1024


def dot(first, second):
    return lax.dot_general(first, second, (((1,), (0,)), ((), ())), preferred_element_type=F32)


def dot_nt(first, second):
    return lax.dot_general(first, second, (((1,), (1,)), ((), ())), preferred_element_type=F32)


def dot_tn(first, second):
    return lax.dot_general(first, second, (((0,), (0,)), ((), ())), preferred_element_type=F32)


def rms_scale(values):
    return lax.rsqrt(jnp.mean(values * values, axis=-1, keepdims=True) + EPS)


def flip(index, bits):
    out = index
    step = 1
    while step <= bits:
        if bits & step:
            out = out + step * (1 - 2 * lax.rem(index // step, 2))
        step *= 2
    return out


def sizes_of(mesh_sizes, tokens, w_query, w_key, w_output, w_gate, w_down, q_gain):
    reps, fsdp = mesh_sizes
    width = q_gain.shape[0]
    heads_q = w_query.shape[1] // width
    heads_kv = w_key.shape[1] // width
    team = math.gcd(reps, heads_kv)
    assert team >= 2 and team & (team - 1) == 0 and team % fsdp == 0
    dims = SimpleNamespace(
        reps=reps,
        fsdp=fsdp,
        team=team,
        width=width,
        seq=tokens.shape[0],
        model=tokens.shape[1],
        kv=heads_kv // team,
        ratio=heads_q // heads_kv,
        qcols=w_query.shape[1] // team,
        kcols=w_key.shape[1] // team,
        ffcols=w_gate.shape[1] // team,
        band=w_query.shape[0],
        share=team // fsdp,
    )
    return dims


def layer_kernel(names, dims, *refs):
    r = SimpleNamespace(**dict(zip(names, refs)))
    team, fsdp = dims.team, dims.fsdp
    seq, model, width = dims.seq, dims.model, dims.width
    kv, ratio, band, share = dims.kv, dims.ratio, dims.band, dims.share
    qc, kc, fc = dims.qcols, dims.kcols, dims.ffcols
    chips = team // 2
    half = width // 2

    rep = lax.axis_index("rep")
    z = lax.axis_index("fsdp")
    me = lax.rem(rep, team)
    base = rep - me
    home = me // share

    def place(member, plane):
        return {"rep": base + member, "fsdp": plane}

    def remote(src, dst, send_sem, recv_sem, member, plane):
        return pltpu.make_async_remote_copy(
            src_ref=src,
            dst_ref=dst,
            send_sem=send_sem,
            recv_sem=recv_sem,
            device_id=place(member, plane),
            device_id_type=pl.DeviceIdType.MESH,
        )

    pending = []

    def launch(copy, cond=None):
        if cond is None:
            copy.start()
        else:
            pl.when(cond)(copy.start)
        pending.append((cond, copy))

    def guarded(cond, action):
        if cond is None:
            action()
        else:
            pl.when(cond)(action)

    queues = {}

    def paced(queue, limit, cond, copy, before=None):
        items = queues.setdefault(queue, [])
        if len(items) >= limit:
            earlier, first = items.pop(0)
            pl.when(earlier)(first.wait_send)

        def start():
            if before is not None:
                before()
            copy.start()

        pl.when(cond)(start)
        items.append((cond, copy))

    def rows(ref, index, count):
        return ref.at[pl.ds(pl.multiple_of(index * count, count), count)]

    def loop(count, step, first=0):
        def run(index, carry):
            step(index)
            return carry

        lax.fori_loop(first, count, run, 0, unroll=2)

    near = [2] if chips == 2 else [2, 4]
    far = [2 * chip for chip in range(1, chips) if 2 * chip not in near]
    core = lax.rem(me, 2)
    passes = chips == 4
    along = flip(me, 2) * (1 - core) + flip(me, 4) * core
    across = flip(me, 4) * (1 - core) + flip(me, 2) * core

    def gather_send(job, block, bits, member, cond):
        send_sem, recv_sem = r.ag_send.at[job, bits], r.ag_recv.at[job, bits]
        launch(remote(block, block, send_sem, recv_sem, member, z), cond)

    def gather_start(job, view, active=None):
        cond = None if active is None else active(me)
        for bits in near + [1] + ([] if passes else far):
            gather_send(job, view(me), bits, flip(me, bits), cond)

    def gather_wait(job, view, bits, active=None):
        block = view(flip(me, bits))
        cond = None if active is None else active(flip(me, bits))
        copy = remote(
            block, block, r.ag_send.at[job, bits], r.ag_recv.at[job, bits], flip(me, 1), z
        )
        guarded(cond, copy.wait_recv)

    def gather_beside(job, view, bits, active):
        block = view(flip(me, bits))
        cond = None if active is None else active(flip(me, bits))
        gather_send(job, block, bits + 1, flip(me, 1), cond)

    def gather_forward(job, view, active=None):
        for bits in near:
            gather_wait(job, view, bits, active)
        if passes:
            block = view(along)
            cond = None if active is None else active(along)
            gather_send(job, block, far[0], across, cond)
        for bits in near:
            gather_beside(job, view, bits, active)

    def gather_last(job, view, active=None):
        for bits in far:
            gather_wait(job, view, bits, active)
            gather_beside(job, view, bits, active)

    def gather_finish(job, view, active=None):
        for chip in range(chips):
            gather_wait(job, view, 2 * chip + 1, active)

    def ring_jobs(which):
        first = 0 if which == 0 else tall_chunks(0)
        for chunk in range(tall_chunks(which)):

            def view(member, chunk=chunk):
                return tall_view[which](member).at[pl.ds(chunk * width, width)]

            yield 10 + first + chunk, view

    def ring_start(which):
        for job, view in ring_jobs(which):
            if not passes:
                gather_start(job, view, home_of)
                continue
            bits = 2 + 2 * core
            block, cond = view(me), home_of(me)
            send, recv = r.ag_send.at[job, 0], r.ag_recv.at[job, bits]
            launch(remote(block, block, send, recv, along, z), cond)
            gather_send(job, block, 1, flip(me, 1), cond)

    def ring_pass(which, stage):
        for job, view in ring_jobs(which):
            if not passes:
                if stage == 1:
                    gather_forward(job, view, home_of)
                    gather_last(job, view, home_of)
                continue
            bits = (2 + 2 * core, 6, 4 - 2 * core)[stage - 1]
            owner = (along, flip(me, 6), across)[stage - 1]
            block, cond = view(owner), home_of(owner)
            recv = r.ag_recv.at[job, bits]
            copy = remote(block, block, r.ag_send.at[job, 0], recv, along, z)
            guarded(cond, copy.wait_recv)
            if stage < 3:
                target = across if stage == 1 else along
                after = r.ag_recv.at[job, 6 if stage == 1 else 4 - 2 * core]
                send = r.ag_send.at[job, 2 * stage]
                launch(remote(block, block, send, after, target, z), cond)
            send, after = r.ag_send.at[job, 1 + 2 * stage], r.ag_recv.at[job, bits + 1]
            launch(remote(block, block, send, after, flip(me, 1), z), cond)

    def ring_finish(which):
        for job, view in ring_jobs(which):
            gather_finish(job, view, home_of)

    def home_of(member):
        return member // share == z

    def scatter_start(job, part):
        for chip in reversed(range(chips)):
            bits = 2 * chip + 1
            r.rs_out[job, chip] = part(flip(me, bits)).astype(BF16)
            launch(
                remote(
                    r.rs_out.at[job, chip],
                    r.rs_in.at[job, chip],
                    r.rs_sem.at[job, 0, chip],
                    r.rs_sem.at[job, 1, chip],
                    flip(me, 1),
                    z,
                )
            )

        def arrived(chip):
            block = r.rs_in.at[job, chip]
            remote(
                block,
                block,
                r.rs_sem.at[job, 0, chip],
                r.rs_sem.at[job, 1, chip],
                flip(me, 1),
                z,
            ).wait_recv()

        for chip in list(reversed(range(1, chips))):
            mine = part(flip(me, 2 * chip))
            arrived(chip)
            r.rs_in[job, chip] = (mine + r.rs_in[job, chip].astype(F32)).astype(BF16)
            launch(
                remote(
                    r.rs_in.at[job, chip],
                    r.rs_last.at[job, chip - 1],
                    r.rs_sem.at[job, 2, chip],
                    r.rs_sem.at[job, 3, chip],
                    flip(me, 2 * chip),
                    z,
                )
            )
        mine = part(me)
        arrived(0)
        r.rs_sum[job] = mine + r.rs_in[job, 0].astype(F32)

    def scatter_finish(job):
        total = r.rs_sum[job]
        for chip in range(1, chips):
            block = r.rs_last.at[job, chip - 1]
            remote(
                block,
                block,
                r.rs_sem.at[job, 2, chip],
                r.rs_sem.at[job, 3, chip],
                flip(me, 2 * chip),
                z,
            ).wait_recv()
            total = total + r.rs_last[job, chip - 1].astype(F32)
        return total

    wide = (r.w_qkv, r.w_gu)
    tall = (r.w_o, r.w_d)
    tall_rows = (qc, fc)

    def wide_block(which, plane):
        return rows(wide[which], plane, band)

    def wide_pass(which, step):
        for way, exists, plane, more, target in (
            (0, z - step >= 0, z - step, z < fsdp - 1, z + 1),
            (1, z + step <= fsdp - 1, z + step, z > 0, z - 1),
        ):
            plane = jnp.clip(plane, 0, fsdp - 1)
            block = wide_block(which, plane)
            copy = remote(
                block,
                block,
                r.ww_send.at[which, way, step],
                r.ww_recv.at[which, plane],
                me,
                jnp.clip(target, 0, fsdp - 1),
            )
            if step > 0:
                pl.when(exists)(copy.wait_recv)
            if step < fsdp - 1:
                paced(("wide", way), 3, jnp.logical_and(exists, more), copy)

    def tall_chunks(which):
        return tall_rows[which] // width

    def tall_pass(which, chunk, stage):
        block = tall[which].at[pl.ds(chunk * width, width)]
        up = jnp.logical_and(z >= home, z < fsdp - 1)
        down = jnp.logical_and(z <= home, z > 0)
        begins = z == home
        ends = jnp.logical_and(z != home, jnp.logical_or(z == 0, z == fsdp - 1))
        between = jnp.logical_and(z != home, jnp.logical_and(z > 0, z < fsdp - 1))
        for way, cond, target in ((0, up, z + 1), (1, down, z - 1)):
            copy = remote(
                block,
                block,
                r.wt_send.at[which, way, chunk],
                r.wt_recv.at[which, chunk],
                me,
                jnp.clip(target, 0, fsdp - 1),
            )
            if stage == 2:
                if way == 0:
                    pl.when(ends)(copy.wait_recv)
                continue
            if stage == 1 and way == 0:
                pl.when(between)(copy.wait_recv)
            own = begins if stage == 0 else between
            paced(("tall", way, stage), 2, jnp.logical_and(cond, own), copy)

    wide_sum = (r.g_qkv, r.g_gu)
    tall_sum = (r.g_o, r.g_d)
    wide_flow = (r.f_qkv, r.f_gu)
    tall_flow = (r.f_o, r.f_d)
    wide_view = (lambda member: rows(r.oqkv, member, band), lambda member: rows(r.ogu, member, band))
    tall_view = (
        lambda member: rows(r.oo, lax.rem(member, share), qc),
        lambda member: rows(r.od, lax.rem(member, share), fc),
    )

    def merge(target, own, start, count, has_incoming):
        step = 32

        def one(index):
            at = pl.ds(pl.multiple_of(start + index * step, step), step)
            value = own[at]
            if has_incoming:
                value = value + target[at].astype(F32)
            target[at] = value.astype(BF16)

        loop(count // step, one)


    def wide_level(which, level, turn):
        for way, here in ((0, level), (1, fsdp - 1 - level)):
            flow = wide_flow[which].at[way]
            plane = fsdp - 1 - turn if way == 0 else turn
            block = flow.at[pl.ds(plane * band, band)]
            copy = remote(
                block,
                block,
                r.gw_send.at[which, way, plane],
                r.gw_recv.at[which, way, plane],
                me,
                here + 1 if way == 0 else here - 1,
            )

            def before(flow=flow, plane=plane, copy=copy):
                if level > 0:
                    copy.wait_recv()
                merge(flow, wide_sum[which], plane * band, band, level > 0)

            paced(("level", way, level), 4, z == here, copy, before)

    def wide_final(which):
        def take(way):
            flow = wide_flow[which].at[way]
            block = rows(flow, z, band)
            remote(
                block,
                block,
                r.gw_send.at[which, way, z],
                r.gw_recv.at[which, way, z],
                me,
                z,
            ).wait_recv()
            step = 32

            def one(index):
                at = pl.ds(pl.multiple_of(z * band + index * step, step), step)
                wide_sum[which][at] = wide_sum[which][at] + flow[at].astype(F32)

            loop(band // step, one)

        pl.when(z > 0)(lambda: take(0))
        pl.when(z < fsdp - 1)(lambda: take(1))
        wide_view[which](me)[...] = rows(wide_sum[which], z, band)[...].astype(BF16)

    def tall_level(which, level, chunk):
        for way, here in ((0, level), (1, fsdp - 1 - level)):
            flow = tall_flow[which].at[way]
            block = flow.at[pl.ds(chunk * width, width)]
            copy = remote(
                block,
                block,
                r.gt_send.at[which, way, chunk],
                r.gt_recv.at[which, way, chunk],
                me,
                here + 1 if way == 0 else here - 1,
            )

            def before(flow=flow, chunk=chunk, copy=copy):
                if level > 0:
                    copy.wait_recv()
                merge(flow, tall_sum[which], chunk * width, width, level > 0)

            toward = home > here if way == 0 else home < here
            paced(("level", way, level), 4, jnp.logical_and(z == here, toward), copy, before)

    flow_order = [("tall", 1, chunk) for chunk in range(tall_chunks(1))]
    flow_order += [("wide", 1, turn) for turn in range(fsdp - 1)]
    flow_order += [("tall", 0, chunk) for chunk in range(tall_chunks(0))]
    flow_order += [("wide", 0, turn) for turn in range(fsdp - 1)]
    reached = [0] * max(fsdp - 1, 1)

    def advance(level, count):
        for kind, which, piece in flow_order[reached[level] : reached[level] + count]:
            if kind == "tall":
                tall_level(which, level, piece)
            elif piece < fsdp - 1 - level:
                wide_level(which, level, piece)
        reached[level] += count

    def advance_to(level, kind, which):
        last = max(at for at, item in enumerate(flow_order) if item[:2] == (kind, which))
        if level < fsdp - 1 and last >= reached[level]:
            advance(level, last + 1 - reached[level])

    def tall_final(which):
        count = tall_rows[which]

        def take(way):
            flow = tall_flow[which].at[way]
            for chunk in range(tall_chunks(which)):
                block = flow.at[pl.ds(chunk * width, width)]
                remote(
                    block,
                    block,
                    r.gt_send.at[which, way, chunk],
                    r.gt_recv.at[which, way, chunk],
                    me,
                    z,
                ).wait_recv()
            step = 32

            def one(index):
                at = pl.ds(pl.multiple_of(index * step, step), step)
                tall_sum[which][at] = tall_sum[which][at] + flow[at].astype(F32)

            loop(count // step, one)

        pl.when(jnp.logical_and(z == home, z > 0))(lambda: take(0))
        pl.when(jnp.logical_and(z == home, z < fsdp - 1))(lambda: take(1))

        def close():
            tall_view[which](me)[...] = tall_sum[which][...].astype(BF16)

        pl.when(z == home)(close)

    loads = []
    wide_at = lambda which, start, size: wide_block(which, z).at[:, pl.ds(start, size)]

    def column(ref, member, size):
        return ref.at[:, pl.ds(pl.multiple_of(member * size, size), size)]

    for src, dst in (
        (column(r.wq, me, qc), wide_at(0, 0, qc)),
        (column(r.wk, me, kc), wide_at(0, qc, kc)),
        (column(r.wv, me, kc), wide_at(0, qc + kc, kc)),
        (column(r.wg, me, fc), wide_at(1, 0, fc)),
        (column(r.wu, me, fc), wide_at(1, fc, fc)),
    ):
        load = pltpu.make_async_copy(src, dst, r.load_sem.at[len(loads)])
        load.start()
        loads.append(load)
    slot = lax.rem(me, share)
    tall_loads = []
    for which, src in ((0, r.wo), (1, r.wd)):
        load = pltpu.make_async_copy(
            rows(src, slot, tall_rows[which]), tall[which], r.load_sem.at[5 + which]
        )
        pl.when(z == home)(load.start)
        tall_loads.append(load)

    barrier = pltpu.get_barrier_semaphore()
    partners = [2 * chip for chip in range(1, chips)] + [1]
    for bits in partners:
        pl.semaphore_signal(
            barrier,
            inc=1,
            device_id=place(flip(me, bits), z),
            device_id_type=pl.DeviceIdType.MESH,
        )
    for away in range(1, fsdp):
        pl.semaphore_signal(
            barrier,
            inc=1,
            device_id=place(me, lax.rem(z + away, fsdp)),
            device_id_type=pl.DeviceIdType.MESH,
        )

    tokens = r.tokens[...].astype(F32)
    in_scale = rms_scale(tokens)
    rows(r.xn, me, seq)[...] = (tokens * in_scale * r.in_gain[...]).astype(BF16)
    rows(r.tab, me, seq)[...] = r.table[...]
    rows(r.msk, me, seq)[...] = r.mask[...]
    rows(r.cot, me, seq)[...] = r.cotangent[...]
    r.gain_own[...] = jnp.zeros_like(r.gain_own)

    pl.semaphore_wait(barrier, len(partners) + fsdp - 1)

    view_xn = lambda member: rows(r.xn, member, seq)
    view_tab = lambda member: rows(r.tab, member, seq)
    view_msk = lambda member: rows(r.msk, member, seq)
    view_cot = lambda member: rows(r.cot, member, seq)
    view_pn = lambda member: rows(r.pn, member, seq)
    view_da = lambda member: rows(r.da, member, seq)

    def home_sends(which, chunk):
        if chunk < tall_chunks(which):
            tall_pass(which, chunk, 0)

    def tall_passes(which, chunk):
        if chunk < tall_chunks(which):
            tall_pass(which, chunk, 1)

    for load in loads[:3]:
        load.wait()
    wide_pass(0, 0)
    for job, view in ((0, view_xn), (1, view_tab), (2, view_msk)):
        gather_start(job, view)
    for load in loads[3:]:
        load.wait()
    for load in tall_loads:
        pl.when(z == home)(load.wait)
    gather_forward(0, view_xn)
    if fsdp > 2:
        wide_pass(0, 1)
    home_sends(0, 0)
    for job, view in ((1, view_tab), (2, view_msk)):
        gather_forward(job, view)
    gather_last(0, view_xn)
    for step in range(2, fsdp - 1):
        wide_pass(0, step)
    wide_pass(1, 0)
    for job, view in ((1, view_tab), (2, view_msk)):
        gather_last(job, view)
    for job, view in ((0, view_xn), (1, view_tab), (2, view_msk)):
        gather_finish(job, view)
    home_sends(0, 1)
    wide_pass(0, fsdp - 1)

    lane = lax.broadcasted_iota(jnp.int32, (seq, width), 1)
    front = lane < half
    sign = jnp.where(front, -1.0, 1.0).astype(F32)
    root = width ** (-0.5)

    def turn(values):
        return pltpu.roll(values, half, 1)

    def tables(at):
        table = r.tab[at]
        swapped = turn(table)
        return jnp.where(front, table, swapped), jnp.where(front, swapped, table)

    def at_seq(index):
        return pl.ds(pl.multiple_of(index * seq, seq), seq)

    def attend(index):
        at = at_seq(index)
        cosine, sine = tables(at)
        signed = sine * sign
        qkv = dot(r.xn[at], r.w_qkv[...])
        r.qk[at] = qkv[:, : qc + kc]
        allowed = r.msk[at].astype(F32) > 0.5
        allowed = jnp.concatenate([allowed] * ratio, 0) if ratio > 1 else allowed

        def spun(values, gain):
            values = values * rms_scale(values) * gain
            return (values * cosine + turn(values) * signed).astype(BF16)

        for group in range(kv):
            k_rot = spun(qkv[:, qc + group * width : qc + (group + 1) * width], r.kg[...])
            start = qc + kc + group * width
            values = qkv[:, start : start + width].astype(BF16)
            spins = []
            for head in range(ratio):
                place_at = (group * ratio + head) * width
                spin = spun(qkv[:, place_at : place_at + width], r.qg[...])
                r.rot[at, place_at : place_at + width] = spin
                spins.append(spin)
            r.rot[at, qc + group * width : qc + (group + 1) * width] = k_rot
            r.rot[at, start : start + width] = values
            q_rot = jnp.concatenate(spins, 0)
            scores = dot_nt(q_rot, k_rot) * root
            masked = jnp.where(allowed, scores, NEG_FILL)
            top = jnp.max(masked, axis=-1, keepdims=True)
            total = top + jnp.log(jnp.sum(jnp.exp(masked - top), axis=-1, keepdims=True))
            probs = jnp.where(allowed, jnp.exp(masked - total), 0.0)
            r.probs[index, group] = probs
            mixed = dot(probs.astype(BF16), values).astype(BF16)
            for head in range(ratio):
                place_at = (group * ratio + head) * width
                r.att[at, place_at : place_at + width] = mixed[head * seq : (head + 1) * seq]

    gather_start(3, view_cot)
    loop(team // 2, attend)
    tall_passes(0, 0)
    if fsdp > 2:
        wide_pass(1, 1)
    loop(team, attend, team // 2)
    for chunk in range(1, tall_chunks(0)):
        tall_passes(0, chunk)
    for chunk in range(2, tall_chunks(0)):
        home_sends(0, chunk)
    home_sends(1, 0)

    for chunk in range(tall_chunks(0)):
        tall_pass(0, chunk, 2)
    scatter_start(0, lambda member: dot(rows(r.att, member, seq)[...], r.w_o[...]))
    for step in range(2, fsdp - 1):
        wide_pass(1, step)
    home_sends(1, 1)
    gather_forward(3, view_cot)
    tall_passes(1, 0)
    middle = tokens + scatter_finish(0)
    r.middle[...] = middle
    post_scale = rms_scale(middle)
    view_pn(me)[...] = (middle * post_scale * r.post_gain[...]).astype(BF16)
    gather_start(4, view_pn)
    for chunk in range(2, tall_chunks(1)):
        home_sends(1, chunk)
    gather_last(3, view_cot)
    tall_passes(1, 1)
    gather_forward(4, view_pn)
    for chunk in range(2, tall_chunks(1)):
        tall_passes(1, chunk)
    gather_last(4, view_pn)
    wide_pass(1, fsdp - 1)
    gather_finish(3, view_cot)
    gather_finish(4, view_pn)
    for chunk in range(tall_chunks(1)):
        tall_pass(1, chunk, 2)

    def feed(index):
        at = at_seq(index)
        both = dot(r.pn[at], r.w_gu[...])
        gate, up = both[:, :fc], both[:, fc:]
        sigm = jax.nn.sigmoid(gate)
        soft = gate * sigm
        r.hid[at] = (soft * up).astype(BF16)
        d_hidden = dot_nt(r.cot[at], r.w_d[...])
        r.dgu[at, :fc] = (d_hidden * up * sigm * (1.0 + gate * (1.0 - sigm))).astype(BF16)
        r.dgu[at, fc:] = (d_hidden * soft).astype(BF16)

    loop(team, feed)

    r.g_d[...] = dot_tn(r.hid[...], r.cot[...])
    advance(0, tall_chunks(1))
    scatter_start(1, lambda member: dot_nt(rows(r.dgu, member, seq)[...], r.w_gu[...]))

    def grad_gu(index):
        at = pl.ds(pl.multiple_of(index * band, band), band)
        r.g_gu[at] = dot_tn(r.pn[:, at], r.dgu[...])

    def grad_qkv(index):
        at = pl.ds(pl.multiple_of(index * band, band), band)
        r.g_qkv[at] = dot_tn(r.xn[:, at], r.dqkv[...])

    loop(fsdp, grad_gu)
    advance(0, 1)
    middle_levels = range(1, fsdp - 1)

    def norm_back(grads, values, scale, gain):
        normal = values * scale
        gain_term = jnp.sum(grads * normal, axis=0, keepdims=True)
        scaled = grads * gain
        back = scale * (scaled - normal * jnp.mean(scaled * normal, axis=-1, keepdims=True))
        return back, gain_term

    d_post = scatter_finish(1)
    middle = r.middle[...]
    back, term = norm_back(d_post, middle, rms_scale(middle), r.post_gain[...])
    r.gain_own[1:2] = term
    d_middle = r.cotangent[...].astype(F32) + back
    r.d_middle[...] = d_middle
    view_da(me)[...] = d_middle.astype(BF16)
    gather_start(5, view_da)
    for level in middle_levels[:1]:
        advance_to(level, "tall", 1)
    advance(0, 1)
    gather_forward(5, view_da)
    advance_to(0, "wide", 1)
    gather_last(5, view_da)
    gather_finish(5, view_da)
    r.g_o[...] = dot_tn(r.att[...], r.da[...])
    advance_to(0, "tall", 0)

    def attend_back(index):
        at = at_seq(index)
        cosine, sine = tables(at)
        d_att = dot_nt(r.da[at], r.w_o[...]).astype(BF16)

        def unspun(grads):
            return grads * cosine - turn(grads * sine) * sign

        for group in range(kv):
            k_at = slice(qc + group * width, qc + (group + 1) * width)
            v_at = slice(qc + kc + group * width, qc + kc + (group + 1) * width)
            heads = [
                slice((group * ratio + head) * width, (group * ratio + head + 1) * width)
                for head in range(ratio)
            ]
            d_mixed = jnp.concatenate([d_att[:, head] for head in heads], 0)
            q_rot = jnp.concatenate([r.rot[at, head] for head in heads], 0)
            k_rot = r.rot[at, k_at]
            values = r.rot[at, v_at]
            probs = r.probs[index, group]
            d_probs = dot_nt(d_mixed, values)
            centre = jnp.sum(probs * d_probs, axis=-1, keepdims=True)
            d_scores = (probs * (d_probs - centre) * root).astype(BF16)
            d_query = dot(d_scores, k_rot)
            d_key = dot_tn(d_scores, q_rot)
            d_value = dot_tn(probs.astype(BF16), d_mixed)
            for number, head in enumerate(heads):
                queries = r.qk[at, head]
                back, term = norm_back(
                    unspun(d_query[number * seq : (number + 1) * seq]),
                    queries,
                    rms_scale(queries),
                    r.qg[...],
                )
                r.dqkv[at, head] = back.astype(BF16)
                r.gain_own[2:3, :width] += term
            keys = r.qk[at, k_at]
            back, term = norm_back(unspun(d_key), keys, rms_scale(keys), r.kg[...])
            r.dqkv[at, k_at] = back.astype(BF16)
            r.gain_own[3:4, :width] += term
            r.dqkv[at, v_at] = d_value.astype(BF16)

    view_gain = lambda member: r.gain_all.at[member]
    view_qkv, view_gu = wide_view
    loop(team // 2, attend_back)
    for level in middle_levels[1:]:
        advance_to(level, "tall", 1)
    for level in middle_levels[:1]:
        advance(level, 1)
    loop(team, attend_back, team // 2)
    scatter_start(3, lambda member: dot_nt(rows(r.dqkv, member, seq)[...], r.w_qkv[...]))
    loop(fsdp, grad_qkv)
    advance(0, 1)
    for level in middle_levels[:1]:
        advance_to(level, "wide", 1)
    tall_final(1)
    ring_start(1)
    scatter_start(2, lambda member: dot(rows(r.hid, member, seq)[...], r.w_d[...]))
    advance(0, 1)
    for level in middle_levels[1:]:
        advance_to(level, "wide", 1)
    d_normed = scatter_finish(3)
    advance_to(0, "wide", 0)
    for level in middle_levels[:1]:
        advance_to(level, "tall", 0)
    tokens = r.tokens[...].astype(F32)
    back, term = norm_back(d_normed, tokens, rms_scale(tokens), r.in_gain[...])
    r.gain_own[0:1] = term
    r.out_grad[...] = (r.d_middle[...] + back).astype(BF16)
    view_gain(me)[...] = r.gain_own[...]
    gather_start(6, view_gain)
    ring_pass(1, 1)
    wide_final(1)
    gather_start(8, view_gu)
    for level in middle_levels[:1]:
        advance(level, 1)
    for level in middle_levels[:1]:
        advance_to(level, "wide", 0)
    ring_pass(1, 2)
    for level in middle_levels[1:]:
        advance_to(level, "tall", 0)
    gather_forward(6, view_gain)
    gather_forward(8, view_gu)
    for level in middle_levels[1:]:
        advance_to(level, "wide", 0)
    gather_last(6, view_gain)
    tall_final(0)
    ring_start(0)
    wide_final(0)
    gather_start(9, view_qkv)
    gather_last(8, view_gu)
    ring_pass(1, 3)
    gather_finish(6, view_gain)
    total = r.gain_all[0]
    for member in range(1, team):
        total = total + r.gain_all[member]
    r.gain_line[z] = total
    for away in range(1, fsdp):
        launch(
            remote(
                r.gain_line.at[z],
                r.gain_line.at[z],
                r.gl_sem.at[0, away],
                r.gl_sem.at[1, away],
                me,
                lax.rem(z + away, fsdp),
            )
        )
    r.out_block[...] = (r.middle[...] + scatter_finish(2)).astype(BF16)
    ring_pass(0, 1)
    for away in range(1, fsdp):
        block = r.gain_line.at[lax.rem(z + fsdp - away, fsdp)]
        remote(block, block, r.gl_sem.at[0, away], r.gl_sem.at[1, away], me, z).wait_recv()
    total = r.gain_line[0]
    for plane in range(1, fsdp):
        total = total + r.gain_line[plane]
    r.out_gain[...] = total
    gather_forward(9, view_qkv)
    ring_pass(0, 2)
    gather_last(9, view_qkv)
    ring_pass(0, 3)
    gather_finish(8, view_gu)
    gather_finish(9, view_qkv)
    ring_finish(1)
    ring_finish(0)
    for items in queues.values():
        pending.extend(items)
    for cond, copy in pending:
        guarded(cond, copy.wait_send)


def run_layer(dims, operands):
    team, fsdp, seq, model = dims.team, dims.fsdp, dims.seq, dims.model
    width, kv, ratio, band = dims.width, dims.kv, dims.ratio, dims.band
    qc, kc, fc = dims.qcols, dims.kcols, dims.ffcols
    chips = team // 2
    qkv, gu, many = qc + 2 * kc, 2 * fc, team * seq
    chunks = max(qc, fc) // width
    jobs = 10 + (qc + fc) // width
    inputs = [
        "tokens",
        "table",
        "mask",
        "cotangent",
        "in_gain",
        "post_gain",
        "qg",
        "kg",
        "wq",
        "wk",
        "wv",
        "wo",
        "wg",
        "wu",
        "wd",
    ]
    outputs = [
        "out_block",
        "out_grad",
        "out_gain",
        "oqkv",
        "ogu",
        "oo",
        "od",
    ]
    dma = pltpu.SemaphoreType.DMA
    scratch = dict(
        xn=pltpu.VMEM((many, model), BF16),
        tab=pltpu.VMEM((many, width), F32),
        msk=pltpu.VMEM((many, seq), BF16),
        cot=pltpu.VMEM((many, model), BF16),
        pn=pltpu.VMEM((many, model), BF16),
        da=pltpu.VMEM((many, model), BF16),
        w_qkv=pltpu.VMEM((model, qkv), BF16),
        w_gu=pltpu.VMEM((model, gu), BF16),
        w_o=pltpu.VMEM((qc, model), BF16),
        w_d=pltpu.VMEM((fc, model), BF16),
        qk=pltpu.VMEM((many, qc + kc), F32),
        rot=pltpu.VMEM((many, qkv), BF16),
        probs=pltpu.VMEM((team, kv, ratio * seq, seq), F32),
        att=pltpu.VMEM((many, qc), BF16),
        hid=pltpu.VMEM((many, fc), BF16),
        dgu=pltpu.VMEM((many, gu), BF16),
        dqkv=pltpu.VMEM((many, qkv), BF16),
        middle=pltpu.VMEM((seq, model), F32),
        d_middle=pltpu.VMEM((seq, model), F32),
        rs_out=pltpu.VMEM((4, chips, seq, model), BF16),
        rs_in=pltpu.VMEM((4, chips, seq, model), BF16),
        rs_last=pltpu.VMEM((4, max(chips - 1, 1), seq, model), BF16),
        rs_sum=pltpu.VMEM((4, seq, model), F32),
        g_qkv=pltpu.VMEM((model, qkv), F32),
        g_gu=pltpu.VMEM((model, gu), F32),
        g_o=pltpu.VMEM((qc, model), F32),
        g_d=pltpu.VMEM((fc, model), F32),
        f_qkv=pltpu.VMEM((2, model, qkv), BF16),
        f_gu=pltpu.VMEM((2, model, gu), BF16),
        f_o=pltpu.VMEM((2, qc, model), BF16),
        f_d=pltpu.VMEM((2, fc, model), BF16),

        gain_own=pltpu.VMEM((8, model), F32),
        gain_all=pltpu.VMEM((team, 8, model), F32),
        gain_line=pltpu.VMEM((fsdp, 8, model), F32),
        ag_send=dma((jobs, team)),
        ag_recv=dma((jobs, team)),
        rs_sem=dma((4, 4, chips)),
        ww_send=dma((2, 2, fsdp)),
        ww_recv=dma((2, fsdp)),
        wt_send=dma((2, 2, chunks)),
        wt_recv=dma((2, chunks)),
        gw_send=dma((2, 2, fsdp)),
        gw_recv=dma((2, 2, fsdp)),
        gt_send=dma((2, 2, chunks)),
        gt_recv=dma((2, 2, chunks)),
        gl_sem=dma((2, fsdp)),
        load_sem=dma((7,)),
    )
    vmem = pl.BlockSpec(memory_space=pltpu.VMEM)
    anywhere = pl.BlockSpec(memory_space=pl.ANY)
    shapes = [
        jax.ShapeDtypeStruct((seq, model), BF16),
        jax.ShapeDtypeStruct((seq, model), BF16),
        jax.ShapeDtypeStruct((8, model), F32),
    ] + [
        jax.ShapeDtypeStruct(shape, BF16)
        for shape in (
            (team * band, qkv),
            (team * band, gu),
            (dims.share * qc, model),
            (dims.share * fc, model),
        )
    ]
    return pl.pallas_call(
        partial(layer_kernel, inputs + outputs + list(scratch), dims),
        out_shape=shapes,
        in_specs=[vmem] * 8 + [anywhere] * 7,
        out_specs=[vmem] * 7,
        scratch_shapes=list(scratch.values()),
        compiler_params=pltpu.CompilerParams(
            collective_id=0, has_side_effects=True, vmem_limit_bytes=VMEM_LIMIT
        ),
        name="layer",
    )(*operands)


def body(
    mesh_sizes,
    tokens_in,
    input_gain,
    q_gain,
    k_gain,
    w_query,
    w_key,
    w_value,
    w_output,
    post_gain,
    w_gate,
    w_up,
    w_down,
    segment_ids,
    positions,
    out_cotangent,
):
    dims = sizes_of(mesh_sizes, tokens_in, w_query, w_key, w_output, w_gate, w_down, q_gain)
    seq, width = dims.seq, dims.width
    ladder = jnp.arange(width // 2, dtype=F32)
    inverse = jnp.exp(ladder * (-2.0 * math.log(ROPE_BASE) / width))
    angles = positions.astype(F32)[:, None] * inverse[None, :]
    table = jnp.concatenate([jnp.cos(angles), jnp.sin(angles)], -1)
    steps = jnp.arange(seq)
    mask = (
        (segment_ids[:, None] == segment_ids[None, :]) & (steps[:, None] >= steps[None, :])
    ).astype(BF16)
    weights = (w_query, w_key, w_value, w_output, w_gate, w_up, w_down)
    done = run_layer(
        dims,
        (
            tokens_in,
            table,
            mask,
            out_cotangent,
            input_gain[None],
            post_gain[None],
            q_gain[None],
            k_gain[None],
            *weights,
        ),
    )
    gains, grads = done[2], tuple(done[3:])
    reps, team = dims.reps, dims.team
    if reps > team:
        rings = [list(range(first, reps, team)) for first in range(team)]
        gains = lax.psum(gains, "rep", axis_index_groups=rings)
        grads = lax.psum(grads, "rep", axis_index_groups=rings)
    return widen(dims, done[0], done[1], gains, grads)


def widen_kernel(dims, *refs):
    width, qc, kc, fc = dims.width, dims.qcols, dims.kcols, dims.ffcols
    block, grad, gains, qkv, gu, tall_o, tall_d = refs[:7]
    outs = refs[7:]
    outs[0][...] = block[...]
    outs[1][...] = grad[...]
    outs[2][...] = gains[0]
    outs[3][...] = gains[2, :width]
    outs[4][...] = gains[3, :width]
    outs[5][...] = gains[1]
    outs[6][...] = qkv[:, :qc].astype(F32)
    outs[7][...] = qkv[:, qc : qc + kc].astype(F32)
    outs[8][...] = qkv[:, qc + kc :].astype(F32)
    outs[9][...] = tall_o[...].astype(F32)
    outs[10][...] = gu[:, :fc].astype(F32)
    outs[11][...] = gu[:, fc:].astype(F32)
    outs[12][...] = tall_d[...].astype(F32)


def widen(dims, block_out, input_grad, gains, grads):
    steps, model, width, band = dims.team, dims.model, dims.width, dims.band
    qc, kc, fc = dims.qcols, dims.kcols, dims.ffcols

    def by_rows(count):
        return pl.BlockSpec((count // steps, model), lambda step: (step, 0))

    def stacked(size):
        return pl.BlockSpec((band, size), lambda step: (step, 0))

    def by_columns(size):
        return pl.BlockSpec((band, size), lambda step: (0, step))

    def flat(size):
        return pl.BlockSpec((size,), lambda step: (0,))

    count_o, count_d = grads[2].shape[0], grads[3].shape[0]
    return pl.pallas_call(
        partial(widen_kernel, dims),
        grid=(steps,),
        in_specs=[
            by_rows(dims.seq),
            by_rows(dims.seq),
            pl.BlockSpec(gains.shape, lambda step: (0, 0)),
            stacked(qc + 2 * kc),
            stacked(2 * fc),
            by_rows(count_o),
            by_rows(count_d),
        ],
        out_specs=[
            by_rows(dims.seq),
            by_rows(dims.seq),
            flat(model),
            flat(width),
            flat(width),
            flat(model),
            by_columns(qc),
            by_columns(kc),
            by_columns(kc),
            by_rows(count_o),
            by_columns(fc),
            by_columns(fc),
            by_rows(count_d),
        ],
        out_shape=[
            jax.ShapeDtypeStruct((dims.seq, model), BF16),
            jax.ShapeDtypeStruct((dims.seq, model), BF16),
            jax.ShapeDtypeStruct((model,), F32),
            jax.ShapeDtypeStruct((width,), F32),
            jax.ShapeDtypeStruct((width,), F32),
            jax.ShapeDtypeStruct((model,), F32),
            jax.ShapeDtypeStruct((band, steps * qc), F32),
            jax.ShapeDtypeStruct((band, steps * kc), F32),
            jax.ShapeDtypeStruct((band, steps * kc), F32),
            jax.ShapeDtypeStruct((count_o, model), F32),
            jax.ShapeDtypeStruct((band, steps * fc), F32),
            jax.ShapeDtypeStruct((band, steps * fc), F32),
            jax.ShapeDtypeStruct((count_d, model), F32),
        ],
        compiler_params=pltpu.CompilerParams(vmem_limit_bytes=VMEM_LIMIT),
        name="widen",
    )(block_out, input_grad, gains, *grads)


def solution(mesh):
    tokens = P(("rep", "fsdp"), None)
    ids = P(("rep", "fsdp"))
    weight = P("fsdp", None)
    in_specs = (
        (tokens,)
        + (P(),) * 3
        + (weight,) * 4
        + (P(),)
        + (weight,) * 3
        + (ids, ids, tokens)
    )
    out_specs = (tokens, tokens) + (P(),) * 4 + (weight,) * 7
    return jax.shard_map(
        partial(body, (mesh.shape["rep"], mesh.shape["fsdp"])),
        mesh=mesh,
        in_specs=in_specs,
        out_specs=out_specs,
        check_vma=False,
    )
```
